256 devices in a mesh: seq: 64 (over y, x_hi, z), head: 4 (over x_lo, core).
Axes of the slice: x: 4 (x_hi: 2, x_lo: 2; x = x_hi * 2 + x_lo), y: 4, z: 8, core: 2. Of those that a mesh axis runs over, the one named last changes fastest.
Arguments:
- encoder_queries: bfloat16 [98304, 2048], P('seq', 'head'), may hold values from -30 to 30
- encoder_keys: bfloat16 [98304, 2048], P('seq', 'head'), may hold values from -4 to 4
- encoder_values: bfloat16 [98304, 2048], P('seq', 'head'), may hold values from -24 to 24
- block_lists: int32 [768, 4], P('seq'), may hold values from 0 to 767, as said below
- block_counts: int32 [768], P('seq'), may hold values from 1 to 4
- decoder_queries: bfloat16 [32768, 2048], P('seq', 'head'), may hold values from -30 to 30
- span_owner: int32 [256], replicated, may hold values from 0 to 63, as said below
- cross_slots: int32 [256, 2], replicated, may hold values from 0 to 11, as said below
- out_weight: bfloat16 [2048, 4096], P('head'), may hold values from -4.1875 to 4.1875
- decoder_input: bfloat16 [32768, 4096], P('seq', 'head'), may hold values from -6 to 6
Outputs:
- encoder_out: bfloat16 [98304, 2048], P('seq', 'head')
- decoder_out: bfloat16 [32768, 4096], P('seq', 'head')
The draws below stay inside these ranges and needn't reach their ends.
Inputs may be any that keep to these rules, and one draw needn't show every extreme that they name: `block_lists`: slot 0 of row b is b; the slots below block_counts[b] hold distinct blocks within 2 blocks of b; the other slots hold b. span_owner[d] differs from d // 4 by at most one. `cross_slots`: the 2 entries of a row are distinct.
All inputs are finite; a program needn't handle non-finite values.
Results may differ from the reference program's by a relative error of at most 0.015.
Values may be sent and summed in bfloat16 or wider, within the bound.
No kernel may reach another device: no remote copies, remote signals or barrier semaphores. Data moves between devices by JAX's collectives and lax.ppermute only.
A program may use at most 128 MiB of HBM per device.

```python
import jax
import jax.numpy as jnp
from jax import lax

D = 4096
HEADS = 32
HD = 64
BLK = 128
REACH = 2
SLOTS = 4
CROSS = 2
HW = 2048
EB = 12
DB = 4
NB = 768
NDB = 256
ETOK = 98304
DTOK = 32768
N_SEQ = 64


def owner_table(key):
    owner_key = jax.random.fold_in(key, 101)
    block_index = jnp.arange(NDB, dtype=jnp.int32)
    drift_steps = jax.random.randint(owner_key, (NDB,), -1, 2, dtype=jnp.int32)
    drift_steps = jnp.where(block_index == DB, -1, drift_steps)
    drift_steps = jnp.where(block_index == (N_SEQ - 2) * DB, 1, drift_steps)
    return jnp.clip(block_index // DB + drift_steps, 0, N_SEQ - 1).astype(jnp.int32)


def slot_table(key):
    slot_key = jax.random.fold_in(key, 102)
    ranking = jax.random.randint(slot_key, (NDB, EB), 0, 1 << 20, dtype=jnp.int32) * EB + jnp.arange(EB, dtype=jnp.int32)[None, :]
    return jnp.argsort(ranking, axis=1)[:, :CROSS].astype(jnp.int32)


def list_table(key):
    list_key = jax.random.fold_in(key, 103)
    count_key = jax.random.fold_in(key, 104)
    block_index = jnp.arange(NB, dtype=jnp.int32)
    offsets = jnp.concatenate([jnp.arange(-REACH, 0, dtype=jnp.int32), jnp.arange(1, REACH + 1, dtype=jnp.int32)])
    positions = jnp.arange(2 * REACH, dtype=jnp.int32)[None, :]
    ranking = jax.random.randint(list_key, (NB, 2 * REACH), 0, 1 << 20, dtype=jnp.int32) * (2 * REACH) + positions
    shuffled = offsets[jnp.argsort(ranking, axis=1)]
    candidate = block_index[:, None] + shuffled
    inside = ((candidate >= 0) & (candidate < NB)).astype(jnp.int32)
    placing = (1 - inside) * (4 * REACH) + positions
    arrangement = jnp.argsort(placing, axis=1)
    candidate = jnp.take_along_axis(candidate, arrangement, axis=1)
    usable = jnp.sum(inside, axis=1)
    drawn_counts = jax.random.randint(count_key, (NB,), 1, SLOTS + 1, dtype=jnp.int32)
    drawn_counts = jnp.where(block_index == NB // 2, SLOTS, drawn_counts)
    counts = jnp.minimum(drawn_counts, usable + 1)
    entries = jnp.concatenate([block_index[:, None], candidate[:, :SLOTS - 1]], axis=1)
    slot_index = jnp.arange(SLOTS, dtype=jnp.int32)[None, :]
    entries = jnp.where(slot_index < counts[:, None], entries, block_index[:, None])
    return (entries.astype(jnp.int32), counts.astype(jnp.int32))


def key_table(key):
    table_shape = (ETOK, HW)
    key_values = jnp.clip(jax.random.normal(jax.random.fold_in(key, 201), table_shape), -4.0, 4.0)
    return key_values


def draw_block_lists(key, part):
    return list_table(key)[0]


def draw_block_counts(key, part):
    return list_table(key)[1]


def draw_span_owner(key, part):
    return owner_table(key)


def draw_cross_slots(key, part):
    return slot_table(key)


def draw_encoder_keys(key, part):
    return key_table(key).astype(jnp.bfloat16)


def draw_encoder_queries(key, part):
    table_shape = (ETOK, HW)
    drawn_rows = jnp.clip(jax.random.normal(jax.random.fold_in(key, 202), table_shape), -4.0, 4.0)
    return drawn_rows.astype(jnp.bfloat16)


def draw_decoder_queries(key, part):
    table_shape = (DTOK, HW)
    drawn_rows = jnp.clip(jax.random.normal(jax.random.fold_in(key, 203), table_shape), -4.0, 4.0)
    return drawn_rows.astype(jnp.bfloat16)


def block_levels(stream_key, dims, pieces, smallest, top_value):
    level = 1.0
    for dim, blocks in pieces:
        steps = jax.random.uniform(jax.random.fold_in(jax.random.fold_in(stream_key, 6), dim), (blocks,), jnp.float32, smallest / len(pieces), top_value / len(pieces))
        level = level * jnp.repeat(jnp.exp(steps), dims[dim] // blocks).reshape((-1,) + (1,) * (len(dims) - 1 - dim))
    return level


def scatter_about(stream_key, shape, scale, reach, shards=(), kind=jnp.bfloat16):
    values = scale * jax.random.normal(stream_key, shape, jnp.float32)
    if shards:
        values = values * block_levels(stream_key, shape, shards, -0.22, 0.18)
    return jnp.clip(values, -reach, reach).astype(kind)


def setup_inputs(seed: int = 0) -> dict:
    key_list = jax.random.split(jax.random.key(seed), 11)
    encoder_queries = draw_encoder_queries(jax.random.fold_in(key_list[10], 71), 0)
    encoder_keys = draw_encoder_keys(jax.random.fold_in(key_list[10], 71), 0)
    encoder_values = scatter_about(key_list[2], (ETOK, HW), 4.0, 24.0, ((0, 64), (1, 4)))
    block_lists = draw_block_lists(jax.random.fold_in(key_list[10], 71), 0)
    block_counts = draw_block_counts(jax.random.fold_in(key_list[10], 71), 0)
    decoder_queries = draw_decoder_queries(jax.random.fold_in(key_list[10], 71), 0)
    span_owner = draw_span_owner(jax.random.fold_in(key_list[10], 71), 0)
    cross_slots = draw_cross_slots(jax.random.fold_in(key_list[10], 71), 0)
    out_weight = scatter_about(key_list[8], (HW, D), 0.7, 4.1875, ((0, 4),))
    decoder_input = scatter_about(key_list[9], (DTOK, D), 1.0, 6.0, ((0, 64), (1, 4)))
    return dict(encoder_queries=encoder_queries, encoder_keys=encoder_keys, encoder_values=encoder_values, block_lists=block_lists, block_counts=block_counts, decoder_queries=decoder_queries, span_owner=span_owner, cross_slots=cross_slots, out_weight=out_weight, decoder_input=decoder_input)


def attend_block(queries, key_rows, value_rows, allowed):
    scores = jnp.einsum("thd,uhd->htu", queries.astype(jnp.float32), key_rows.astype(jnp.float32)) * 0.125
    scores = jnp.where(allowed[None, None, :], scores, -1e30)
    largest = jnp.max(scores, axis=-1, keepdims=True)
    weights = jnp.exp(scores - largest)
    weights = (weights / jnp.sum(weights, axis=-1, keepdims=True)).astype(jnp.bfloat16)
    mixed_rows = jnp.einsum("htu,uhd->thd", weights.astype(jnp.float32), value_rows.astype(jnp.float32))
    return mixed_rows.astype(jnp.bfloat16)


def reference(encoder_queries, encoder_keys, encoder_values, block_lists, block_counts, decoder_queries, span_owner, cross_slots, out_weight, decoder_input):
    query_blocks = encoder_queries.reshape(NB, BLK, HEADS, HD)
    key_blocks = encoder_keys.reshape(NB, BLK, HEADS, HD)
    value_blocks = encoder_values.reshape(NB, BLK, HEADS, HD)
    slot_index = jnp.arange(SLOTS, dtype=jnp.int32)

    def encode(block_index):
        lists_here = block_lists[block_index]
        allowed = jnp.repeat(slot_index < block_counts[block_index], BLK)
        key_rows = key_blocks[lists_here].reshape(SLOTS * BLK, HEADS, HD)
        value_rows = value_blocks[lists_here].reshape(SLOTS * BLK, HEADS, HD)
        return attend_block(query_blocks[block_index], key_rows, value_rows, allowed)

    encoder_out = lax.map(encode, jnp.arange(NB, dtype=jnp.int32)).reshape(ETOK, HW)
    out_blocks = encoder_out.reshape(NB, BLK, HEADS, HD)
    decoder_split = decoder_queries.reshape(NDB, BLK, HEADS, HD)
    always_live = jnp.ones((CROSS * BLK,), dtype=jnp.bool_)

    def decode(block_index):
        chosen = (span_owner[block_index] * EB + cross_slots[block_index]).astype(jnp.int32)
        key_rows = key_blocks[chosen].reshape(CROSS * BLK, HEADS, HD)
        value_rows = out_blocks[chosen].reshape(CROSS * BLK, HEADS, HD)
        return attend_block(decoder_split[block_index], key_rows, value_rows, always_live)

    context = lax.map(decode, jnp.arange(NDB, dtype=jnp.int32)).reshape(DTOK, HW)
    projected = jnp.dot(context, out_weight, preferred_element_type=jnp.float32)
    decoder_out = (projected + decoder_input.astype(jnp.float32)).astype(jnp.bfloat16)
    return encoder_out, decoder_out
```

```python
import functools

import jax
import jax.numpy as jnp
from jax import lax
from jax.experimental import pallas as pl
from jax.experimental.pallas import tpu as pltpu
from jax.sharding import Mesh
from jax.sharding import PartitionSpec as P

HD = 64
BLK = 128
REACH = 2
SLOTS = 4
CROSS = 2
QUAD = 4
QW = HD * QUAD
HEAD = ("head_0", "head_1")
EXP_SCALE = 0.125 * 1.4426950408889634


def attend(q, k_blocks, v_blocks):
    lane = lax.broadcasted_iota(jnp.int32, (BLK, QW), 1) // HD
    zero = jnp.zeros_like(q)
    rows = jnp.concatenate([jnp.where(lane == h, q, zero) for h in range(QUAD)], axis=0)
    k = jnp.concatenate(k_blocks, axis=0)
    v = jnp.concatenate(v_blocks, axis=0)
    s = lax.dot_general(rows, k, (((1,), (1,)), ((), ())), preferred_element_type=jnp.float32)
    m = jnp.max(s, axis=1, keepdims=True)
    p = jnp.exp2((s - m) * EXP_SCALE)
    l = jnp.sum(p, axis=1, keepdims=True)
    o = lax.dot_general(
        p.astype(jnp.bfloat16), v, (((1,), (0,)), ((), ())), preferred_element_type=jnp.float32
    )
    o = o * (1.0 / l)
    out = o[:BLK]
    for h in range(1, QUAD):
        out = jnp.where(lane == h, o[h * BLK : (h + 1) * BLK], out)
    return out.astype(jnp.bfloat16)


def attend_listed(q_ref, k_ref, v_ref, ids, o_ref):
    for c in range(q_ref.shape[-1] // QW):
        cols = pl.ds(c * QW, QW)
        o_ref[:, cols] = attend(
            q_ref[:, cols], [k_ref[i, :, cols] for i in ids], [v_ref[i, :, cols] for i in ids]
        )


def branch_on_count(count, ids, q_ref, k_ref, v_ref, o_ref):
    for n in range(1, SLOTS + 1):

        @pl.when(count == n)
        def _(n=n):
            attend_listed(q_ref, k_ref, v_ref, ids[:n], o_ref)


def inner_kernel(counts, lists, q_ref, k_ref, v_ref, o_ref):
    b = REACH + pl.program_id(0)
    ids = [lists[b * SLOTS + j] - REACH for j in range(SLOTS)]
    branch_on_count(counts[b], ids, q_ref, k_ref, v_ref, o_ref)


def inner_call(counts, lists, q, k3, v3):
    blocks, _, width = k3.shape
    inner = blocks - 2 * REACH
    whole = pl.BlockSpec((blocks, BLK, width), lambda b, c, l: (0, 0, 0))
    return pl.pallas_call(
        inner_kernel,
        grid_spec=pltpu.PrefetchScalarGridSpec(
            num_scalar_prefetch=2,
            grid=(inner,),
            in_specs=[pl.BlockSpec((BLK, width), lambda b, c, l: (REACH + b, 0)), whole, whole],
            out_specs=pl.BlockSpec((BLK, width), lambda b, c, l: (REACH + b, 0)),
        ),
        out_shape=jax.ShapeDtypeStruct((blocks * BLK, width), jnp.bfloat16),
        cost_estimate=pl.CostEstimate(
            flops=inner * 4 * BLK * SLOTS * BLK * width * 4,
            transcendentals=inner * BLK * SLOTS * BLK * width // HD,
            bytes_accessed=20_000_000,
        ),
        name="encoder_inner",
    )(counts, lists, q, k3, v3)


def edge_block(t, last):
    return jnp.where(t < REACH, t, last - 2 * REACH + t)


def edge_kernel(counts, lists, q_ref, k_lo, k_hi, v_lo, v_hi, kb, vb, ka, va, _, o_ref, ks, vs):
    t = pl.program_id(0)
    blocks = counts.shape[0]
    near = 2 * REACH
    b = edge_block(t, blocks)

    @pl.when(t == 0)
    def _():
        ks[:REACH] = kb[...]
        ks[REACH : REACH + near] = k_lo[...]
        ks[REACH + near : REACH + 2 * near] = k_hi[...]
        ks[REACH + 2 * near :] = ka[...]
        vs[:REACH] = vb[...]
        vs[REACH : REACH + near] = v_lo[...]
        vs[REACH + near : REACH + 2 * near] = v_hi[...]
        vs[REACH + 2 * near :] = va[...]

    shift = jnp.where(t < REACH, 0, blocks - 2 * near)
    ids = [lists[b * SLOTS + j] - shift for j in range(SLOTS)]
    branch_on_count(counts[b], ids, q_ref, ks, vs, o_ref)


def edge_call(counts, lists, q, k3, v3, k_before, v_before, k_after, v_after, partial_out):
    blocks, _, width = k3.shape
    near = 2 * REACH
    last = blocks // near - 1
    lo = pl.BlockSpec((near, BLK, width), lambda t, c, l: (0, 0, 0))
    hi = pl.BlockSpec((near, BLK, width), lambda t, c, l: (last, 0, 0))
    halo = pl.BlockSpec((REACH, BLK, width), lambda t, c, l: (0, 0, 0))
    rows = pl.BlockSpec((BLK, width), lambda t, c, l: (edge_block(t, blocks), 0))
    return pl.pallas_call(
        edge_kernel,
        grid_spec=pltpu.PrefetchScalarGridSpec(
            num_scalar_prefetch=2,
            grid=(near,),
            in_specs=[rows, lo, hi, lo, hi, halo, halo, halo, halo, pl.BlockSpec(memory_space=pl.ANY)],
            out_specs=rows,
            scratch_shapes=[pltpu.VMEM((3 * near, BLK, width), jnp.bfloat16)] * 2,
        ),
        out_shape=jax.ShapeDtypeStruct((blocks * BLK, width), jnp.bfloat16),
        input_output_aliases={11: 0},
        cost_estimate=pl.CostEstimate(
            flops=near * 4 * BLK * SLOTS * BLK * width * 4,
            transcendentals=near * BLK * SLOTS * BLK * width // HD,
            bytes_accessed=10_000_000,
        ),
        name="encoder_edge",
    )(counts, lists, q, k3, k3, v3, v3, k_before, v_before, k_after, v_after, partial_out)


def serve_kernel(active, slots, q_ref, k0, k1, v0, v1, o_ref):
    t = pl.program_id(0)

    @pl.when(active[t] == 1)
    def _():
        for c in range(q_ref.shape[-1] // QW):
            cols = pl.ds(c * QW, QW)
            o_ref[:, cols] = attend(
                q_ref[:, cols], [k0[0, :, cols], k1[0, :, cols]], [v0[0, :, cols], v1[0, :, cols]]
            )

    @pl.when(active[t] == 0)
    def _():
        o_ref[...] = jnp.zeros_like(o_ref)


def serve_call(active, slots, q, k3, e3):
    width = q.shape[1]
    count = q.shape[0] // BLK
    first = pl.BlockSpec((1, BLK, width), lambda t, a, s: (s[t * CROSS], 0, 0))
    second = pl.BlockSpec((1, BLK, width), lambda t, a, s: (s[t * CROSS + 1], 0, 0))
    rows = pl.BlockSpec((BLK, width), lambda t, a, s: (t, 0))
    return pl.pallas_call(
        serve_kernel,
        grid_spec=pltpu.PrefetchScalarGridSpec(
            num_scalar_prefetch=2,
            grid=(count,),
            in_specs=[rows, first, second, first, second],
            out_specs=rows,
        ),
        out_shape=jax.ShapeDtypeStruct(q.shape, jnp.bfloat16),
        cost_estimate=pl.CostEstimate(
            flops=count * 4 * BLK * CROSS * BLK * width,
            transcendentals=count * BLK * CROSS * BLK * width // HD,
            bytes_accessed=4_000_000,
        ),
        name="serve",
    )(active, slots, q, k3, k3, e3, e3)


def project_kernel(part, c0, c1, c2, c3, w0, w1, w2, w3, r_ref, o_ref):
    total = r_ref[...].astype(jnp.float32)
    for c, w in ((c0, w0), (c1, w1), (c2, w2), (c3, w3)):
        total = total + jnp.dot(c[...], w[...], preferred_element_type=jnp.float32)
    o_ref[...] = total.astype(o_ref.dtype)


def project_call(part, contexts, own_weight, weights, residual):
    tokens, width = contexts[0].shape
    columns = residual.shape[1]
    tile = min(tokens, 256)
    c_spec = pl.BlockSpec((tile, width), lambda i, p: (i, 0))
    w_own = pl.BlockSpec((width, columns), lambda i, p: (0, p[0]))
    w_spec = pl.BlockSpec((width, columns), lambda i, p: (0, 0))
    r_spec = pl.BlockSpec((tile, columns), lambda i, p: (i, 0))
    return pl.pallas_call(
        project_kernel,
        grid_spec=pltpu.PrefetchScalarGridSpec(
            num_scalar_prefetch=1,
            grid=(tokens // tile,),
            in_specs=[c_spec] * 4 + [w_own, w_spec, w_spec, w_spec, r_spec],
            out_specs=r_spec,
        ),
        out_shape=jax.ShapeDtypeStruct(residual.shape, jnp.bfloat16),
        cost_estimate=pl.CostEstimate(
            flops=2 * tokens * width * 4 * columns, transcendentals=0, bytes_accessed=8_000_000
        ),
        name="project",
    )(part, *contexts, own_weight, *weights, residual)


def shifted(block, axis, distance):
    devices = range(lax.axis_size(axis))
    route = [(i - distance, i) for i in devices if i - distance in devices]
    return lax.ppermute(block, axis, route)


def swapped(block, flip):
    return lax.ppermute(block, HEAD, [(i, i ^ flip) for i in range(4)])


def body(
    encoder_queries,
    encoder_keys,
    encoder_values,
    block_lists,
    block_counts,
    decoder_queries,
    span_owner,
    cross_slots,
    out_weight,
    decoder_input,
):
    position = lax.axis_index("seq")
    part = lax.axis_index(HEAD)
    seq_count = lax.axis_size("seq")
    blocks = encoder_queries.shape[0] // BLK
    width = encoder_queries.shape[1]
    columns = decoder_input.shape[1]
    halo = REACH * BLK
    tail = encoder_keys.shape[0] - halo

    k_before = shifted(encoder_keys[tail:], "seq", 1)
    v_before = shifted(encoder_values[tail:], "seq", 1)
    k_after = shifted(encoder_keys[:halo], "seq", -1)
    v_after = shifted(encoder_values[:halo], "seq", -1)
    q_from_prev = shifted(decoder_queries, "seq", 1)
    q_from_next = shifted(decoder_queries, "seq", -1)
    weights = [
        swapped(lax.dynamic_slice_in_dim(out_weight, (part ^ flip) * columns, columns, 1), flip)
        for flip in (1, 2, 3)
    ]

    near = (block_lists - (position * blocks - REACH)).reshape(-1)
    k3 = encoder_keys.reshape(blocks, BLK, width)
    v3 = encoder_values.reshape(blocks, BLK, width)
    encoder_out = inner_call(block_counts, near, encoder_queries, k3, v3)
    encoder_out = edge_call(
        block_counts,
        near,
        encoder_queries,
        k3,
        v3,
        *(x.reshape(REACH, BLK, width) for x in (k_before, v_before, k_after, v_after)),
        encoder_out,
    )
    e3 = encoder_out.reshape(blocks, BLK, width)
    decoder_blocks = decoder_queries.shape[0] // BLK

    def serve(queries, source):
        valid = (source >= 0) & (source < seq_count)
        start = jnp.clip(source, 0, seq_count - 1) * decoder_blocks
        owners = lax.dynamic_slice_in_dim(span_owner, start, decoder_blocks)
        slots = lax.dynamic_slice_in_dim(cross_slots, start, decoder_blocks, 0)
        active = (valid & (owners == position)).astype(jnp.int32)
        slots = jnp.where(active[:, None] == 1, slots, 0).reshape(-1)
        return serve_call(active, slots, queries, k3, e3)

    for_prev = serve(q_from_prev, position - 1)
    back_from_next = shifted(for_prev, "seq", -1)
    for_next = serve(q_from_next, position + 1)
    back_from_prev = shifted(for_next, "seq", 1)
    own = serve(decoder_queries, position)
    context = own + back_from_next + back_from_prev
    across = swapped(context, 2)
    contexts = [context, swapped(context, 1), across, swapped(across, 1)]
    decoder_out = project_call(
        part.astype(jnp.int32).reshape(1), contexts, out_weight, weights, decoder_input
    )
    return (encoder_out, decoder_out)


def solution(mesh):
    split = Mesh(mesh.devices.reshape(mesh.shape["seq"], 2, 2), ("seq", "head_0", "head_1"))
    placed = (
        P("seq", HEAD),
        P("seq", HEAD),
        P("seq", HEAD),
        P("seq", None),
        P("seq"),
        P("seq", HEAD),
        P(),
        P(),
        P(HEAD, None),
        P("seq", HEAD),
    )
    return jax.shard_map(
        body,
        mesh=split,
        in_specs=placed,
        out_specs=(P("seq", HEAD), P("seq", HEAD)),
        check_vma=False,
    )
```

```python
import functools

import jax
import jax.numpy as jnp
from jax import lax
from jax.experimental import pallas as pl
from jax.experimental.pallas import tpu as pltpu
from jax.sharding import Mesh
from jax.sharding import PartitionSpec as P


HD = 64
BLK = 128
REACH = 2
SLOTS = 4
QUAD = 4
QW = HD * QUAD
HEAD = ("head_0", "head_1")
EXP_SCALE = 0.125 * 1.4426950408889634


def attend(q, k_blocks, v_blocks):
    lane = lax.broadcasted_iota(jnp.int32, (BLK, QW), 1) // HD
    zero = jnp.zeros_like(q)
    rows = jnp.concatenate([jnp.where(lane == h, q, zero) for h in range(QUAD)], axis=0)
    k = jnp.concatenate(k_blocks, axis=0)
    v = jnp.concatenate(v_blocks, axis=0)
    s = lax.dot_general(rows, k, (((1,), (1,)), ((), ())), preferred_element_type=jnp.float32)
    m = jnp.max(s, axis=1, keepdims=True)
    p = jnp.exp2((s - m) * EXP_SCALE)
    l = jnp.sum(p, axis=1, keepdims=True)
    o = lax.dot_general(
        p.astype(jnp.bfloat16), v, (((1,), (0,)), ((), ())), preferred_element_type=jnp.float32
    )
    o = o * (1.0 / l)
    out = o[:BLK]
    for h in range(1, QUAD):
        out = jnp.where(lane == h, o[h * BLK : (h + 1) * BLK], out)
    return out.astype(jnp.bfloat16)


def attend_listed(q_ref, k_ref, v_ref, ids, o_ref):
    for c in range(q_ref.shape[-1] // QW):
        cols = pl.ds(c * QW, QW)
        o_ref[:, cols] = attend(
            q_ref[:, cols], [k_ref[i, :, cols] for i in ids], [v_ref[i, :, cols] for i in ids]
        )


def branch_on_count(count, ids, q_ref, k_ref, v_ref, o_ref):
    for n in range(1, SLOTS + 1):

        @pl.when(count == n)
        def _(n=n):
            attend_listed(q_ref, k_ref, v_ref, ids[:n], o_ref)


def send_kernel(k, v, q, up, down, sem):
    halo = REACH * BLK
    tail = k.shape[0] - halo
    copies = [
        pltpu.make_async_copy(src, dst, sem)
        for src, dst in (
            (q, up.at[pl.ds(2 * halo, q.shape[0])]),
            (q, down.at[pl.ds(2 * halo, q.shape[0])]),
            (k.at[pl.ds(tail, halo)], up.at[pl.ds(0, halo)]),
            (k.at[pl.ds(0, halo)], down.at[pl.ds(0, halo)]),
            (v.at[pl.ds(tail, halo)], up.at[pl.ds(halo, halo)]),
            (v.at[pl.ds(0, halo)], down.at[pl.ds(halo, halo)]),
        )
    ]
    for copy in copies:
        copy.start()
    for copy in copies:
        copy.wait()


def send_call(k, v, q):
    rows = 2 * REACH * BLK + q.shape[0]
    shape = jax.ShapeDtypeStruct((rows, k.shape[1]), k.dtype)
    hbm = pl.BlockSpec(memory_space=pl.ANY)
    return pl.pallas_call(
        send_kernel,
        in_specs=[hbm] * 3,
        out_specs=[hbm] * 2,
        out_shape=[shape] * 2,
        scratch_shapes=[pltpu.SemaphoreType.DMA],
        name="pack_edges",
    )(k, v, q)


def cut_kernel(part, w, a, b, c, sem):
    columns = a.shape[1]
    copies = []
    for flip, dst in ((2, a), (3, b), (1, c)):
        start = pl.multiple_of((part[0] ^ flip) * columns, columns)
        half = w.shape[0] // 2
        for i in range(2):
            rows = pl.ds(i * half, half)
            copies.append(
                pltpu.make_async_copy(w.at[rows, pl.ds(start, columns)], dst.at[rows], sem)
            )
    for copy in copies:
        copy.start()
    for copy in copies:
        copy.wait()


def cut_call(part, w, columns):
    shape = jax.ShapeDtypeStruct((w.shape[0], columns), w.dtype)
    hbm = pl.BlockSpec(memory_space=pl.ANY)
    return pl.pallas_call(
        cut_kernel,
        in_specs=[pl.BlockSpec(memory_space=pltpu.SMEM), hbm],
        out_specs=[hbm] * 3,
        out_shape=[shape] * 3,
        scratch_shapes=[pltpu.SemaphoreType.DMA],
        name="cut_weight",
    )(part, w)


def inner_kernel(position, counts, lists, q_ref, k_ref, v_ref, o_ref):
    b = REACH + pl.program_id(0)
    base = position[0] * k_ref.shape[0]
    ids = [lists[j, b] - base for j in range(SLOTS)]
    branch_on_count(counts[b], ids, q_ref, k_ref, v_ref, o_ref)


def inner_call(position, counts, lists, q, k3, v3):
    blocks, _, width = k3.shape
    inner = blocks - 2 * REACH
    whole = pl.BlockSpec((blocks, BLK, width), lambda b, p, c, l: (0, 0, 0))
    rows = pl.BlockSpec((BLK, width), lambda b, p, c, l: (REACH + b, 0))
    return pl.pallas_call(
        inner_kernel,
        grid_spec=pltpu.PrefetchScalarGridSpec(
            num_scalar_prefetch=3, grid=(inner,), in_specs=[rows, whole, whole], out_specs=rows
        ),
        out_shape=jax.ShapeDtypeStruct((blocks * BLK, width), jnp.bfloat16),
        name="encoder_inner",
    )(position, counts, lists, q, k3, v3)


def stage_kernel(
    sources, take_needed, pos, counts, lists, owners, slots, q, k, v, up, down, dec, _, *refs
):
    e = refs[0]
    answers = refs[1 : 1 + len(sources)]
    kb, vb, eb, qe, qd, ob, sems = refs[1 + len(sources) :]
    blocks = k.shape[0]
    near = 2 * REACH
    mine = pos[0]
    per = answers[0].shape[0]
    total = owners.shape[0] // per
    hold = pl.ds(0, REACH)
    next_hold = pl.ds(REACH, REACH)
    first = [
        (up.at[hold], kb.at[pl.ds(0, REACH)]),
        (k, kb.at[pl.ds(REACH, blocks)]),
        (down.at[hold], kb.at[pl.ds(REACH + blocks, REACH)]),
        (up.at[next_hold], vb.at[pl.ds(0, REACH)]),
        (v.at[pl.ds(0, near)], vb.at[pl.ds(REACH, near)]),
        (v.at[pl.ds(blocks - near, near)], vb.at[pl.ds(REACH + blocks - near, near)]),
        (down.at[next_hold], vb.at[pl.ds(REACH + blocks, REACH)]),
        (q.at[pl.ds(0, REACH)], qe.at[pl.ds(0, REACH)]),
        (q.at[pl.ds(blocks - REACH, REACH)], qe.at[pl.ds(REACH, REACH)]),
    ]
    inner = pl.ds(REACH, blocks - near)
    second = [(e.at[inner], eb.at[inner])]
    if not take_needed:
        second = [(e, eb)]
    for i, shift in enumerate(sources):
        src = {-1: up.at[pl.ds(near, per)], 1: down.at[pl.ds(near, per)], 0: dec}[shift]
        second.append((src, qd.at[pl.ds(i * per, per)]))
    first = [pltpu.make_async_copy(a, b, sems.at[0]) for a, b in first]
    second = [pltpu.make_async_copy(a, b, sems.at[1]) for a, b in second]
    for copy in first + second:
        copy.start()

    def candidate(shift, t):
        source = mine + shift
        valid = (source >= 0) & (source < total)
        d = jnp.clip(source, 0, total - 1) * per + t
        return valid & (owners[d] == mine), slots[0, d], slots[1, d]

    needed = jnp.int32(0)
    for shift in (-1, 1):
        for t in range(per):
            live, s0, s1 = candidate(shift, t)
            bits = jnp.left_shift(jnp.int32(1), s0) | jnp.left_shift(jnp.int32(1), s1)
            needed = needed | jnp.where(live, bits, 0)

    def edge_of(t):
        return jnp.where(t < REACH, t, blocks - near + t)

    def due(t):
        return (jnp.right_shift(needed, edge_of(t)) & 1) == (1 if take_needed else 0)

    for copy in first:
        copy.wait()
    if not take_needed:
        for copy in second:
            copy.wait()

    @pl.loop(0, near)
    def _(t):
        @pl.when(due(t))
        def _():
            b = edge_of(t)
            base = mine * blocks - REACH
            ids = [lists[j, b] - base for j in range(SLOTS)]
            branch_on_count(counts[b], ids, qe.at[t], kb, vb, eb.at[b])
            pltpu.make_async_copy(eb.at[b], e.at[b], sems.at[2]).start()

    if take_needed:
        for copy in second:
            copy.wait()

    for i, shift in enumerate(sources):

        @pl.loop(0, per)
        def _(t, i=i, shift=shift):
            live, s0, s1 = candidate(shift, t)

            @pl.when(live)
            def _():
                for c in range(ob.shape[-1] // QW):
                    cols = pl.ds(c * QW, QW)
                    ob[i * per + t, :, cols] = attend(
                        qd[i * per + t, :, cols],
                        [kb[REACH + s, :, cols] for s in (s0, s1)],
                        [eb[s, :, cols] for s in (s0, s1)],
                    )

            @pl.when(jnp.logical_not(live))
            def _():
                ob[i * per + t] = jnp.zeros(ob.shape[1:], ob.dtype)

        pltpu.make_async_copy(ob.at[pl.ds(i * per, per)], answers[i], sems.at[3]).start()

    for i in range(len(sources)):
        pltpu.make_async_copy(ob.at[pl.ds(i * per, per)], answers[i], sems.at[3]).wait()

    @pl.loop(0, near)
    def _(t):
        @pl.when(due(t))
        def _():
            b = edge_of(t)
            pltpu.make_async_copy(eb.at[b], e.at[b], sems.at[2]).wait()


def stage_call(sources, take_needed, scalars, q, k3, v3, up, down, dec, e):
    blocks, _, width = k3.shape
    near = 2 * REACH
    per = dec.shape[0] // BLK
    smem = pl.BlockSpec(memory_space=pltpu.SMEM)
    hbm = pl.BlockSpec(memory_space=pl.ANY)
    answer = jax.ShapeDtypeStruct((per, BLK, width), jnp.bfloat16)

    def cut(x):
        return x.reshape(-1, BLK, width)

    def room(n):
        return pltpu.VMEM((n, BLK, width), jnp.bfloat16)

    served = per * len(sources)
    out = pl.pallas_call(
        functools.partial(stage_kernel, sources, take_needed),
        in_specs=[smem] * 5 + [hbm] * 7,
        out_specs=[hbm] * (1 + len(sources)),
        out_shape=[jax.ShapeDtypeStruct(k3.shape, jnp.bfloat16)] + [answer] * len(sources),
        scratch_shapes=[
            room(blocks + near),
            room(blocks + near),
            room(blocks),
            room(near),
            room(served),
            room(served),
            pltpu.SemaphoreType.DMA((4,)),
        ],
        input_output_aliases={11: 0},
        name="serve_remote" if take_needed else "serve_own",
    )(*scalars, cut(q), k3, v3, cut(up), cut(down), cut(dec), e)
    return out[0], [x.reshape(per * BLK, width) for x in out[1:]]


def project_kernel(part, c0, c1, c2, c3, w0, w1, w2, w3, r_ref, o_ref):
    total = r_ref[...].astype(jnp.float32)
    for c, w in ((c0, w0), (c1, w1), (c2, w2), (c3, w3)):
        total = total + jnp.dot(c[...], w[...], preferred_element_type=jnp.float32)
    o_ref[...] = total.astype(o_ref.dtype)


def project_call(part, contexts, own_weight, weights, residual):
    tokens, width = contexts[0].shape
    columns = residual.shape[1]
    tile = min(tokens, 256)
    c_spec = pl.BlockSpec((tile, width), lambda i, p: (i, 0))
    w_own = pl.BlockSpec((width, columns), lambda i, p: (0, p[0]))
    w_spec = pl.BlockSpec((width, columns), lambda i, p: (0, 0))
    r_spec = pl.BlockSpec((tile, columns), lambda i, p: (i, 0))
    return pl.pallas_call(
        project_kernel,
        grid_spec=pltpu.PrefetchScalarGridSpec(
            num_scalar_prefetch=1,
            grid=(tokens // tile,),
            in_specs=[c_spec] * 4 + [w_own, w_spec, w_spec, w_spec, r_spec],
            out_specs=r_spec,
        ),
        out_shape=jax.ShapeDtypeStruct(residual.shape, jnp.bfloat16),
        cost_estimate=pl.CostEstimate(
            flops=2 * tokens * width * 4 * columns, transcendentals=0, bytes_accessed=8_000_000
        ),
        name="project",
    )(part, *contexts, own_weight, *weights, residual)


def shifted(block, axis, distance):
    devices = range(lax.axis_size(axis))
    route = [(i - distance, i) for i in devices if i - distance in devices]
    return lax.ppermute(block, axis, route)


def swapped(block, flip):
    return lax.ppermute(block, HEAD, [(i, i ^ flip) for i in range(4)])


def body(
    encoder_queries,
    encoder_keys,
    encoder_values,
    block_lists,
    block_counts,
    decoder_queries,
    span_owner,
    cross_slots,
    out_weight,
    decoder_input,
):
    position = lax.axis_index("seq").astype(jnp.int32).reshape(1)
    part = lax.axis_index(HEAD).astype(jnp.int32).reshape(1)
    blocks = encoder_queries.shape[0] // BLK
    width = encoder_queries.shape[1]
    columns = decoder_input.shape[1]
    lists = block_lists.T
    slots = cross_slots.T
    up, down = send_call(encoder_keys, encoder_values, decoder_queries)
    up = shifted(up, "seq", 1)
    down = shifted(down, "seq", -1)
    across2, across3, across1 = cut_call(part, out_weight, columns)
    w2 = swapped(across2, 2)
    w3 = swapped(across3, 3)
    w1 = swapped(across1, 1)
    k3 = encoder_keys.reshape(blocks, BLK, width)
    v3 = encoder_values.reshape(blocks, BLK, width)
    partial = inner_call(position, block_counts, lists, encoder_queries, k3, v3)
    scalars = (position, block_counts, lists, span_owner, slots)
    shared = (encoder_queries, k3, v3, up, down, decoder_queries)
    e3, (for_prev, for_next) = stage_call(
        (-1, 1), True, scalars, *shared, partial.reshape(blocks, BLK, width)
    )
    from_next = shifted(for_prev, "seq", -1)
    from_prev = shifted(for_next, "seq", 1)
    e3, (own,) = stage_call((0,), False, scalars, *shared, e3)
    context = own + from_next + from_prev
    across = swapped(context, 2)
    beside = swapped(context, 1)
    corner = swapped(across, 1)
    decoder_out = project_call(
        part, [context, beside, across, corner], out_weight, [w1, w2, w3], decoder_input
    )
    return (e3.reshape(blocks * BLK, width), decoder_out)


def solution(mesh):
    split = Mesh(mesh.devices.reshape(mesh.shape["seq"], 2, 2), ("seq", "head_0", "head_1"))
    placed = (
        P("seq", HEAD),
        P("seq", HEAD),
        P("seq", HEAD),
        P("seq", None),
        P("seq"),
        P("seq", HEAD),
        P(),
        P(),
        P(HEAD, None),
        P("seq", HEAD),
    )
    return jax.shard_map(
        body,
        mesh=split,
        in_specs=placed,
        out_specs=(P("seq", HEAD), P("seq", HEAD)),
        check_vma=False,
    )
```

```python
import functools

import jax
import jax.numpy as jnp
from jax import lax
from jax.experimental import pallas as pl
from jax.experimental.pallas import tpu as pltpu
from jax.sharding import Mesh
from jax.sharding import PartitionSpec as P


HD = 64
BLK = 128
REACH = 2
SLOTS = 4
QUAD = 4
QW = HD * QUAD
HEAD = ("head_0", "head_1")
EXP_SCALE = 0.125 * 1.4426950408889634


def attend(q, k_blocks, v_blocks):
    lane = lax.broadcasted_iota(jnp.int32, (BLK, QW), 1) // HD
    zero = jnp.zeros_like(q)
    rows = jnp.concatenate([jnp.where(lane == h, q, zero) for h in range(QUAD)], axis=0)
    k = jnp.concatenate(k_blocks, axis=0)
    v = jnp.concatenate(v_blocks, axis=0)
    s = lax.dot_general(rows, k, (((1,), (1,)), ((), ())), preferred_element_type=jnp.float32)
    m = jnp.max(s, axis=1, keepdims=True)
    p = jnp.exp2((s - m) * EXP_SCALE)
    l = jnp.sum(p, axis=1, keepdims=True)
    o = lax.dot_general(
        p.astype(jnp.bfloat16), v, (((1,), (0,)), ((), ())), preferred_element_type=jnp.float32
    )
    o = o * (1.0 / l)
    out = o[:BLK]
    for h in range(1, QUAD):
        out = jnp.where(lane == h, o[h * BLK : (h + 1) * BLK], out)
    return out.astype(jnp.bfloat16)


def attend_listed(q_ref, k_ref, v_ref, ids, o_ref):
    for c in range(q_ref.shape[-1] // QW):
        cols = pl.ds(c * QW, QW)
        o_ref[:, cols] = attend(
            q_ref[:, cols], [k_ref[i, :, cols] for i in ids], [v_ref[i, :, cols] for i in ids]
        )


def branch_on_count(count, ids, q_ref, k_ref, v_ref, o_ref):
    for n in range(1, SLOTS + 1):

        @pl.when(count == n)
        def _(n=n):
            attend_listed(q_ref, k_ref, v_ref, ids[:n], o_ref)


def move(plan, stages, load_sem, store_sem):
    loads = [pltpu.make_async_copy(src, stages[i], load_sem.at[i]) for src, i, _ in plan]
    stores = []
    for load in loads:
        load.start()
    for load, (_, i, targets) in zip(loads, plan):
        load.wait()
        for dst in targets:
            stores.append(pltpu.make_async_copy(stages[i], dst, store_sem))
            stores[-1].start()
    for store in stores:
        store.wait()


def send_kernel(k, v, q, up, down, s0, s1, s2, s3, s4, load_sem, store_sem):
    halo = REACH * BLK
    tail = pl.ds(k.shape[0] - halo, halo)
    head = pl.ds(0, halo)
    rest = pl.ds(2 * halo, q.shape[0])
    plan = (
        (k.at[tail], 0, (up.at[head],)),
        (v.at[tail], 1, (up.at[pl.ds(halo, halo)],)),
        (k.at[head], 2, (down.at[head],)),
        (v.at[head], 3, (down.at[pl.ds(halo, halo)],)),
        (q, 4, (up.at[rest], down.at[rest])),
    )
    move(plan, (s0, s1, s2, s3, s4), load_sem, store_sem)


def send_call(k, v, q):
    halo = REACH * BLK
    width = k.shape[1]
    shape = jax.ShapeDtypeStruct((2 * halo + q.shape[0], width), k.dtype)
    hbm = pl.BlockSpec(memory_space=pl.ANY)
    return pl.pallas_call(
        send_kernel,
        in_specs=[hbm] * 3,
        out_specs=[hbm] * 2,
        out_shape=[shape] * 2,
        scratch_shapes=[pltpu.VMEM((halo, width), k.dtype)] * 4
        + [
            pltpu.VMEM(q.shape, q.dtype),
            pltpu.SemaphoreType.DMA((5,)),
            pltpu.SemaphoreType.DMA,
        ],
        name="pack_edges",
    )(k, v, q)


def cut_kernel(part, w, a, b, c, sa, sb, sc, load_sem, store_sem):
    columns = a.shape[1]
    plan = []
    for i, (flip, dst) in enumerate(((2, a), (3, b), (1, c))):
        start = pl.multiple_of((part[0] ^ flip) * columns, columns)
        plan.append((w.at[:, pl.ds(start, columns)], i, (dst,)))
    move(plan, (sa, sb, sc), load_sem, store_sem)


def cut_call(part, w, columns):
    shape = jax.ShapeDtypeStruct((w.shape[0], columns), w.dtype)
    hbm = pl.BlockSpec(memory_space=pl.ANY)
    return pl.pallas_call(
        cut_kernel,
        in_specs=[pl.BlockSpec(memory_space=pltpu.SMEM), hbm],
        out_specs=[hbm] * 3,
        out_shape=[shape] * 3,
        scratch_shapes=[pltpu.VMEM(shape.shape, w.dtype)] * 3
        + [pltpu.SemaphoreType.DMA((3,)), pltpu.SemaphoreType.DMA],
        name="cut_weight",
    )(part, w)


def inner_kernel(position, counts, lists, q_ref, k_ref, v_ref, o_ref):
    b = REACH + pl.program_id(0)
    base = position[0] * k_ref.shape[0]
    ids = [lists[j, b] - base for j in range(SLOTS)]
    branch_on_count(counts[b], ids, q_ref, k_ref, v_ref, o_ref)


def inner_call(position, counts, lists, q, k3, v3):
    blocks, _, width = k3.shape
    inner = blocks - 2 * REACH
    whole = pl.BlockSpec((blocks, BLK, width), lambda b, p, c, l: (0, 0, 0))
    rows = pl.BlockSpec((BLK, width), lambda b, p, c, l: (REACH + b, 0))
    return pl.pallas_call(
        inner_kernel,
        grid_spec=pltpu.PrefetchScalarGridSpec(
            num_scalar_prefetch=3, grid=(inner,), in_specs=[rows, whole, whole], out_specs=rows
        ),
        out_shape=jax.ShapeDtypeStruct((blocks * BLK, width), jnp.bfloat16),
        name="encoder_inner",
    )(position, counts, lists, q, k3, v3)


def stage_kernel(
    sources, take_needed, pos, counts, lists, owners, slots, q, k, v, up, down, dec, _, *refs
):
    e = refs[0]
    answers = refs[1 : 1 + len(sources)]
    kb, vb, eb, qe, qd, ob, sems = refs[1 + len(sources) :]
    blocks = k.shape[0]
    near = 2 * REACH
    mine = pos[0]
    per = answers[0].shape[0]
    total = owners.shape[0] // per
    hold = pl.ds(0, REACH)
    next_hold = pl.ds(REACH, REACH)
    first = [
        (up.at[hold], kb.at[pl.ds(0, REACH)]),
        (k, kb.at[pl.ds(REACH, blocks)]),
        (down.at[hold], kb.at[pl.ds(REACH + blocks, REACH)]),
        (up.at[next_hold], vb.at[pl.ds(0, REACH)]),
        (v.at[pl.ds(0, near)], vb.at[pl.ds(REACH, near)]),
        (v.at[pl.ds(blocks - near, near)], vb.at[pl.ds(REACH + blocks - near, near)]),
        (down.at[next_hold], vb.at[pl.ds(REACH + blocks, REACH)]),
        (q.at[pl.ds(0, REACH)], qe.at[pl.ds(0, REACH)]),
        (q.at[pl.ds(blocks - REACH, REACH)], qe.at[pl.ds(REACH, REACH)]),
    ]
    inner = pl.ds(REACH, blocks - near)
    second = [(e.at[inner], eb.at[inner])]
    if not take_needed:
        second = [(e, eb)]
    for i, shift in enumerate(sources):
        src = {-1: up.at[pl.ds(near, per)], 1: down.at[pl.ds(near, per)], 0: dec}[shift]
        second.append((src, qd.at[pl.ds(i * per, per)]))
    first = [pltpu.make_async_copy(a, b, sems.at[0]) for a, b in first]
    second = [pltpu.make_async_copy(a, b, sems.at[1]) for a, b in second]
    for copy in first + second:
        copy.start()

    def candidate(shift, t):
        source = mine + shift
        valid = (source >= 0) & (source < total)
        d = jnp.clip(source, 0, total - 1) * per + t
        return valid & (owners[d] == mine), slots[0, d], slots[1, d]

    needed = jnp.int32(0)
    for shift in (-1, 1):
        for t in range(per):
            live, s0, s1 = candidate(shift, t)
            bits = jnp.left_shift(jnp.int32(1), s0) | jnp.left_shift(jnp.int32(1), s1)
            needed = needed | jnp.where(live, bits, 0)

    def edge_of(t):
        return jnp.where(t < REACH, t, blocks - near + t)

    def due(t):
        return (jnp.right_shift(needed, edge_of(t)) & 1) == (1 if take_needed else 0)

    for copy in first:
        copy.wait()
    if not take_needed:
        for copy in second:
            copy.wait()

    @pl.loop(0, near)
    def _(t):
        @pl.when(due(t))
        def _():
            b = edge_of(t)
            base = mine * blocks - REACH
            ids = [lists[j, b] - base for j in range(SLOTS)]
            branch_on_count(counts[b], ids, qe.at[t], kb, vb, eb.at[b])
            pltpu.make_async_copy(eb.at[b], e.at[b], sems.at[2]).start()

    if take_needed:
        for copy in second:
            copy.wait()

    for i, shift in enumerate(sources):

        @pl.loop(0, per)
        def _(t, i=i, shift=shift):
            live, s0, s1 = candidate(shift, t)

            @pl.when(live)
            def _():
                for c in range(ob.shape[-1] // QW):
                    cols = pl.ds(c * QW, QW)
                    ob[i * per + t, :, cols] = attend(
                        qd[i * per + t, :, cols],
                        [kb[REACH + s, :, cols] for s in (s0, s1)],
                        [eb[s, :, cols] for s in (s0, s1)],
                    )

            @pl.when(jnp.logical_not(live))
            def _():
                ob[i * per + t] = jnp.zeros(ob.shape[1:], ob.dtype)

        pltpu.make_async_copy(ob.at[pl.ds(i * per, per)], answers[i], sems.at[3]).start()

    for i in range(len(sources)):
        pltpu.make_async_copy(ob.at[pl.ds(i * per, per)], answers[i], sems.at[3]).wait()

    @pl.loop(0, near)
    def _(t):
        @pl.when(due(t))
        def _():
            b = edge_of(t)
            pltpu.make_async_copy(eb.at[b], e.at[b], sems.at[2]).wait()


def stage_call(sources, take_needed, scalars, q, k3, v3, up, down, dec, e):
    blocks, _, width = k3.shape
    near = 2 * REACH
    per = dec.shape[0] // BLK
    smem = pl.BlockSpec(memory_space=pltpu.SMEM)
    hbm = pl.BlockSpec(memory_space=pl.ANY)
    answer = jax.ShapeDtypeStruct((per, BLK, width), jnp.bfloat16)

    def cut(x):
        return x.reshape(-1, BLK, width)

    def room(n):
        return pltpu.VMEM((n, BLK, width), jnp.bfloat16)

    served = per * len(sources)
    out = pl.pallas_call(
        functools.partial(stage_kernel, sources, take_needed),
        in_specs=[smem] * 5 + [hbm] * 7,
        out_specs=[hbm] * (1 + len(sources)),
        out_shape=[jax.ShapeDtypeStruct(k3.shape, jnp.bfloat16)] + [answer] * len(sources),
        scratch_shapes=[
            room(blocks + near),
            room(blocks + near),
            room(blocks),
            room(near),
            room(served),
            room(served),
            pltpu.SemaphoreType.DMA((4,)),
        ],
        input_output_aliases={11: 0},
        name="serve_remote" if take_needed else "serve_own",
    )(*scalars, cut(q), k3, v3, cut(up), cut(down), cut(dec), e)
    return out[0], [x.reshape(per * BLK, width) for x in out[1:]]


def project_kernel(part, c0, c1, c2, c3, w0, w1, w2, w3, r_ref, o_ref):
    total = r_ref[...].astype(jnp.float32)
    for c, w in ((c0, w0), (c1, w1), (c2, w2), (c3, w3)):
        total = total + jnp.dot(c[...], w[...], preferred_element_type=jnp.float32)
    o_ref[...] = total.astype(o_ref.dtype)


def project_call(part, contexts, own_weight, weights, residual):
    tokens, width = contexts[0].shape
    columns = residual.shape[1]
    tile = min(tokens, 256)
    c_spec = pl.BlockSpec((tile, width), lambda i, p: (i, 0))
    w_own = pl.BlockSpec((width, columns), lambda i, p: (0, p[0]))
    w_spec = pl.BlockSpec((width, columns), lambda i, p: (0, 0))
    r_spec = pl.BlockSpec((tile, columns), lambda i, p: (i, 0))
    return pl.pallas_call(
        project_kernel,
        grid_spec=pltpu.PrefetchScalarGridSpec(
            num_scalar_prefetch=1,
            grid=(tokens // tile,),
            in_specs=[c_spec] * 4 + [w_own, w_spec, w_spec, w_spec, r_spec],
            out_specs=r_spec,
        ),
        out_shape=jax.ShapeDtypeStruct(residual.shape, jnp.bfloat16),
        cost_estimate=pl.CostEstimate(
            flops=2 * tokens * width * 4 * columns, transcendentals=0, bytes_accessed=8_000_000
        ),
        name="project",
    )(part, *contexts, own_weight, *weights, residual)


def shifted(block, axis, distance):
    devices = range(lax.axis_size(axis))
    route = [(i - distance, i) for i in devices if i - distance in devices]
    return lax.ppermute(block, axis, route)


def swapped(block, flip):
    return lax.ppermute(block, HEAD, [(i, i ^ flip) for i in range(4)])


def body(
    encoder_queries,
    encoder_keys,
    encoder_values,
    block_lists,
    block_counts,
    decoder_queries,
    span_owner,
    cross_slots,
    out_weight,
    decoder_input,
):
    position = lax.axis_index("seq").astype(jnp.int32).reshape(1)
    part = lax.axis_index(HEAD).astype(jnp.int32).reshape(1)
    blocks = encoder_queries.shape[0] // BLK
    width = encoder_queries.shape[1]
    columns = decoder_input.shape[1]
    lists = block_lists.T
    slots = cross_slots.T
    up, down = send_call(encoder_keys, encoder_values, decoder_queries)
    up = shifted(up, "seq", 1)
    down = shifted(down, "seq", -1)
    across2, across3, across1 = cut_call(part, out_weight, columns)
    w2 = swapped(across2, 2)
    w3 = swapped(across3, 3)
    w1 = swapped(across1, 1)
    k3 = encoder_keys.reshape(blocks, BLK, width)
    v3 = encoder_values.reshape(blocks, BLK, width)
    partial = inner_call(position, block_counts, lists, encoder_queries, k3, v3)
    scalars = (position, block_counts, lists, span_owner, slots)
    shared = (encoder_queries, k3, v3, up, down, decoder_queries)
    e3, (for_prev, for_next) = stage_call(
        (-1, 1), True, scalars, *shared, partial.reshape(blocks, BLK, width)
    )
    from_next = shifted(for_prev, "seq", -1)
    from_prev = shifted(for_next, "seq", 1)
    e3, (own,) = stage_call((0,), False, scalars, *shared, e3)
    context = own + from_next + from_prev
    across = swapped(context, 2)
    beside = swapped(context, 1)
    corner = swapped(across, 1)
    decoder_out = project_call(
        part, [context, beside, across, corner], out_weight, [w1, w2, w3], decoder_input
    )
    return (e3.reshape(blocks * BLK, width), decoder_out)


def solution(mesh):
    split = Mesh(mesh.devices.reshape(mesh.shape["seq"], 2, 2), ("seq", "head_0", "head_1"))
    placed = (
        P("seq", HEAD),
        P("seq", HEAD),
        P("seq", HEAD),
        P("seq", None),
        P("seq"),
        P("seq", HEAD),
        P(),
        P(),
        P(HEAD, None),
        P("seq", HEAD),
    )
    return jax.shard_map(
        body,
        mesh=split,
        in_specs=placed,
        out_specs=(P("seq", HEAD), P("seq", HEAD)),
        check_vma=False,
    )
```

```python
import functools

import jax
import jax.numpy as jnp
from jax import lax
from jax.experimental import pallas as pl
from jax.experimental.pallas import tpu as pltpu
from jax.sharding import Mesh
from jax.sharding import PartitionSpec as P


HD = 64
BLK = 128
REACH = 2
SLOTS = 4
QUAD = 4
Z_CHIPS = 8
QW = HD * QUAD
HEAD = ("head_0", "head_1")
EXP_SCALE = 0.125 * 1.4426950408889634


def attend(q, k_blocks, v_blocks):
    lane = lax.broadcasted_iota(jnp.int32, (BLK, QW), 1) // HD
    zero = jnp.zeros_like(q)
    rows = jnp.concatenate([jnp.where(lane == h, q, zero) for h in range(QUAD)], axis=0)
    k = jnp.concatenate(k_blocks, axis=0)
    v = jnp.concatenate(v_blocks, axis=0)
    s = lax.dot_general(rows, k, (((1,), (1,)), ((), ())), preferred_element_type=jnp.float32)
    m = jnp.max(s, axis=1, keepdims=True)
    p = jnp.exp2((s - m) * EXP_SCALE)
    l = jnp.sum(p, axis=1, keepdims=True)
    o = lax.dot_general(
        p.astype(jnp.bfloat16), v, (((1,), (0,)), ((), ())), preferred_element_type=jnp.float32
    )
    o = o * (1.0 / l)
    out = o[:BLK]
    for h in range(1, QUAD):
        out = jnp.where(lane == h, o[h * BLK : (h + 1) * BLK], out)
    return out.astype(jnp.bfloat16)


def attend_listed(q_ref, k_ref, v_ref, ids, o_ref):
    for c in range(q_ref.shape[-1] // QW):
        cols = pl.ds(c * QW, QW)
        o_ref[:, cols] = attend(
            q_ref[:, cols], [k_ref[i, :, cols] for i in ids], [v_ref[i, :, cols] for i in ids]
        )


def branch_on_count(count, ids, q_ref, k_ref, v_ref, o_ref):
    for n in range(1, SLOTS + 1):

        @pl.when(count == n)
        def _(n=n):
            attend_listed(q_ref, k_ref, v_ref, ids[:n], o_ref)


def move(plan, stages, load_sem, store_sem):
    loads = [pltpu.make_async_copy(src, stages[i], load_sem.at[i]) for src, i, _ in plan]
    stores = []
    for load in loads:
        load.start()
    for load, (_, i, targets) in zip(loads, plan):
        load.wait()
        for dst in targets:
            stores.append(pltpu.make_async_copy(stages[i], dst, store_sem))
            stores[-1].start()
    for store in stores:
        store.wait()


def send_kernel(k, v, q, up, down, s0, s1, s2, s3, s4, load_sem, store_sem):
    halo = REACH * BLK
    tail = pl.ds(k.shape[0] - halo, halo)
    head = pl.ds(0, halo)
    rest = pl.ds(2 * halo, q.shape[0])
    plan = (
        (k.at[tail], 0, (up.at[head],)),
        (v.at[tail], 1, (up.at[pl.ds(halo, halo)],)),
        (k.at[head], 2, (down.at[head],)),
        (v.at[head], 3, (down.at[pl.ds(halo, halo)],)),
        (q, 4, (up.at[rest], down.at[rest])),
    )
    move(plan, (s0, s1, s2, s3, s4), load_sem, store_sem)


def send_call(k, v, q):
    halo = REACH * BLK
    width = k.shape[1]
    shape = jax.ShapeDtypeStruct((2 * halo + q.shape[0], width), k.dtype)
    hbm = pl.BlockSpec(memory_space=pl.ANY)
    return pl.pallas_call(
        send_kernel,
        in_specs=[hbm] * 3,
        out_specs=[hbm] * 2,
        out_shape=[shape] * 2,
        scratch_shapes=[pltpu.VMEM((halo, width), k.dtype)] * 4
        + [
            pltpu.VMEM(q.shape, q.dtype),
            pltpu.SemaphoreType.DMA((5,)),
            pltpu.SemaphoreType.DMA,
        ],
        name="pack_edges",
    )(k, v, q)


def cut_kernel(part, w, a, b, c, sa, sb, sc, load_sem, store_sem):
    columns = a.shape[1]
    plan = []
    for i, (flip, dst) in enumerate(((2, a), (3, b), (1, c))):
        start = pl.multiple_of((part[0] ^ flip) * columns, columns)
        plan.append((w.at[:, pl.ds(start, columns)], i, (dst,)))
    move(plan, (sa, sb, sc), load_sem, store_sem)


def cut_call(part, w, columns):
    shape = jax.ShapeDtypeStruct((w.shape[0], columns), w.dtype)
    hbm = pl.BlockSpec(memory_space=pl.ANY)
    return pl.pallas_call(
        cut_kernel,
        in_specs=[pl.BlockSpec(memory_space=pltpu.SMEM), hbm],
        out_specs=[hbm] * 3,
        out_shape=[shape] * 3,
        scratch_shapes=[pltpu.VMEM(shape.shape, w.dtype)] * 3
        + [pltpu.SemaphoreType.DMA((3,)), pltpu.SemaphoreType.DMA],
        name="cut_weight",
    )(part, w)


def inner_kernel(position, counts, lists, q_ref, k_ref, v_ref, o_ref):
    b = REACH + pl.program_id(0)
    base = position[0] * k_ref.shape[0]
    ids = [lists[j, b] - base for j in range(SLOTS)]
    branch_on_count(counts[b], ids, q_ref, k_ref, v_ref, o_ref)


def inner_call(position, counts, lists, q, k3, v3):
    blocks, _, width = k3.shape
    inner = blocks - 2 * REACH
    whole = pl.BlockSpec((blocks, BLK, width), lambda b, p, c, l: (0, 0, 0))
    rows = pl.BlockSpec((BLK, width), lambda b, p, c, l: (REACH + b, 0))
    return pl.pallas_call(
        inner_kernel,
        grid_spec=pltpu.PrefetchScalarGridSpec(
            num_scalar_prefetch=3, grid=(inner,), in_specs=[rows, whole, whole], out_specs=rows
        ),
        out_shape=jax.ShapeDtypeStruct((blocks * BLK, width), jnp.bfloat16),
        name="encoder_inner",
    )(position, counts, lists, q, k3, v3)


def stage_kernel(
    sources, take_needed, pos, counts, lists, owners, slots, q, k, v, up, down, dec, _, *refs
):
    e = refs[0]
    answers = refs[1 : 1 + len(sources)]
    kb, vb, eb, qe, qd, ob, sems = refs[1 + len(sources) :]
    blocks = k.shape[0]
    near = 2 * REACH
    mine = pos[0]
    per = answers[0].shape[0]
    total = owners.shape[0] // per
    hold = pl.ds(0, REACH)
    next_hold = pl.ds(REACH, REACH)
    first = [
        (up.at[hold], kb.at[pl.ds(0, REACH)]),
        (k, kb.at[pl.ds(REACH, blocks)]),
        (down.at[hold], kb.at[pl.ds(REACH + blocks, REACH)]),
        (up.at[next_hold], vb.at[pl.ds(0, REACH)]),
        (v.at[pl.ds(0, near)], vb.at[pl.ds(REACH, near)]),
        (v.at[pl.ds(blocks - near, near)], vb.at[pl.ds(REACH + blocks - near, near)]),
        (down.at[next_hold], vb.at[pl.ds(REACH + blocks, REACH)]),
        (q.at[pl.ds(0, REACH)], qe.at[pl.ds(0, REACH)]),
        (q.at[pl.ds(blocks - REACH, REACH)], qe.at[pl.ds(REACH, REACH)]),
    ]
    inner = pl.ds(REACH, blocks - near)
    second = [(e.at[inner], eb.at[inner])]
    if not take_needed:
        second = [(e, eb)]
    for i, shift in enumerate(sources):
        src = {-1: up.at[pl.ds(near, per)], 1: down.at[pl.ds(near, per)], 0: dec}[shift]
        second.append((src, qd.at[pl.ds(i * per, per)]))
    first = [pltpu.make_async_copy(a, b, sems.at[0]) for a, b in first]
    second = [pltpu.make_async_copy(a, b, sems.at[1]) for a, b in second]
    for copy in first + second:
        copy.start()

    def candidate(shift, t):
        source = mine + shift
        valid = (source >= 0) & (source < total)
        d = jnp.clip(source, 0, total - 1) * per + t
        return valid & (owners[d] == mine), slots[0, d], slots[1, d]

    needed = jnp.int32(0)
    for shift in (-1, 1):
        for t in range(per):
            live, s0, s1 = candidate(shift, t)
            bits = jnp.left_shift(jnp.int32(1), s0) | jnp.left_shift(jnp.int32(1), s1)
            needed = needed | jnp.where(live, bits, 0)

    def edge_of(t):
        return jnp.where(t < REACH, t, blocks - near + t)

    def due(t):
        return (jnp.right_shift(needed, edge_of(t)) & 1) == (1 if take_needed else 0)

    for copy in first:
        copy.wait()
    if not take_needed:
        for copy in second:
            copy.wait()

    @pl.loop(0, near)
    def _(t):
        @pl.when(due(t))
        def _():
            b = edge_of(t)
            base = mine * blocks - REACH
            ids = [lists[j, b] - base for j in range(SLOTS)]
            branch_on_count(counts[b], ids, qe.at[t], kb, vb, eb.at[b])
            pltpu.make_async_copy(eb.at[b], e.at[b], sems.at[2]).start()

    if take_needed:
        for copy in second:
            copy.wait()

    for i, shift in enumerate(sources):

        @pl.loop(0, per)
        def _(t, i=i, shift=shift):
            live, s0, s1 = candidate(shift, t)

            @pl.when(live)
            def _():
                for c in range(ob.shape[-1] // QW):
                    cols = pl.ds(c * QW, QW)
                    ob[i * per + t, :, cols] = attend(
                        qd[i * per + t, :, cols],
                        [kb[REACH + s, :, cols] for s in (s0, s1)],
                        [eb[s, :, cols] for s in (s0, s1)],
                    )

            @pl.when(jnp.logical_not(live))
            def _():
                ob[i * per + t] = jnp.zeros(ob.shape[1:], ob.dtype)

        pltpu.make_async_copy(ob.at[pl.ds(i * per, per)], answers[i], sems.at[3]).start()

    for i in range(len(sources)):
        pltpu.make_async_copy(ob.at[pl.ds(i * per, per)], answers[i], sems.at[3]).wait()

    @pl.loop(0, near)
    def _(t):
        @pl.when(due(t))
        def _():
            b = edge_of(t)
            pltpu.make_async_copy(eb.at[b], e.at[b], sems.at[2]).wait()


def stage_call(sources, take_needed, scalars, q, k3, v3, up, down, dec, e):
    blocks, _, width = k3.shape
    near = 2 * REACH
    per = dec.shape[0] // BLK
    smem = pl.BlockSpec(memory_space=pltpu.SMEM)
    hbm = pl.BlockSpec(memory_space=pl.ANY)
    answer = jax.ShapeDtypeStruct((per, BLK, width), jnp.bfloat16)

    def cut(x):
        return x.reshape(-1, BLK, width)

    def room(n):
        return pltpu.VMEM((n, BLK, width), jnp.bfloat16)

    served = per * len(sources)
    out = pl.pallas_call(
        functools.partial(stage_kernel, sources, take_needed),
        in_specs=[smem] * 5 + [hbm] * 7,
        out_specs=[hbm] * (1 + len(sources)),
        out_shape=[jax.ShapeDtypeStruct(k3.shape, jnp.bfloat16)] + [answer] * len(sources),
        scratch_shapes=[
            room(blocks + near),
            room(blocks + near),
            room(blocks),
            room(near),
            room(served),
            room(served),
            pltpu.SemaphoreType.DMA((4,)),
        ],
        input_output_aliases={11: 0},
        name="serve_remote" if take_needed else "serve_own",
    )(*scalars, cut(q), k3, v3, cut(up), cut(down), cut(dec), e)
    return out[0], [x.reshape(per * BLK, width) for x in out[1:]]


def project_kernel(part, c0, c1, w0, w1, r_ref, o_ref):
    total = r_ref[...].astype(jnp.float32)
    for c, w in ((c0, w0), (c1, w1)):
        total = total + jnp.dot(c[...], w[...], preferred_element_type=jnp.float32)
    o_ref[...] = total.astype(o_ref.dtype)


def project_call(part, contexts, weights, added, dtype):
    tokens, width = contexts[0].shape
    columns = added.shape[1]
    tile = min(tokens, 256)
    c_spec = pl.BlockSpec((tile, width), lambda i, p: (i, 0))
    w_specs = [
        pl.BlockSpec((width, columns), lambda i, p: (0, p[0]))
        if w.shape[1] > columns
        else pl.BlockSpec((width, columns), lambda i, p: (0, 0))
        for w in weights
    ]
    r_spec = pl.BlockSpec((tile, columns), lambda i, p: (i, 0))
    return pl.pallas_call(
        project_kernel,
        grid_spec=pltpu.PrefetchScalarGridSpec(
            num_scalar_prefetch=1,
            grid=(tokens // tile,),
            in_specs=[c_spec] * 2 + w_specs + [r_spec],
            out_specs=r_spec,
        ),
        out_shape=jax.ShapeDtypeStruct(added.shape, dtype),
    )(part, *contexts, *weights, added)


def shifted(block, axis, distance):
    devices = range(lax.axis_size(axis))
    route = [(i - distance, i) for i in devices if i - distance in devices]
    return lax.ppermute(block, axis, route)


def swapped(block, flip):
    return lax.ppermute(block, HEAD, [(i, i ^ flip) for i in range(4)])


def other_side(block, flip):
    axes = ("seq", *HEAD)
    route = []
    for s in range(lax.axis_size("seq")):
        for h in range(4):
            route.append((s * 4 + h, (s ^ Z_CHIPS) * 4 + (h ^ flip)))
    return lax.ppermute(block, axes, route)


def body(
    encoder_queries,
    encoder_keys,
    encoder_values,
    block_lists,
    block_counts,
    decoder_queries,
    span_owner,
    cross_slots,
    out_weight,
    decoder_input,
):
    position = lax.axis_index("seq").astype(jnp.int32).reshape(1)
    part = lax.axis_index(HEAD).astype(jnp.int32).reshape(1)
    blocks = encoder_queries.shape[0] // BLK
    width = encoder_queries.shape[1]
    columns = decoder_input.shape[1]
    lists = block_lists.T
    slots = cross_slots.T
    up, down = send_call(encoder_keys, encoder_values, decoder_queries)
    up = shifted(up, "seq", 1)
    down = shifted(down, "seq", -1)
    across2, across3, across1 = cut_call(part, out_weight, columns)
    w2 = swapped(across2, 2)
    w3 = other_side(across3, 3)
    w1 = swapped(across1, 1)
    k3 = encoder_keys.reshape(blocks, BLK, width)
    v3 = encoder_values.reshape(blocks, BLK, width)
    partial = inner_call(position, block_counts, lists, encoder_queries, k3, v3)
    scalars = (position, block_counts, lists, span_owner, slots)
    shared = (encoder_queries, k3, v3, up, down, decoder_queries)
    e3, (for_prev, for_next) = stage_call(
        (-1, 1), True, scalars, *shared, partial.reshape(blocks, BLK, width)
    )
    from_next = shifted(for_prev, "seq", -1)
    from_prev = shifted(for_next, "seq", 1)
    e3, (own,) = stage_call((0,), False, scalars, *shared, e3)
    context = own + from_next + from_prev
    across = swapped(context, 2)
    beside = swapped(context, 1)
    corner = swapped(across, 1)
    total = project_call(part, [context, beside], [out_weight, w1], decoder_input, jnp.float32)
    decoder_out = project_call(part, [across, corner], [w2, w3], total, jnp.bfloat16)
    return (e3.reshape(blocks * BLK, width), decoder_out)


def solution(mesh):
    split = Mesh(mesh.devices.reshape(mesh.shape["seq"], 2, 2), ("seq", "head_0", "head_1"))
    placed = (
        P("seq", HEAD),
        P("seq", HEAD),
        P("seq", HEAD),
        P("seq", None),
        P("seq"),
        P("seq", HEAD),
        P(),
        P(),
        P(HEAD, None),
        P("seq", HEAD),
    )
    return jax.shard_map(
        body,
        mesh=split,
        in_specs=placed,
        out_specs=(P("seq", HEAD), P("seq", HEAD)),
        check_vma=False,
    )
```

```python
import functools

import jax
import jax.numpy as jnp
from jax import lax
from jax.experimental import pallas as pl
from jax.experimental.pallas import tpu as pltpu
from jax.sharding import Mesh
from jax.sharding import PartitionSpec as P


HD = 64
BLK = 128
REACH = 2
SLOTS = 4
QUAD = 4
Z_CHIPS = 8
QW = HD * QUAD
HEAD = ("head_0", "head_1")
EXP_SCALE = 0.125 * 1.4426950408889634


def attend(q, k_blocks, v_blocks):
    lane = lax.broadcasted_iota(jnp.int32, (BLK, QW), 1) // HD
    zero = jnp.zeros_like(q)
    rows = jnp.concatenate([jnp.where(lane == h, q, zero) for h in range(QUAD)], axis=0)
    k = jnp.concatenate(k_blocks, axis=0)
    v = jnp.concatenate(v_blocks, axis=0)
    s = lax.dot_general(rows, k, (((1,), (1,)), ((), ())), preferred_element_type=jnp.float32)
    m = jnp.max(s, axis=1, keepdims=True)
    p = jnp.exp2((s - m) * EXP_SCALE)
    l = jnp.sum(p, axis=1, keepdims=True)
    o = lax.dot_general(
        p.astype(jnp.bfloat16), v, (((1,), (0,)), ((), ())), preferred_element_type=jnp.float32
    )
    o = o * (1.0 / l)
    out = o[:BLK]
    for h in range(1, QUAD):
        out = jnp.where(lane == h, o[h * BLK : (h + 1) * BLK], out)
    return out.astype(jnp.bfloat16)


def attend_listed(q_ref, k_ref, v_ref, ids, o_ref):
    for c in range(q_ref.shape[-1] // QW):
        cols = pl.ds(c * QW, QW)
        o_ref[:, cols] = attend(
            q_ref[:, cols], [k_ref[i, :, cols] for i in ids], [v_ref[i, :, cols] for i in ids]
        )


def branch_on_count(count, ids, q_ref, k_ref, v_ref, o_ref):
    for n in range(1, SLOTS + 1):

        @pl.when(count == n)
        def _(n=n):
            attend_listed(q_ref, k_ref, v_ref, ids[:n], o_ref)


def send_kernel(pos, k, v, q, near, far, s0, s1, s2, s3, s4, load_sem, store_sem):
    halo = REACH * BLK
    tail = pl.ds(k.shape[0] - halo, halo)
    head = pl.ds(0, halo)
    rest = pl.ds(2 * halo, q.shape[0])
    values = pl.ds(halo, halo)
    stages = (s0, s1, s2, s3, s4)
    sources = (k.at[tail], v.at[tail], k.at[head], v.at[head], q)
    loads = [pltpu.make_async_copy(x, stages[i], load_sem.at[i]) for i, x in enumerate(sources)]
    for load in loads:
        load.start()
    for load in loads:
        load.wait()

    def stores(up, down):
        pairs = (
            (s0, up.at[head]),
            (s1, up.at[values]),
            (s2, down.at[head]),
            (s3, down.at[values]),
            (s4, up.at[rest]),
            (s4, down.at[rest]),
        )
        return [pltpu.make_async_copy(a, b, store_sem) for a, b in pairs]

    even = pos[0] % 2 == 0

    @pl.when(even)
    def _():
        for store in stores(near, far):
            store.start()

    @pl.when(jnp.logical_not(even))
    def _():
        for store in stores(far, near):
            store.start()

    for store in stores(near, far):
        store.wait()


def send_call(position, k, v, q):
    halo = REACH * BLK
    width = k.shape[1]
    shape = jax.ShapeDtypeStruct((2 * halo + q.shape[0], width), k.dtype)
    hbm = pl.BlockSpec(memory_space=pl.ANY)
    return pl.pallas_call(
        send_kernel,
        in_specs=[pl.BlockSpec(memory_space=pltpu.SMEM)] + [hbm] * 3,
        out_specs=[hbm] * 2,
        out_shape=[shape] * 2,
        scratch_shapes=[pltpu.VMEM((halo, width), k.dtype)] * 4
        + [
            pltpu.VMEM(q.shape, q.dtype),
            pltpu.SemaphoreType.DMA((5,)),
            pltpu.SemaphoreType.DMA,
        ],
        name="pack_edges",
    )(position, k, v, q)


def move(plan, stages, load_sem, store_sem):
    loads = [pltpu.make_async_copy(src, stages[i], load_sem.at[i]) for i, (src, _) in enumerate(plan)]
    stores = [pltpu.make_async_copy(stages[i], dst, store_sem) for i, (_, dst) in enumerate(plan)]
    for load in loads:
        load.start()
    for load, store in zip(loads, stores):
        load.wait()
        store.start()
    for store in stores:
        store.wait()


def cut_kernel(part, w, a, b, c, sa, sb, sc, load_sem, store_sem):
    columns = a.shape[1]
    plan = []
    for flip, dst in ((2, a), (3, b), (1, c)):
        start = pl.multiple_of((part[0] ^ flip) * columns, columns)
        plan.append((w.at[:, pl.ds(start, columns)], dst))
    move(plan, (sa, sb, sc), load_sem, store_sem)


def cut_call(part, w, columns):
    shape = jax.ShapeDtypeStruct((w.shape[0], columns), w.dtype)
    hbm = pl.BlockSpec(memory_space=pl.ANY)
    return pl.pallas_call(
        cut_kernel,
        in_specs=[pl.BlockSpec(memory_space=pltpu.SMEM), hbm],
        out_specs=[hbm] * 3,
        out_shape=[shape] * 3,
        scratch_shapes=[pltpu.VMEM(shape.shape, w.dtype)] * 3
        + [pltpu.SemaphoreType.DMA((3,)), pltpu.SemaphoreType.DMA],
        name="cut_weight",
    )(part, w)


def inner_kernel(position, counts, lists, q_ref, k_ref, v_ref, o_ref):
    b = REACH + pl.program_id(0)
    base = position[0] * k_ref.shape[0]
    ids = [lists[j, b] - base for j in range(SLOTS)]
    branch_on_count(counts[b], ids, q_ref, k_ref, v_ref, o_ref)


def inner_call(position, counts, lists, q, k3, v3):
    blocks, _, width = k3.shape
    inner = blocks - 2 * REACH
    whole = pl.BlockSpec((blocks, BLK, width), lambda b, p, c, l: (0, 0, 0))
    rows = pl.BlockSpec((BLK, width), lambda b, p, c, l: (REACH + b, 0))
    return pl.pallas_call(
        inner_kernel,
        grid_spec=pltpu.PrefetchScalarGridSpec(
            num_scalar_prefetch=3, grid=(inner,), in_specs=[rows, whole, whole], out_specs=rows
        ),
        out_shape=jax.ShapeDtypeStruct((blocks * BLK, width), jnp.bfloat16),
        name="encoder_inner",
    )(position, counts, lists, q, k3, v3)


def stage_kernel(
    sources, take_needed, pos, counts, lists, owners, slots, q, k, v, beside, beyond, dec, _, *refs
):
    e = refs[0]
    answers = refs[1 : 1 + len(sources)]
    kb, vb, eb, qe, qd, ob, sems = refs[1 + len(sources) :]
    blocks = k.shape[0]
    near = 2 * REACH
    mine = pos[0]
    per = answers[0].shape[0]
    total = owners.shape[0] // per
    even = mine % 2 == 0
    inner = pl.ds(REACH, blocks - near)
    edge_sem, rest_sem, edge_out_sem, answer_sem = (sems.at[i] for i in range(4))

    def from_neighbours(up, down):
        first = [
            (up.at[pl.ds(0, REACH)], kb.at[pl.ds(0, REACH)]),
            (down.at[pl.ds(0, REACH)], kb.at[pl.ds(REACH + blocks, REACH)]),
            (up.at[pl.ds(REACH, REACH)], vb.at[pl.ds(0, REACH)]),
            (down.at[pl.ds(REACH, REACH)], vb.at[pl.ds(REACH + blocks, REACH)]),
        ]
        second = []
        for i, shift in enumerate(sources):
            if shift:
                src = (up if shift < 0 else down).at[pl.ds(near, per)]
                second.append((src, qd.at[pl.ds(i * per, per)]))
        return [pltpu.make_async_copy(a, b, edge_sem) for a, b in first], [
            pltpu.make_async_copy(a, b, rest_sem) for a, b in second
        ]

    first = [
        (k, kb.at[pl.ds(REACH, blocks)]),
        (v.at[pl.ds(0, near)], vb.at[pl.ds(REACH, near)]),
        (v.at[pl.ds(blocks - near, near)], vb.at[pl.ds(REACH + blocks - near, near)]),
        (q.at[pl.ds(0, REACH)], qe.at[pl.ds(0, REACH)]),
        (q.at[pl.ds(blocks - REACH, REACH)], qe.at[pl.ds(REACH, REACH)]),
    ]
    second = [(e.at[inner], eb.at[inner]) if take_needed else (e, eb)]
    if 0 in sources:
        second.append((dec, qd.at[pl.ds(sources.index(0) * per, per)]))
    first = [pltpu.make_async_copy(a, b, edge_sem) for a, b in first]
    second = [pltpu.make_async_copy(a, b, rest_sem) for a, b in second]

    @pl.when(even)
    def _():
        for group in from_neighbours(beyond, beside):
            for copy in group:
                copy.start()

    @pl.when(jnp.logical_not(even))
    def _():
        for group in from_neighbours(beside, beyond):
            for copy in group:
                copy.start()

    for copy in first + second:
        copy.start()
    more_first, more_second = from_neighbours(beyond, beside)
    first += more_first
    second += more_second

    def candidate(shift, t):
        source = mine + shift
        valid = (source >= 0) & (source < total)
        d = jnp.clip(source, 0, total - 1) * per + t
        return valid & (owners[d] == mine), slots[0, d], slots[1, d]

    needed = jnp.int32(0)
    for shift in (-1, 1):
        for t in range(per):
            live, s0, s1 = candidate(shift, t)
            bits = jnp.left_shift(jnp.int32(1), s0) | jnp.left_shift(jnp.int32(1), s1)
            needed = needed | jnp.where(live, bits, 0)

    def edge_of(t):
        return jnp.where(t < REACH, t, blocks - near + t)

    def due(t):
        return (jnp.right_shift(needed, edge_of(t)) & 1) == (1 if take_needed else 0)

    for copy in first:
        copy.wait()
    if not take_needed:
        for copy in second:
            copy.wait()

    @pl.loop(0, near)
    def _(t):
        @pl.when(due(t))
        def _():
            b = edge_of(t)
            base = mine * blocks - REACH
            ids = [lists[j, b] - base for j in range(SLOTS)]
            branch_on_count(counts[b], ids, qe.at[t], kb, vb, eb.at[b])
            pltpu.make_async_copy(eb.at[b], e.at[b], edge_out_sem).start()

    if take_needed:
        for copy in second:
            copy.wait()

    for i, shift in enumerate(sources):

        @pl.loop(0, per)
        def _(t, i=i, shift=shift):
            live, s0, s1 = candidate(shift, t)

            @pl.when(live)
            def _():
                for c in range(ob.shape[-1] // QW):
                    cols = pl.ds(c * QW, QW)
                    ob[i * per + t, :, cols] = attend(
                        qd[i * per + t, :, cols],
                        [kb[REACH + s, :, cols] for s in (s0, s1)],
                        [eb[s, :, cols] for s in (s0, s1)],
                    )

            @pl.when(jnp.logical_not(live))
            def _():
                ob[i * per + t] = jnp.zeros(ob.shape[1:], ob.dtype)

        rows = ob.at[pl.ds(i * per, per)]
        if shift == 0:
            pltpu.make_async_copy(rows, answers[0], answer_sem).start()
        else:
            to_beside = even if shift > 0 else jnp.logical_not(even)

            @pl.when(to_beside)
            def _(rows=rows):
                pltpu.make_async_copy(rows, answers[0], answer_sem).start()

            @pl.when(jnp.logical_not(to_beside))
            def _(rows=rows):
                pltpu.make_async_copy(rows, answers[1], answer_sem).start()

    for i in range(len(sources)):
        pltpu.make_async_copy(ob.at[pl.ds(i * per, per)], answers[i], answer_sem).wait()

    @pl.loop(0, near)
    def _(t):
        @pl.when(due(t))
        def _():
            b = edge_of(t)
            pltpu.make_async_copy(eb.at[b], e.at[b], edge_out_sem).wait()


def stage_call(sources, take_needed, scalars, q, k3, v3, beside, beyond, dec, e):
    blocks, _, width = k3.shape
    near = 2 * REACH
    per = dec.shape[0] // BLK
    smem = pl.BlockSpec(memory_space=pltpu.SMEM)
    hbm = pl.BlockSpec(memory_space=pl.ANY)
    answer = jax.ShapeDtypeStruct((per, BLK, width), jnp.bfloat16)

    def cut(x):
        return x.reshape(-1, BLK, width)

    def room(n):
        return pltpu.VMEM((n, BLK, width), jnp.bfloat16)

    served = per * len(sources)
    out = pl.pallas_call(
        functools.partial(stage_kernel, sources, take_needed),
        in_specs=[smem] * 5 + [hbm] * 7,
        out_specs=[hbm] * (1 + len(sources)),
        out_shape=[jax.ShapeDtypeStruct(k3.shape, jnp.bfloat16)] + [answer] * len(sources),
        scratch_shapes=[
            room(blocks + near),
            room(blocks + near),
            room(blocks),
            room(near),
            room(served),
            room(served),
            pltpu.SemaphoreType.DMA((4,)),
        ],
        input_output_aliases={11: 0},
        name="serve_remote" if take_needed else "serve_own",
    )(*scalars, cut(q), k3, v3, cut(beside), cut(beyond), cut(dec), e)
    return out[0], [x.reshape(per * BLK, width) for x in out[1:]]


def project_kernel(part, c0, c1, w0, w1, r_ref, o_ref):
    total = r_ref[...].astype(jnp.float32)
    for c, w in ((c0, w0), (c1, w1)):
        total = total + jnp.dot(c[...], w[...], preferred_element_type=jnp.float32)
    o_ref[...] = total.astype(o_ref.dtype)


def project_call(part, contexts, weights, added, dtype):
    tokens, width = contexts[0].shape
    columns = added.shape[1]
    tile = min(tokens, 256)
    c_spec = pl.BlockSpec((tile, width), lambda i, p: (i, 0))
    w_specs = [
        pl.BlockSpec((width, columns), lambda i, p: (0, p[0]))
        if w.shape[1] > columns
        else pl.BlockSpec((width, columns), lambda i, p: (0, 0))
        for w in weights
    ]
    r_spec = pl.BlockSpec((tile, columns), lambda i, p: (i, 0))
    return pl.pallas_call(
        project_kernel,
        grid_spec=pltpu.PrefetchScalarGridSpec(
            num_scalar_prefetch=1,
            grid=(tokens // tile,),
            in_specs=[c_spec] * 2 + w_specs + [r_spec],
            out_specs=r_spec,
        ),
        out_shape=jax.ShapeDtypeStruct(added.shape, dtype),
    )(part, *contexts, *weights, added)


def exchanged(block, first):
    route = []
    for i in range(first, lax.axis_size("seq") - 1, 2):
        route += [(i, i + 1), (i + 1, i)]
    return lax.ppermute(block, "seq", route)


def swapped(block, flip):
    return lax.ppermute(block, HEAD, [(i, i ^ flip) for i in range(4)])


def other_side(block, flip):
    axes = ("seq", *HEAD)
    route = []
    for s in range(lax.axis_size("seq")):
        for h in range(4):
            route.append((s * 4 + h, (s ^ Z_CHIPS) * 4 + (h ^ flip)))
    return lax.ppermute(block, axes, route)


def body(
    encoder_queries,
    encoder_keys,
    encoder_values,
    block_lists,
    block_counts,
    decoder_queries,
    span_owner,
    cross_slots,
    out_weight,
    decoder_input,
):
    position = lax.axis_index("seq").astype(jnp.int32).reshape(1)
    part = lax.axis_index(HEAD).astype(jnp.int32).reshape(1)
    blocks = encoder_queries.shape[0] // BLK
    width = encoder_queries.shape[1]
    columns = decoder_input.shape[1]
    lists = block_lists.T
    slots = cross_slots.T
    beside, beyond = send_call(position, encoder_keys, encoder_values, decoder_queries)
    beside = exchanged(beside, 0)
    beyond = exchanged(beyond, 1)
    across2, across3, across1 = cut_call(part, out_weight, columns)
    w2 = swapped(across2, 2)
    w3 = other_side(across3, 3)
    w1 = swapped(across1, 1)
    k3 = encoder_keys.reshape(blocks, BLK, width)
    v3 = encoder_values.reshape(blocks, BLK, width)
    partial = inner_call(position, block_counts, lists, encoder_queries, k3, v3)
    scalars = (position, block_counts, lists, span_owner, slots)
    shared = (encoder_queries, k3, v3, beside, beyond, decoder_queries)
    e3, (for_beside, for_beyond) = stage_call(
        (-1, 1), True, scalars, *shared, partial.reshape(blocks, BLK, width)
    )
    from_beside = exchanged(for_beside, 0)
    from_beyond = exchanged(for_beyond, 1)
    e3, (own,) = stage_call((0,), False, scalars, *shared, e3)
    context = own + from_beside + from_beyond
    across = swapped(context, 2)
    beside = swapped(context, 1)
    corner = swapped(across, 1)
    total = project_call(part, [context, beside], [out_weight, w1], decoder_input, jnp.float32)
    decoder_out = project_call(part, [across, corner], [w2, w3], total, jnp.bfloat16)
    return (e3.reshape(blocks * BLK, width), decoder_out)


def solution(mesh):
    split = Mesh(mesh.devices.reshape(mesh.shape["seq"], 2, 2), ("seq", "head_0", "head_1"))
    placed = (
        P("seq", HEAD),
        P("seq", HEAD),
        P("seq", HEAD),
        P("seq", None),
        P("seq"),
        P("seq", HEAD),
        P(),
        P(),
        P(HEAD, None),
        P("seq", HEAD),
    )
    return jax.shard_map(
        body,
        mesh=split,
        in_specs=placed,
        out_specs=(P("seq", HEAD), P("seq", HEAD)),
        check_vma=False,
    )
```

```python
import jax
import jax.numpy as jnp
from jax import lax
from jax.experimental import pallas as pl
from jax.experimental.pallas import tpu as pltpu
from jax.sharding import Mesh
from jax.sharding import PartitionSpec as P


HD = 64
BLK = 128
REACH = 2
SLOTS = 4
CROSS = 2
QUAD = 4
Z_CHIPS = 8
QW = HD * QUAD
HEAD = ("head_0", "head_1")
EXP_SCALE = 0.125 * 1.4426950408889634


def attend(q_ref, k_refs, v_refs, o_ref):
    quads = [pl.ds(c * QW, QW) for c in range(q_ref.shape[-1] // QW)]
    lane = lax.broadcasted_iota(jnp.int32, (BLK, QW), 1) // HD
    scores = []
    for cols in quads:
        q = q_ref[:, cols]
        zero = jnp.zeros_like(q)
        rows = jnp.concatenate([jnp.where(lane == h, q, zero) for h in range(QUAD)], axis=0)
        k = jnp.concatenate([r[:, cols] for r in k_refs], axis=0)
        scores.append(
            lax.dot_general(rows, k, (((1,), (1,)), ((), ())), preferred_element_type=jnp.float32)
        )
    for cols, s in zip(quads, scores):
        m = jnp.max(s, axis=1, keepdims=True)
        p = jnp.exp2((s - m) * EXP_SCALE)
        l = jnp.sum(p, axis=1, keepdims=True)
        v = jnp.concatenate([r[:, cols] for r in v_refs], axis=0)
        o = lax.dot_general(
            p.astype(jnp.bfloat16), v, (((1,), (0,)), ((), ())), preferred_element_type=jnp.float32
        )
        o = o * (1.0 / l)
        out = o[:BLK]
        for h in range(1, QUAD):
            out = jnp.where(lane == h, o[h * BLK : (h + 1) * BLK], out)
        o_ref[:, cols] = out.astype(jnp.bfloat16)


def send_kernel(pos, k, v, beside, beyond, s0, s1, s2, s3, load_sem, store_sem):
    halo = REACH * BLK
    tail = pl.ds(k.shape[0] - halo, halo)
    head = pl.ds(0, halo)
    values = pl.ds(halo, halo)
    sources = ((k.at[tail], s0), (v.at[tail], s1), (k.at[head], s2), (v.at[head], s3))
    loads = [pltpu.make_async_copy(x, y, load_sem) for x, y in sources]
    for load in loads:
        load.start()
    for load in loads:
        load.wait()

    def stores(up, down):
        pairs = ((s0, up.at[head]), (s1, up.at[values]), (s2, down.at[head]), (s3, down.at[values]))
        return [pltpu.make_async_copy(a, b, store_sem) for a, b in pairs]

    even = pos[0] % 2 == 0

    @pl.when(even)
    def _():
        for store in stores(beside, beyond):
            store.start()

    @pl.when(jnp.logical_not(even))
    def _():
        for store in stores(beyond, beside):
            store.start()

    for store in stores(beside, beyond):
        store.wait()


def send_call(position, k, v):
    halo = REACH * BLK
    width = k.shape[1]
    shape = jax.ShapeDtypeStruct((2 * halo, width), k.dtype)
    hbm = pl.BlockSpec(memory_space=pl.ANY)
    return pl.pallas_call(
        send_kernel,
        in_specs=[pl.BlockSpec(memory_space=pltpu.SMEM)] + [hbm] * 2,
        out_specs=[hbm] * 2,
        out_shape=[shape] * 2,
        scratch_shapes=[pltpu.VMEM((halo, width), k.dtype)] * 4
        + [pltpu.SemaphoreType.DMA, pltpu.SemaphoreType.DMA],
        name="pack_edges",
    )(position, k, v)


def encoder_kernel(
    pos, counts, lists, q, k, v, beside, beyond, e, kb, vb, qb, eb, edge_sem, k_sem, v_sem, q_sem, e_sem
):
    blocks = k.shape[0]
    even = pos[0] % 2 == 0
    base = pos[0] * blocks - REACH

    def edges(up, down):
        pairs = (
            (up.at[pl.ds(0, REACH)], kb.at[pl.ds(0, REACH)]),
            (up.at[pl.ds(REACH, REACH)], vb.at[pl.ds(0, REACH)]),
            (down.at[pl.ds(0, REACH)], kb.at[pl.ds(REACH + blocks, REACH)]),
            (down.at[pl.ds(REACH, REACH)], vb.at[pl.ds(REACH + blocks, REACH)]),
        )
        return [pltpu.make_async_copy(a, b, edge_sem) for a, b in pairs]

    def keys(i):
        return pltpu.make_async_copy(k.at[i], kb.at[REACH + i], k_sem.at[i])

    def values(i):
        return pltpu.make_async_copy(v.at[i], vb.at[REACH + i], v_sem.at[i])

    def queries(i):
        return pltpu.make_async_copy(q.at[i], qb.at[i], q_sem.at[i])

    def result(i):
        return pltpu.make_async_copy(eb.at[i], e.at[i], e_sem)

    @pl.when(even)
    def _():
        for copy in edges(beyond, beside):
            copy.start()

    @pl.when(jnp.logical_not(even))
    def _():
        for copy in edges(beside, beyond):
            copy.start()

    for i in range(blocks):
        keys(i).start()
        values(i).start()
        queries(i).start()
    for copy in edges(beyond, beside):
        copy.wait()
    for i in range(REACH):
        keys(i).wait()
        values(i).wait()

    @pl.loop(0, blocks)
    def _(b):
        @pl.when(b + REACH < blocks)
        def _():
            keys(b + REACH).wait()
            values(b + REACH).wait()

        queries(b).wait()
        count = counts[b]
        ids = [lists[j, b] - base for j in range(SLOTS)]
        for n in range(1, SLOTS + 1):

            @pl.when(count == n)
            def _(n=n):
                attend(
                    qb.at[b], [kb.at[i] for i in ids[:n]], [vb.at[i] for i in ids[:n]], eb.at[b]
                )

        result(b).start()

    for i in range(blocks):
        result(i).wait()


def encoder_call(position, counts, lists, q, k3, v3, beside, beyond):
    blocks, _, width = k3.shape
    smem = pl.BlockSpec(memory_space=pltpu.SMEM)
    hbm = pl.BlockSpec(memory_space=pl.ANY)
    vmem = pl.BlockSpec(memory_space=pltpu.VMEM)

    def room(n):
        return pltpu.VMEM((n, BLK, width), jnp.bfloat16)

    return pl.pallas_call(
        encoder_kernel,
        in_specs=[smem] * 3 + [hbm] * 3 + [vmem] * 2,
        out_specs=hbm,
        out_shape=jax.ShapeDtypeStruct(k3.shape, jnp.bfloat16),
        scratch_shapes=[
            room(blocks + 2 * REACH),
            room(blocks + 2 * REACH),
            room(blocks),
            room(blocks),
            pltpu.SemaphoreType.DMA,
            pltpu.SemaphoreType.DMA((blocks,)),
            pltpu.SemaphoreType.DMA((blocks,)),
            pltpu.SemaphoreType.DMA((blocks,)),
            pltpu.SemaphoreType.DMA,
        ],
        name="encoder",
    )(position, counts, lists, cut(q), k3, v3, in_vmem(cut(beside)), in_vmem(cut(beyond)))


def serve_kernel(pos, owners, slots, k, e, *refs):
    sources = (len(refs) - 6) // 2
    queries = refs[:sources]
    answers = refs[sources : 2 * sources]
    kb, eb, qb, ob, load_sems, answer_sem = refs[2 * sources :]
    mine = pos[0]
    per = queries[0].shape[0]
    total = owners.shape[0] // per
    ahead = jnp.where(mine % 2 == 0, 1, -1)
    shifts = (0,) if sources == 1 else (ahead, -ahead)

    def candidate(i, t):
        source = mine + shifts[i]
        d = jnp.clip(source, 0, total - 1) * per + t
        live = (source >= 0) & (source < total) & (owners[d] == mine)
        return live, slots[0, d], slots[1, d]

    def loads(i, t, s0, s1):
        n = i * per + t
        sem = load_sems.at[n]
        return [
            pltpu.make_async_copy(a, b, sem)
            for a, b in (
                (queries[i].at[t], qb.at[n]),
                (k.at[s0], kb.at[n, 0]),
                (k.at[s1], kb.at[n, 1]),
                (e.at[s0], eb.at[n, 0]),
                (e.at[s1], eb.at[n, 1]),
            )
        ]

    for i in range(sources):
        for t in range(per):
            live, s0, s1 = candidate(i, t)

            @pl.when(live)
            def _(i=i, t=t, s0=s0, s1=s1):
                for copy in loads(i, t, s0, s1):
                    copy.start()

    for i in range(sources):

        @pl.loop(0, per)
        def _(t, i=i):
            live, s0, s1 = candidate(i, t)
            n = i * per + t

            @pl.when(live)
            def _():
                for copy in loads(i, t, s0, s1):
                    copy.wait()
                attend(
                    qb.at[n],
                    [kb.at[n, j] for j in range(CROSS)],
                    [eb.at[n, j] for j in range(CROSS)],
                    ob.at[n],
                )

            @pl.when(jnp.logical_not(live))
            def _():
                ob[n] = jnp.zeros(ob.shape[1:], ob.dtype)

        pltpu.make_async_copy(ob.at[pl.ds(i * per, per)], answers[i], answer_sem).start()

    for i in range(sources):
        pltpu.make_async_copy(ob.at[pl.ds(i * per, per)], answers[i], answer_sem).wait()


def serve_call(position, owners, slots, k3, e3, queries):
    width = k3.shape[-1]
    sources = len(queries)
    queries = [cut(x) for x in queries]
    per = queries[0].shape[0]
    smem = pl.BlockSpec(memory_space=pltpu.SMEM)
    hbm = pl.BlockSpec(memory_space=pl.ANY)
    vmem = pl.BlockSpec(memory_space=pltpu.VMEM)
    served = per * sources
    if sources > 1:
        queries = [in_vmem(x) for x in queries]
    out = pl.pallas_call(
        serve_kernel,
        in_specs=[smem] * 3 + [hbm] * 2 + [vmem if sources > 1 else hbm] * sources,
        out_specs=[hbm] * sources,
        out_shape=[jax.ShapeDtypeStruct((per, BLK, width), jnp.bfloat16)] * sources,
        scratch_shapes=[
            pltpu.VMEM((served, CROSS, BLK, width), jnp.bfloat16),
            pltpu.VMEM((served, CROSS, BLK, width), jnp.bfloat16),
            pltpu.VMEM((served, BLK, width), jnp.bfloat16),
            pltpu.VMEM((served, BLK, width), jnp.bfloat16),
            pltpu.SemaphoreType.DMA((served,)),
            pltpu.SemaphoreType.DMA,
        ],
    )(position, owners, slots, k3, e3, *queries)
    return [x.reshape(per * BLK, width) for x in out]


def cut(x):
    return x.reshape(-1, BLK, x.shape[-1])


def in_vmem(x):
    return pltpu.with_memory_space_constraint(x, pltpu.VMEM)


def move(plan, stages, load_sem, store_sem):
    loads = [pltpu.make_async_copy(src, stages[i], load_sem.at[i]) for i, (src, _) in enumerate(plan)]
    stores = [pltpu.make_async_copy(stages[i], dst, store_sem) for i, (_, dst) in enumerate(plan)]
    for load in loads:
        load.start()
    for load, store in zip(loads, stores):
        load.wait()
        store.start()
    for store in stores:
        store.wait()


def cut_kernel(part, w, a, b, c, sa, sb, sc, load_sem, store_sem):
    columns = a.shape[1]
    plan = []
    for flip, dst in ((2, a), (3, b), (1, c)):
        start = pl.multiple_of((part[0] ^ flip) * columns, columns)
        plan.append((w.at[:, pl.ds(start, columns)], dst))
    move(plan, (sa, sb, sc), load_sem, store_sem)


def cut_call(part, w, columns):
    shape = jax.ShapeDtypeStruct((w.shape[0], columns), w.dtype)
    hbm = pl.BlockSpec(memory_space=pl.ANY)
    return pl.pallas_call(
        cut_kernel,
        in_specs=[pl.BlockSpec(memory_space=pltpu.SMEM), hbm],
        out_specs=[hbm] * 3,
        out_shape=[shape] * 3,
        scratch_shapes=[pltpu.VMEM(shape.shape, w.dtype)] * 3
        + [pltpu.SemaphoreType.DMA((3,)), pltpu.SemaphoreType.DMA],
        name="cut_weight",
    )(part, w)


def project_kernel(part, c0, c1, w0, w1, r_ref, o_ref):
    total = r_ref[...].astype(jnp.float32)
    for c, w in ((c0, w0), (c1, w1)):
        total = total + jnp.dot(c[...], w[...], preferred_element_type=jnp.float32)
    o_ref[...] = total.astype(o_ref.dtype)


def project_call(part, contexts, weights, added, dtype):
    tokens, width = contexts[0].shape
    columns = added.shape[1]
    tile = min(tokens, 256)
    c_spec = pl.BlockSpec((tile, width), lambda i, p: (i, 0))
    w_specs = [
        pl.BlockSpec((width, columns), lambda i, p: (0, p[0]))
        if w.shape[1] > columns
        else pl.BlockSpec((width, columns), lambda i, p: (0, 0))
        for w in weights
    ]
    r_spec = pl.BlockSpec((tile, columns), lambda i, p: (i, 0))
    return pl.pallas_call(
        project_kernel,
        grid_spec=pltpu.PrefetchScalarGridSpec(
            num_scalar_prefetch=1,
            grid=(tokens // tile,),
            in_specs=[c_spec] * 2 + w_specs + [r_spec],
            out_specs=r_spec,
        ),
        out_shape=jax.ShapeDtypeStruct(added.shape, dtype),
    )(part, *[in_vmem(c) for c in contexts], *weights, added)


def exchanged(block, first):
    route = []
    for i in range(first, lax.axis_size("seq") - 1, 2):
        route += [(i, i + 1), (i + 1, i)]
    return lax.ppermute(block, "seq", route)


def swapped(block, flip):
    return lax.ppermute(block, HEAD, [(i, i ^ flip) for i in range(4)])


def other_side(block, flip):
    axes = ("seq", *HEAD)
    route = []
    for s in range(lax.axis_size("seq")):
        for h in range(4):
            route.append((s * 4 + h, (s ^ Z_CHIPS) * 4 + (h ^ flip)))
    return lax.ppermute(block, axes, route)


def body(
    encoder_queries,
    encoder_keys,
    encoder_values,
    block_lists,
    block_counts,
    decoder_queries,
    span_owner,
    cross_slots,
    out_weight,
    decoder_input,
):
    position = lax.axis_index("seq").astype(jnp.int32).reshape(1)
    part = lax.axis_index(HEAD).astype(jnp.int32).reshape(1)
    blocks = encoder_queries.shape[0] // BLK
    width = encoder_queries.shape[1]
    columns = decoder_input.shape[1]
    lists = block_lists.T
    slots = cross_slots.T
    k3 = cut(encoder_keys)
    v3 = cut(encoder_values)
    beside, beyond = send_call(position, encoder_keys, encoder_values)
    beside = exchanged(beside, 0)
    beyond = exchanged(beyond, 1)
    q_beside = exchanged(decoder_queries, 0)
    q_beyond = exchanged(decoder_queries, 1)
    across2, across3, across1 = cut_call(part, out_weight, columns)
    w2 = swapped(across2, 2)
    w3 = other_side(across3, 3)
    w1 = swapped(across1, 1)
    e3 = encoder_call(position, block_counts, lists, encoder_queries, k3, v3, beside, beyond)
    tables = (position, span_owner, slots, k3, e3)
    (own,) = serve_call(*tables, [decoder_queries])
    for_beside, for_beyond = serve_call(*tables, [q_beside, q_beyond])
    from_beside = exchanged(for_beside, 0)
    from_beyond = exchanged(for_beyond, 1)
    context = own + from_beside + from_beyond
    across = swapped(context, 2)
    beside = swapped(context, 1)
    corner = swapped(across, 1)
    total = project_call(part, [context, beside], [out_weight, w1], decoder_input, jnp.float32)
    decoder_out = project_call(part, [across, corner], [w2, w3], total, jnp.bfloat16)
    return (e3.reshape(blocks * BLK, width), decoder_out)


def solution(mesh):
    split = Mesh(mesh.devices.reshape(mesh.shape["seq"], 2, 2), ("seq", "head_0", "head_1"))
    placed = (
        P("seq", HEAD),
        P("seq", HEAD),
        P("seq", HEAD),
        P("seq", None),
        P("seq"),
        P("seq", HEAD),
        P(),
        P(),
        P(HEAD, None),
        P("seq", HEAD),
    )
    return jax.shard_map(
        body,
        mesh=split,
        in_specs=placed,
        out_specs=(P("seq", HEAD), P("seq", HEAD)),
        check_vma=False,
    )
```

```python
import jax
import jax.numpy as jnp
from jax import lax
from jax.experimental import pallas as pl
from jax.experimental.pallas import tpu as pltpu
from jax.sharding import Mesh
from jax.sharding import PartitionSpec as P


HD = 64
BLK = 128
REACH = 2
SLOTS = 4
CROSS = 2
QUAD = 4
PARTS = 2
Z_CHIPS = 8
QW = HD * QUAD
HEAD = ("head_0", "head_1")
EXP_SCALE = 0.125 * 1.4426950408889634


def attend(q_ref, k_refs, v_refs, o_ref):
    quads = [pl.ds(c * QW, QW) for c in range(q_ref.shape[-1] // QW)]
    lane = lax.broadcasted_iota(jnp.int32, (BLK, QW), 1) // HD
    scores = []
    for cols in quads:
        q = q_ref[:, cols]
        zero = jnp.zeros_like(q)
        rows = jnp.concatenate([jnp.where(lane == h, q, zero) for h in range(QUAD)], axis=0)
        k = jnp.concatenate([r[:, cols] for r in k_refs], axis=0)
        scores.append(
            lax.dot_general(rows, k, (((1,), (1,)), ((), ())), preferred_element_type=jnp.float32)
        )
    for cols, s in zip(quads, scores):
        m = jnp.max(s, axis=1, keepdims=True)
        p = jnp.exp2((s - m) * EXP_SCALE)
        l = jnp.sum(p, axis=1, keepdims=True)
        v = jnp.concatenate([r[:, cols] for r in v_refs], axis=0)
        o = lax.dot_general(
            p.astype(jnp.bfloat16), v, (((1,), (0,)), ((), ())), preferred_element_type=jnp.float32
        )
        o = o * (1.0 / l)
        out = o[:BLK]
        for h in range(1, QUAD):
            out = jnp.where(lane == h, o[h * BLK : (h + 1) * BLK], out)
        o_ref[:, cols] = out.astype(jnp.bfloat16)


def send_kernel(pos, k, v, beside, beyond, s0, s1, s2, s3, load_sem, store_sem):
    halo = REACH * BLK
    tail = pl.ds(k.shape[0] - halo, halo)
    head = pl.ds(0, halo)
    values = pl.ds(halo, halo)
    sources = ((k.at[tail], s0), (v.at[tail], s1), (k.at[head], s2), (v.at[head], s3))
    loads = [pltpu.make_async_copy(x, y, load_sem) for x, y in sources]
    for load in loads:
        load.start()
    for load in loads:
        load.wait()

    def stores(up, down):
        pairs = ((s0, up.at[head]), (s1, up.at[values]), (s2, down.at[head]), (s3, down.at[values]))
        return [pltpu.make_async_copy(a, b, store_sem) for a, b in pairs]

    even = pos[0] % 2 == 0

    @pl.when(even)
    def _():
        for store in stores(beside, beyond):
            store.start()

    @pl.when(jnp.logical_not(even))
    def _():
        for store in stores(beyond, beside):
            store.start()

    for store in stores(beside, beyond):
        store.wait()


def send_call(position, k, v):
    halo = REACH * BLK
    width = k.shape[1]
    shape = jax.ShapeDtypeStruct((2 * halo, width), k.dtype)
    hbm = pl.BlockSpec(memory_space=pl.ANY)
    return pl.pallas_call(
        send_kernel,
        in_specs=[pl.BlockSpec(memory_space=pltpu.SMEM)] + [hbm] * 2,
        out_specs=[hbm] * 2,
        out_shape=[shape] * 2,
        scratch_shapes=[pltpu.VMEM((halo, width), k.dtype)] * 4
        + [pltpu.SemaphoreType.DMA, pltpu.SemaphoreType.DMA],
        name="pack_edges",
    )(position, k, v)


def encode_block(b, base, counts, lists, q_ref, kb, vb, o_ref):
    count = counts[b]
    ids = [lists[j, b] - base for j in range(SLOTS)]
    for n in range(1, SLOTS + 1):

        @pl.when(count == n)
        def _(n=n):
            attend(q_ref, [kb.at[i] for i in ids[:n]], [vb.at[i] for i in ids[:n]], o_ref)


def inner_kernel(pos, counts, lists, q, k, v, e, kb, vb, qb, eb, k_sem, v_sem, q_sem, e_sem):
    blocks = k.shape[0]
    base = pos[0] * blocks

    def keys(i):
        return pltpu.make_async_copy(k.at[i], kb.at[i], k_sem.at[i])

    def values(i):
        return pltpu.make_async_copy(v.at[i], vb.at[i], v_sem.at[i])

    def queries(i):
        return pltpu.make_async_copy(q.at[i], qb.at[i], q_sem.at[i])

    def result(i):
        return pltpu.make_async_copy(eb.at[i], e.at[i], e_sem)

    for i in range(blocks):
        keys(i).start()
        values(i).start()
        if REACH <= i < blocks - REACH:
            queries(i).start()
    for i in range(2 * REACH):
        keys(i).wait()
        values(i).wait()

    @pl.loop(REACH, blocks - REACH)
    def _(b):
        keys(b + REACH).wait()
        values(b + REACH).wait()
        queries(b).wait()
        encode_block(b, base, counts, lists, qb.at[b], kb, vb, eb.at[b])
        result(b).start()

    for i in range(REACH, blocks - REACH):
        result(i).wait()


def edge_kernel(
    pos, counts, lists, q, k, v, beside, beyond, _, e, kb, vb, qb, eb, far_sem, in_sem, e_sem
):
    blocks = k.shape[0]
    near = 2 * REACH
    even = pos[0] % 2 == 0
    base = pos[0] * blocks - REACH

    def edges(up, down):
        pairs = (
            (up.at[pl.ds(0, REACH)], kb.at[pl.ds(0, REACH)]),
            (up.at[pl.ds(REACH, REACH)], vb.at[pl.ds(0, REACH)]),
            (down.at[pl.ds(0, REACH)], kb.at[pl.ds(REACH + blocks, REACH)]),
            (down.at[pl.ds(REACH, REACH)], vb.at[pl.ds(REACH + blocks, REACH)]),
        )
        return [pltpu.make_async_copy(a, b, far_sem) for a, b in pairs]

    local = []
    for start in (0, blocks - near):
        here = pl.ds(start, near)
        there = pl.ds(REACH + start, near)
        local.append(pltpu.make_async_copy(k.at[here], kb.at[there], in_sem))
        local.append(pltpu.make_async_copy(v.at[here], vb.at[there], in_sem))
    for i, start in enumerate((0, blocks - REACH)):
        local.append(
            pltpu.make_async_copy(q.at[pl.ds(start, REACH)], qb.at[pl.ds(i * REACH, REACH)], in_sem)
        )
    for copy in local:
        copy.start()

    @pl.when(even)
    def _():
        for copy in edges(beyond, beside):
            copy.start()

    @pl.when(jnp.logical_not(even))
    def _():
        for copy in edges(beside, beyond):
            copy.start()

    for copy in local + edges(beyond, beside):
        copy.wait()

    @pl.loop(0, near)
    def _(t):
        b = jnp.where(t < REACH, t, blocks - near + t)
        encode_block(b, base, counts, lists, qb.at[t], kb, vb, eb.at[t])
        pltpu.make_async_copy(eb.at[t], e.at[b], e_sem).start()

    for t in range(near):
        pltpu.make_async_copy(eb.at[t], e.at[t], e_sem).wait()


def encoder_call(position, counts, lists, q, k3, v3, edges=None):
    blocks, _, width = k3.shape
    smem = pl.BlockSpec(memory_space=pltpu.SMEM)
    hbm = pl.BlockSpec(memory_space=pl.ANY)
    dma = pltpu.SemaphoreType.DMA

    def room(n):
        return pltpu.VMEM((n, BLK, width), jnp.bfloat16)

    shape = jax.ShapeDtypeStruct(k3.shape, jnp.bfloat16)
    args = (position, counts, lists, cut(q), k3, v3)
    if edges is None:
        return pl.pallas_call(
            inner_kernel,
            in_specs=[smem] * 3 + [hbm] * 3,
            out_specs=hbm,
            out_shape=shape,
            scratch_shapes=[room(blocks)] * 4 + [dma((blocks,))] * 3 + [dma],
            name="encoder_inner",
        )(*args)
    beside, beyond, partial = edges
    return pl.pallas_call(
        edge_kernel,
        in_specs=[smem] * 3 + [hbm] * 3 + [pl.BlockSpec(memory_space=pltpu.VMEM)] * 2 + [hbm],
        out_specs=hbm,
        out_shape=shape,
        scratch_shapes=[room(blocks + 2 * REACH)] * 2 + [room(2 * REACH)] * 2 + [dma] * 3,
        input_output_aliases={8: 0},
        name="encoder_edge",
    )(*args, in_vmem(cut(beside)), in_vmem(cut(beyond)), partial)


def serve_kernel(pos, owners, slots, k, e, *refs):
    sources = (len(refs) - 6) // (1 + PARTS)
    queries = refs[:sources]
    answers = refs[sources : (1 + PARTS) * sources]
    kb, eb, qb, ob, load_sems, answer_sem = refs[(1 + PARTS) * sources :]
    mine = pos[0]
    per = queries[0].shape[0]
    total = owners.shape[0] // per
    ahead = jnp.where(mine % 2 == 0, 1, -1)
    shifts = (0,) if sources == 1 else (ahead, -ahead)

    def candidate(i, t):
        source = mine + shifts[i]
        d = jnp.clip(source, 0, total - 1) * per + t
        live = (source >= 0) & (source < total) & (owners[d] == mine)
        return live, slots[0, d], slots[1, d]

    def loads(i, t, s0, s1):
        n = i * per + t
        sem = load_sems.at[n]
        return [
            pltpu.make_async_copy(a, b, sem)
            for a, b in (
                (queries[i].at[t], qb.at[n]),
                (k.at[s0], kb.at[n, 0]),
                (k.at[s1], kb.at[n, 1]),
                (e.at[s0], eb.at[n, 0]),
                (e.at[s1], eb.at[n, 1]),
            )
        ]

    for i in range(sources):
        for t in range(per):
            live, s0, s1 = candidate(i, t)

            @pl.when(live)
            def _(i=i, t=t, s0=s0, s1=s1):
                for copy in loads(i, t, s0, s1):
                    copy.start()

    share = per // PARTS

    def answer(part, i):
        rows = ob.at[pl.ds(i * per + part * share, share)]
        return pltpu.make_async_copy(rows, answers[part * sources + i], answer_sem)

    for part in range(PARTS):
        for i in range(sources):

            @pl.loop(part * share, (part + 1) * share)
            def _(t, i=i):
                live, s0, s1 = candidate(i, t)
                n = i * per + t

                @pl.when(live)
                def _():
                    for copy in loads(i, t, s0, s1):
                        copy.wait()
                    attend(
                        qb.at[n],
                        [kb.at[n, j] for j in range(CROSS)],
                        [eb.at[n, j] for j in range(CROSS)],
                        ob.at[n],
                    )

                @pl.when(jnp.logical_not(live))
                def _():
                    ob[n] = jnp.zeros(ob.shape[1:], ob.dtype)

            answer(part, i).start()

    for part in range(PARTS):
        for i in range(sources):
            answer(part, i).wait()


def serve_call(position, owners, slots, k3, e3, queries):
    width = k3.shape[-1]
    sources = len(queries)
    queries = [cut(x) for x in queries]
    per = queries[0].shape[0]
    smem = pl.BlockSpec(memory_space=pltpu.SMEM)
    hbm = pl.BlockSpec(memory_space=pl.ANY)
    vmem = pl.BlockSpec(memory_space=pltpu.VMEM)
    served = per * sources
    if sources > 1:
        queries = [in_vmem(x) for x in queries]
    out = pl.pallas_call(
        serve_kernel,
        in_specs=[smem] * 3 + [hbm] * 2 + [vmem if sources > 1 else hbm] * sources,
        out_specs=[hbm] * (sources * PARTS),
        out_shape=[jax.ShapeDtypeStruct((per // PARTS, BLK, width), jnp.bfloat16)]
        * (sources * PARTS),
        scratch_shapes=[
            pltpu.VMEM((served, CROSS, BLK, width), jnp.bfloat16),
            pltpu.VMEM((served, CROSS, BLK, width), jnp.bfloat16),
            pltpu.VMEM((served, BLK, width), jnp.bfloat16),
            pltpu.VMEM((served, BLK, width), jnp.bfloat16),
            pltpu.SemaphoreType.DMA((served,)),
            pltpu.SemaphoreType.DMA,
        ],
    )(position, owners, slots, k3, e3, *queries)
    return [x.reshape(-1, width) for x in out]


def cut(x):
    return x.reshape(-1, BLK, x.shape[-1])


def in_vmem(x):
    return pltpu.with_memory_space_constraint(x, pltpu.VMEM)


def move(plan, stages, load_sem, store_sem):
    loads = [pltpu.make_async_copy(src, stages[i], load_sem.at[i]) for i, (src, _) in enumerate(plan)]
    stores = [pltpu.make_async_copy(stages[i], dst, store_sem) for i, (_, dst) in enumerate(plan)]
    for load in loads:
        load.start()
    for load, store in zip(loads, stores):
        load.wait()
        store.start()
    for store in stores:
        store.wait()


def cut_kernel(part, w, a, b, c, sa, sb, sc, load_sem, store_sem):
    columns = a.shape[1]
    plan = []
    for flip, dst in ((2, a), (3, b), (1, c)):
        start = pl.multiple_of((part[0] ^ flip) * columns, columns)
        plan.append((w.at[:, pl.ds(start, columns)], dst))
    move(plan, (sa, sb, sc), load_sem, store_sem)


def cut_call(part, w, columns):
    shape = jax.ShapeDtypeStruct((w.shape[0], columns), w.dtype)
    hbm = pl.BlockSpec(memory_space=pl.ANY)
    return pl.pallas_call(
        cut_kernel,
        in_specs=[pl.BlockSpec(memory_space=pltpu.SMEM), hbm],
        out_specs=[hbm] * 3,
        out_shape=[shape] * 3,
        scratch_shapes=[pltpu.VMEM(shape.shape, w.dtype)] * 3
        + [pltpu.SemaphoreType.DMA((3,)), pltpu.SemaphoreType.DMA],
        name="cut_weight",
    )(part, w)


def project_kernel(part, c0, c1, w0, w1, r_ref, *refs):
    total = r_ref[...].astype(jnp.float32)
    for c, w in ((c0, w0), (c1, w1)):
        total = total + jnp.dot(c[...], w[...], preferred_element_type=jnp.float32)
    refs[-1][...] = total.astype(refs[-1].dtype)


def project_call(part, contexts, weights, added, dtype, index, out_tokens, earlier=None):
    tokens, width = contexts[0].shape
    columns = added.shape[1]
    here = index if added.shape[0] > tokens else 0
    there = index if out_tokens > tokens else 0
    c_spec = pl.BlockSpec((tokens, width), lambda i, p: (0, 0))
    w_specs = [
        pl.BlockSpec((width, columns), lambda i, p: (0, p[0]))
        if w.shape[1] > columns
        else pl.BlockSpec((width, columns), lambda i, p: (0, 0))
        for w in weights
    ]
    more = [] if earlier is None else [earlier]
    return pl.pallas_call(
        project_kernel,
        grid_spec=pltpu.PrefetchScalarGridSpec(
            num_scalar_prefetch=1,
            grid=(1,),
            in_specs=[c_spec] * 2
            + w_specs
            + [pl.BlockSpec((tokens, columns), lambda i, p: (here, 0))]
            + [pl.BlockSpec(memory_space=pl.ANY)] * len(more),
            out_specs=pl.BlockSpec((tokens, columns), lambda i, p: (there, 0)),
        ),
        out_shape=jax.ShapeDtypeStruct((out_tokens, columns), dtype),
        input_output_aliases={6: 0} if more else {},
    )(part, *[in_vmem(c) for c in contexts], *weights, added, *more)


def exchanged(block, first):
    route = []
    for i in range(first, lax.axis_size("seq") - 1, 2):
        route += [(i, i + 1), (i + 1, i)]
    return lax.ppermute(block, "seq", route)


def swapped(block, flip):
    return lax.ppermute(block, HEAD, [(i, i ^ flip) for i in range(4)])


def other_side(block, flip):
    axes = ("seq", *HEAD)
    route = []
    for s in range(lax.axis_size("seq")):
        for h in range(4):
            route.append((s * 4 + h, (s ^ Z_CHIPS) * 4 + (h ^ flip)))
    return lax.ppermute(block, axes, route)


def body(
    encoder_queries,
    encoder_keys,
    encoder_values,
    block_lists,
    block_counts,
    decoder_queries,
    span_owner,
    cross_slots,
    out_weight,
    decoder_input,
):
    position = lax.axis_index("seq").astype(jnp.int32).reshape(1)
    part = lax.axis_index(HEAD).astype(jnp.int32).reshape(1)
    blocks = encoder_queries.shape[0] // BLK
    width = encoder_queries.shape[1]
    columns = decoder_input.shape[1]
    lists = block_lists.T
    slots = cross_slots.T
    k3 = cut(encoder_keys)
    v3 = cut(encoder_values)
    beside, beyond = send_call(position, encoder_keys, encoder_values)
    beside = exchanged(beside, 0)
    beyond = exchanged(beyond, 1)
    q_beside = exchanged(decoder_queries, 0)
    q_beyond = exchanged(decoder_queries, 1)
    across2, across3, across1 = cut_call(part, out_weight, columns)
    w2 = swapped(across2, 2)
    w3 = other_side(across3, 3)
    w1 = swapped(across1, 1)
    encoder_args = (position, block_counts, lists, encoder_queries, k3, v3)
    partial = encoder_call(*encoder_args)
    e3 = encoder_call(*encoder_args, edges=(beside, beyond, partial))
    tables = (position, span_owner, slots, k3, e3)
    answers = serve_call(*tables, [q_beside, q_beyond])
    returned = []
    for i in range(PARTS):
        from_beside = exchanged(answers[2 * i], 0)
        from_beyond = exchanged(answers[2 * i + 1], 1)
        returned.append((from_beside, from_beyond))
    own = serve_call(*tables, [decoder_queries])
    tokens = decoder_input.shape[0]
    decoder_out = None
    for i in range(PARTS):
        context = own[i] + returned[i][0] + returned[i][1]
        across = swapped(context, 2)
        aside = swapped(context, 1)
        corner = swapped(across, 1)
        total = project_call(
            part, [context, aside], [out_weight, w1], decoder_input, jnp.float32, i, tokens // PARTS
        )
        decoder_out = project_call(
            part, [across, corner], [w2, w3], total, jnp.bfloat16, i, tokens, decoder_out
        )
    return (e3.reshape(blocks * BLK, width), decoder_out)


def solution(mesh):
    split = Mesh(mesh.devices.reshape(mesh.shape["seq"], 2, 2), ("seq", "head_0", "head_1"))
    placed = (
        P("seq", HEAD),
        P("seq", HEAD),
        P("seq", HEAD),
        P("seq", None),
        P("seq"),
        P("seq", HEAD),
        P(),
        P(),
        P(HEAD, None),
        P("seq", HEAD),
    )
    return jax.shard_map(
        body,
        mesh=split,
        in_specs=placed,
        out_specs=(P("seq", HEAD), P("seq", HEAD)),
        check_vma=False,
    )
```

```python
import jax
import jax.numpy as jnp
from jax import lax
from jax.experimental import pallas as pl
from jax.experimental.pallas import tpu as pltpu
from jax.sharding import Mesh
from jax.sharding import PartitionSpec as P


HD = 64
BLK = 128
REACH = 2
SLOTS = 4
CROSS = 2
QUAD = 4
PARTS = 2
Z_CHIPS = 8
QW = HD * QUAD
HEAD = ("head_0", "head_1")
EXP_SCALE = 0.125 * 1.4426950408889634


def attend(q_ref, k_refs, v_refs, o_ref):
    quads = [pl.ds(c * QW, QW) for c in range(q_ref.shape[-1] // QW)]
    lane = lax.broadcasted_iota(jnp.int32, (BLK, QW), 1) // HD
    scores = []
    for cols in quads:
        q = q_ref[:, cols]
        zero = jnp.zeros_like(q)
        rows = jnp.concatenate([jnp.where(lane == h, q, zero) for h in range(QUAD)], axis=0)
        k = jnp.concatenate([r[:, cols] for r in k_refs], axis=0)
        scores.append(
            lax.dot_general(rows, k, (((1,), (1,)), ((), ())), preferred_element_type=jnp.float32)
        )
    for cols, s in zip(quads, scores):
        m = jnp.max(s, axis=1, keepdims=True)
        p = jnp.exp2((s - m) * EXP_SCALE)
        l = jnp.sum(p, axis=1, keepdims=True)
        v = jnp.concatenate([r[:, cols] for r in v_refs], axis=0)
        o = lax.dot_general(
            p.astype(jnp.bfloat16), v, (((1,), (0,)), ((), ())), preferred_element_type=jnp.float32
        )
        o = o * (1.0 / l)
        out = o[:BLK]
        for h in range(1, QUAD):
            out = jnp.where(lane == h, o[h * BLK : (h + 1) * BLK], out)
        o_ref[:, cols] = out.astype(jnp.bfloat16)


def send_kernel(pos, k, v, beside, beyond, s0, s1, s2, s3, load_sem, store_sem):
    halo = REACH * BLK
    tail = pl.ds(k.shape[0] - halo, halo)
    head = pl.ds(0, halo)
    values = pl.ds(halo, halo)
    sources = ((k.at[tail], s0), (v.at[tail], s1), (k.at[head], s2), (v.at[head], s3))
    loads = [pltpu.make_async_copy(x, y, load_sem) for x, y in sources]
    for load in loads:
        load.start()
    for load in loads:
        load.wait()

    def stores(up, down):
        pairs = ((s0, up.at[head]), (s1, up.at[values]), (s2, down.at[head]), (s3, down.at[values]))
        return [pltpu.make_async_copy(a, b, store_sem) for a, b in pairs]

    even = pos[0] % 2 == 0

    @pl.when(even)
    def _():
        for store in stores(beside, beyond):
            store.start()

    @pl.when(jnp.logical_not(even))
    def _():
        for store in stores(beyond, beside):
            store.start()

    for store in stores(beside, beyond):
        store.wait()


def send_call(position, k, v):
    halo = REACH * BLK
    width = k.shape[1]
    shape = jax.ShapeDtypeStruct((2 * halo, width), k.dtype)
    hbm = pl.BlockSpec(memory_space=pl.ANY)
    return pl.pallas_call(
        send_kernel,
        in_specs=[pl.BlockSpec(memory_space=pltpu.SMEM)] + [hbm] * 2,
        out_specs=[hbm] * 2,
        out_shape=[shape] * 2,
        scratch_shapes=[pltpu.VMEM((halo, width), k.dtype)] * 4
        + [pltpu.SemaphoreType.DMA, pltpu.SemaphoreType.DMA],
        name="pack_edges",
    )(position, k, v)


def encode_block(b, base, counts, lists, q_ref, kb, vb, o_ref):
    count = counts[b]
    ids = [lists[j, b] - base for j in range(SLOTS)]
    for n in range(1, SLOTS + 1):

        @pl.when(count == n)
        def _(n=n):
            attend(q_ref, [kb.at[i] for i in ids[:n]], [vb.at[i] for i in ids[:n]], o_ref)


def inner_kernel(pos, counts, lists, q, k, v, e, kb, vb, qb, eb, k_sem, v_sem, q_sem, e_sem):
    blocks = k.shape[0]
    base = pos[0] * blocks

    def keys(i):
        return pltpu.make_async_copy(k.at[i], kb.at[i], k_sem.at[i])

    def values(i):
        return pltpu.make_async_copy(v.at[i], vb.at[i], v_sem.at[i])

    def queries(i):
        return pltpu.make_async_copy(q.at[i], qb.at[i], q_sem.at[i])

    def result(i):
        return pltpu.make_async_copy(eb.at[i], e.at[i], e_sem)

    for i in range(blocks):
        keys(i).start()
        values(i).start()
        if REACH <= i < blocks - REACH:
            queries(i).start()
    for i in range(2 * REACH):
        keys(i).wait()
        values(i).wait()

    @pl.loop(REACH, blocks - REACH)
    def _(b):
        keys(b + REACH).wait()
        values(b + REACH).wait()
        queries(b).wait()
        encode_block(b, base, counts, lists, qb.at[b], kb, vb, eb.at[b])
        result(b).start()

    for i in range(REACH, blocks - REACH):
        result(i).wait()


def edge_kernel(
    pos, counts, lists, q, k, v, beside, beyond, _, e, kb, vb, qb, eb, far_sem, in_sem, e_sem
):
    blocks = k.shape[0]
    near = 2 * REACH
    even = pos[0] % 2 == 0
    base = pos[0] * blocks - REACH

    def edges(up, down):
        pairs = (
            (up.at[pl.ds(0, REACH)], kb.at[pl.ds(0, REACH)]),
            (up.at[pl.ds(REACH, REACH)], vb.at[pl.ds(0, REACH)]),
            (down.at[pl.ds(0, REACH)], kb.at[pl.ds(REACH + blocks, REACH)]),
            (down.at[pl.ds(REACH, REACH)], vb.at[pl.ds(REACH + blocks, REACH)]),
        )
        return [pltpu.make_async_copy(a, b, far_sem) for a, b in pairs]

    local = []
    for start in (0, blocks - near):
        here = pl.ds(start, near)
        there = pl.ds(REACH + start, near)
        local.append(pltpu.make_async_copy(k.at[here], kb.at[there], in_sem))
        local.append(pltpu.make_async_copy(v.at[here], vb.at[there], in_sem))
    for i, start in enumerate((0, blocks - REACH)):
        local.append(
            pltpu.make_async_copy(q.at[pl.ds(start, REACH)], qb.at[pl.ds(i * REACH, REACH)], in_sem)
        )
    for copy in local:
        copy.start()

    @pl.when(even)
    def _():
        for copy in edges(beyond, beside):
            copy.start()

    @pl.when(jnp.logical_not(even))
    def _():
        for copy in edges(beside, beyond):
            copy.start()

    for copy in local + edges(beyond, beside):
        copy.wait()

    @pl.loop(0, near)
    def _(t):
        b = jnp.where(t < REACH, t, blocks - near + t)
        encode_block(b, base, counts, lists, qb.at[t], kb, vb, eb.at[t])
        pltpu.make_async_copy(eb.at[t], e.at[b], e_sem).start()

    for t in range(near):
        pltpu.make_async_copy(eb.at[t], e.at[t], e_sem).wait()


def encoder_call(position, counts, lists, q, k3, v3, edges=None):
    blocks, _, width = k3.shape
    smem = pl.BlockSpec(memory_space=pltpu.SMEM)
    hbm = pl.BlockSpec(memory_space=pl.ANY)
    dma = pltpu.SemaphoreType.DMA

    def room(n):
        return pltpu.VMEM((n, BLK, width), jnp.bfloat16)

    shape = jax.ShapeDtypeStruct(k3.shape, jnp.bfloat16)
    args = (position, counts, lists, cut(q), k3, v3)
    if edges is None:
        return pl.pallas_call(
            inner_kernel,
            in_specs=[smem] * 3 + [hbm] * 3,
            out_specs=hbm,
            out_shape=shape,
            scratch_shapes=[room(blocks)] * 4 + [dma((blocks,))] * 3 + [dma],
            name="encoder_inner",
        )(*args)
    beside, beyond, partial = edges
    return pl.pallas_call(
        edge_kernel,
        in_specs=[smem] * 3 + [hbm] * 3 + [pl.BlockSpec(memory_space=pltpu.VMEM)] * 2 + [hbm],
        out_specs=hbm,
        out_shape=shape,
        scratch_shapes=[room(blocks + 2 * REACH)] * 2 + [room(2 * REACH)] * 2 + [dma] * 3,
        input_output_aliases={8: 0},
        name="encoder_edge",
    )(*args, in_vmem(cut(beside)), in_vmem(cut(beyond)), partial)


def serve_kernel(pos, owners, slots, k, e, *refs):
    sources = (len(refs) - 6) // (1 + PARTS)
    queries = refs[:sources]
    answers = refs[sources : (1 + PARTS) * sources]
    kb, eb, qb, ob, load_sems, answer_sem = refs[(1 + PARTS) * sources :]
    mine = pos[0]
    per = queries[0].shape[0]
    total = owners.shape[0] // per
    ahead = jnp.where(mine % 2 == 0, 1, -1)
    shifts = (0,) if sources == 1 else (ahead, -ahead)

    def candidate(i, t):
        source = mine + shifts[i]
        d = jnp.clip(source, 0, total - 1) * per + t
        live = (source >= 0) & (source < total) & (owners[d] == mine)
        return live, slots[0, d], slots[1, d]

    def loads(i, t, s0, s1):
        n = i * per + t
        sem = load_sems.at[n]
        return [
            pltpu.make_async_copy(a, b, sem)
            for a, b in (
                (queries[i].at[t], qb.at[n]),
                (k.at[s0], kb.at[n, 0]),
                (k.at[s1], kb.at[n, 1]),
                (e.at[s0], eb.at[n, 0]),
                (e.at[s1], eb.at[n, 1]),
            )
        ]

    for i in range(sources):
        for t in range(per):
            live, s0, s1 = candidate(i, t)

            @pl.when(live)
            def _(i=i, t=t, s0=s0, s1=s1):
                for copy in loads(i, t, s0, s1):
                    copy.start()

    share = per // PARTS

    def answer(part, i):
        rows = ob.at[pl.ds(i * per + part * share, share)]
        return pltpu.make_async_copy(rows, answers[part * sources + i], answer_sem)

    for part in range(PARTS):
        for i in range(sources):

            @pl.loop(part * share, (part + 1) * share)
            def _(t, i=i):
                live, s0, s1 = candidate(i, t)
                n = i * per + t

                @pl.when(live)
                def _():
                    for copy in loads(i, t, s0, s1):
                        copy.wait()
                    attend(
                        qb.at[n],
                        [kb.at[n, j] for j in range(CROSS)],
                        [eb.at[n, j] for j in range(CROSS)],
                        ob.at[n],
                    )

                @pl.when(jnp.logical_not(live))
                def _():
                    ob[n] = jnp.zeros(ob.shape[1:], ob.dtype)

            answer(part, i).start()

    for part in range(PARTS):
        for i in range(sources):
            answer(part, i).wait()


def serve_call(position, owners, slots, k3, e3, queries):
    width = k3.shape[-1]
    sources = len(queries)
    queries = [cut(x) for x in queries]
    per = queries[0].shape[0]
    smem = pl.BlockSpec(memory_space=pltpu.SMEM)
    hbm = pl.BlockSpec(memory_space=pl.ANY)
    vmem = pl.BlockSpec(memory_space=pltpu.VMEM)
    served = per * sources
    if sources > 1:
        queries = [in_vmem(x) for x in queries]
    out = pl.pallas_call(
        serve_kernel,
        in_specs=[smem] * 3 + [hbm] * 2 + [vmem if sources > 1 else hbm] * sources,
        out_specs=[hbm] * (sources * PARTS),
        out_shape=[jax.ShapeDtypeStruct((per // PARTS, BLK, width), jnp.bfloat16)]
        * (sources * PARTS),
        scratch_shapes=[
            pltpu.VMEM((served, CROSS, BLK, width), jnp.bfloat16),
            pltpu.VMEM((served, CROSS, BLK, width), jnp.bfloat16),
            pltpu.VMEM((served, BLK, width), jnp.bfloat16),
            pltpu.VMEM((served, BLK, width), jnp.bfloat16),
            pltpu.SemaphoreType.DMA((served,)),
            pltpu.SemaphoreType.DMA,
        ],
    )(position, owners, slots, k3, e3, *queries)
    return [x.reshape(-1, width) for x in out]


def cut(x):
    return x.reshape(-1, BLK, x.shape[-1])


def in_vmem(x):
    return pltpu.with_memory_space_constraint(x, pltpu.VMEM)


def move(plan, stages, load_sem, store_sem):
    loads = [pltpu.make_async_copy(src, stages[i], load_sem.at[i]) for i, (src, _) in enumerate(plan)]
    stores = [pltpu.make_async_copy(stages[i], dst, store_sem) for i, (_, dst) in enumerate(plan)]
    for load in loads:
        load.start()
    for load, store in zip(loads, stores):
        load.wait()
        store.start()
    for store in stores:
        store.wait()


def cut_kernel(part, w, a, b, c, sa, sb, sc, load_sem, store_sem):
    columns = a.shape[1]
    plan = []
    for flip, dst in ((2, a), (3, b), (1, c)):
        start = pl.multiple_of((part[0] ^ flip) * columns, columns)
        plan.append((w.at[:, pl.ds(start, columns)], dst))
    move(plan, (sa, sb, sc), load_sem, store_sem)


def cut_call(part, w, columns):
    shape = jax.ShapeDtypeStruct((w.shape[0], columns), w.dtype)
    hbm = pl.BlockSpec(memory_space=pl.ANY)
    return pl.pallas_call(
        cut_kernel,
        in_specs=[pl.BlockSpec(memory_space=pltpu.SMEM), hbm],
        out_specs=[hbm] * 3,
        out_shape=[shape] * 3,
        scratch_shapes=[pltpu.VMEM(shape.shape, w.dtype)] * 3
        + [pltpu.SemaphoreType.DMA((3,)), pltpu.SemaphoreType.DMA],
        name="cut_weight",
    )(part, w)


def project_kernel(part, c0, c1, w0, w1, r_ref, *refs):
    total = r_ref[...].astype(jnp.float32)
    for c, w in ((c0, w0), (c1, w1)):
        total = total + jnp.dot(c[...], w[...], preferred_element_type=jnp.float32)
    refs[-1][...] = total.astype(refs[-1].dtype)


def project_call(part, contexts, weights, added, dtype, index, out_tokens, earlier=None):
    tokens, width = contexts[0].shape
    columns = added.shape[1]
    here = index if added.shape[0] > tokens else 0
    there = index if out_tokens > tokens else 0
    c_spec = pl.BlockSpec((tokens, width), lambda i, p: (0, 0))
    w_specs = [
        pl.BlockSpec((width, columns), lambda i, p: (0, p[0]))
        if w.shape[1] > columns
        else pl.BlockSpec((width, columns), lambda i, p: (0, 0))
        for w in weights
    ]
    more = [] if earlier is None else [earlier]
    return pl.pallas_call(
        project_kernel,
        grid_spec=pltpu.PrefetchScalarGridSpec(
            num_scalar_prefetch=1,
            grid=(1,),
            in_specs=[c_spec] * 2
            + w_specs
            + [pl.BlockSpec((tokens, columns), lambda i, p: (here, 0))]
            + [pl.BlockSpec(memory_space=pl.ANY)] * len(more),
            out_specs=pl.BlockSpec((tokens, columns), lambda i, p: (there, 0)),
        ),
        out_shape=jax.ShapeDtypeStruct((out_tokens, columns), dtype),
        input_output_aliases={6: 0} if more else {},
    )(part, *[in_vmem(c) for c in contexts], *weights, added, *more)


def exchanged(block, first):
    route = []
    for i in range(first, lax.axis_size("seq") - 1, 2):
        route += [(i, i + 1), (i + 1, i)]
    return lax.ppermute(block, "seq", route)


def swapped(block, flip):
    return lax.ppermute(block, HEAD, [(i, i ^ flip) for i in range(4)])


def other_side(block, flip):
    axes = ("seq", *HEAD)
    route = []
    for s in range(lax.axis_size("seq")):
        for h in range(4):
            route.append((s * 4 + h, (s ^ Z_CHIPS) * 4 + (h ^ flip)))
    return lax.ppermute(block, axes, route)


def end_plane(s):
    return s % Z_CHIPS in (0, Z_CHIPS - 1)


def within_planes(block, flip):
    axes = ("seq", *HEAD)
    seqs = [s for s in range(lax.axis_size("seq")) if not end_plane(s)]
    return lax.ppermute(
        block, axes, [(s * 4 + h, s * 4 + (h ^ flip)) for s in seqs for h in range(4)]
    )


def to_end_planes(block, flip):
    axes = ("seq", *HEAD)
    route = []
    for s in range(lax.axis_size("seq")):
        if end_plane(s):
            inward = 1 if s % Z_CHIPS == 0 else -1
            for h in range(4):
                source = s + inward * (1 + h % 2)
                route.append((source * 4 + (h ^ flip), s * 4 + h))
    return lax.ppermute(block, axes, route)


def body(
    encoder_queries,
    encoder_keys,
    encoder_values,
    block_lists,
    block_counts,
    decoder_queries,
    span_owner,
    cross_slots,
    out_weight,
    decoder_input,
):
    position = lax.axis_index("seq").astype(jnp.int32).reshape(1)
    part = lax.axis_index(HEAD).astype(jnp.int32).reshape(1)
    blocks = encoder_queries.shape[0] // BLK
    width = encoder_queries.shape[1]
    columns = decoder_input.shape[1]
    lists = block_lists.T
    slots = cross_slots.T
    k3 = cut(encoder_keys)
    v3 = cut(encoder_values)
    beside, beyond = send_call(position, encoder_keys, encoder_values)
    beside = exchanged(beside, 0)
    beyond = exchanged(beyond, 1)
    q_beside = exchanged(decoder_queries, 0)
    q_beyond = exchanged(decoder_queries, 1)
    across2, across3, across1 = cut_call(part, out_weight, columns)
    w2_end = to_end_planes(across2, 2)
    w2 = within_planes(across2, 2)
    w3 = other_side(across3, 3)
    w1 = swapped(across1, 1)
    encoder_args = (position, block_counts, lists, encoder_queries, k3, v3)
    partial = encoder_call(*encoder_args)
    e3 = encoder_call(*encoder_args, edges=(beside, beyond, partial))
    tables = (position, span_owner, slots, k3, e3)
    answers = serve_call(*tables, [q_beside, q_beyond])
    returned = []
    for i in range(PARTS):
        from_beside = exchanged(answers[2 * i], 0)
        from_beyond = exchanged(answers[2 * i + 1], 1)
        returned.append((from_beside, from_beyond))
    own = serve_call(*tables, [decoder_queries])
    tokens = decoder_input.shape[0]
    contexts = [own[i] + returned[i][0] + returned[i][1] for i in range(PARTS)]
    decoder_out = None
    exchanges = []
    for context in contexts:
        across = swapped(context, 2)
        aside = swapped(context, 1)
        corner = swapped(across, 1)
        exchanges.append((aside, across, corner))
    aside, across, corner = exchanges[-1]
    w2, w2_end, aside = lax.optimization_barrier((w2, w2_end, aside))
    exchanges[-1] = (aside, across, corner)
    w2 = w2 + w2_end
    for i, context in enumerate(contexts):
        aside, across, corner = exchanges[i]
        total = project_call(
            part, [context, aside], [out_weight, w1], decoder_input, jnp.float32, i, tokens // PARTS
        )
        decoder_out = project_call(
            part, [across, corner], [w2, w3], total, jnp.bfloat16, i, tokens, decoder_out
        )
    return (e3.reshape(blocks * BLK, width), decoder_out)


def solution(mesh):
    split = Mesh(mesh.devices.reshape(mesh.shape["seq"], 2, 2), ("seq", "head_0", "head_1"))
    placed = (
        P("seq", HEAD),
        P("seq", HEAD),
        P("seq", HEAD),
        P("seq", None),
        P("seq"),
        P("seq", HEAD),
        P(),
        P(),
        P(HEAD, None),
        P("seq", HEAD),
    )
    return jax.shard_map(
        body,
        mesh=split,
        in_specs=placed,
        out_specs=(P("seq", HEAD), P("seq", HEAD)),
        check_vma=False,
    )
```

```python
import functools

import jax
import jax.numpy as jnp
from jax import lax
from jax.experimental import pallas as pl
from jax.experimental.pallas import tpu as pltpu
from jax.sharding import Mesh
from jax.sharding import PartitionSpec as P


HD = 64
BLK = 128
REACH = 2
SLOTS = 4
CROSS = 2
QUAD = 4
PARTS = 2
ANSWERS = 1
Z_CHIPS = 8
QW = HD * QUAD
HEAD = ("head_0", "head_1")
EXP_SCALE = 0.125 * 1.4426950408889634


def attend(q_ref, k_refs, v_refs, o_ref):
    quads = [pl.ds(c * QW, QW) for c in range(q_ref.shape[-1] // QW)]
    lane = lax.broadcasted_iota(jnp.int32, (BLK, QW), 1) // HD
    scores = []
    for cols in quads:
        q = q_ref[:, cols]
        zero = jnp.zeros_like(q)
        rows = jnp.concatenate([jnp.where(lane == h, q, zero) for h in range(QUAD)], axis=0)
        k = jnp.concatenate([r[:, cols] for r in k_refs], axis=0)
        scores.append(
            lax.dot_general(rows, k, (((1,), (1,)), ((), ())), preferred_element_type=jnp.float32)
        )
    for cols, s in zip(quads, scores):
        m = jnp.max(s, axis=1, keepdims=True)
        p = jnp.exp2((s - m) * EXP_SCALE)
        l = jnp.sum(p, axis=1, keepdims=True)
        v = jnp.concatenate([r[:, cols] for r in v_refs], axis=0)
        o = lax.dot_general(
            p.astype(jnp.bfloat16), v, (((1,), (0,)), ((), ())), preferred_element_type=jnp.float32
        )
        o = o * (1.0 / l)
        out = o[:BLK]
        for h in range(1, QUAD):
            out = jnp.where(lane == h, o[h * BLK : (h + 1) * BLK], out)
        o_ref[:, cols] = out.astype(jnp.bfloat16)


def send_kernel(pos, k, v, beside, beyond, s0, s1, s2, s3, load_sem, store_sem):
    halo = REACH * BLK
    tail = pl.ds(k.shape[0] - halo, halo)
    head = pl.ds(0, halo)
    values = pl.ds(halo, halo)
    sources = ((k.at[tail], s0), (v.at[tail], s1), (k.at[head], s2), (v.at[head], s3))
    loads = [pltpu.make_async_copy(x, y, load_sem) for x, y in sources]
    for load in loads:
        load.start()
    for load in loads:
        load.wait()

    def stores(up, down):
        pairs = ((s0, up.at[head]), (s1, up.at[values]), (s2, down.at[head]), (s3, down.at[values]))
        return [pltpu.make_async_copy(a, b, store_sem) for a, b in pairs]

    even = pos[0] % 2 == 0

    @pl.when(even)
    def _():
        for store in stores(beside, beyond):
            store.start()

    @pl.when(jnp.logical_not(even))
    def _():
        for store in stores(beyond, beside):
            store.start()

    for store in stores(beside, beyond):
        store.wait()


def send_call(position, k, v):
    halo = REACH * BLK
    width = k.shape[1]
    shape = jax.ShapeDtypeStruct((2 * halo, width), k.dtype)
    hbm = pl.BlockSpec(memory_space=pl.ANY)
    return pl.pallas_call(
        send_kernel,
        in_specs=[pl.BlockSpec(memory_space=pltpu.SMEM)] + [hbm] * 2,
        out_specs=[hbm] * 2,
        out_shape=[shape] * 2,
        scratch_shapes=[pltpu.VMEM((halo, width), k.dtype)] * 4
        + [pltpu.SemaphoreType.DMA, pltpu.SemaphoreType.DMA],
        name="pack_edges",
    )(position, k, v)


def encode_block(b, base, counts, lists, q_ref, kb, vb, o_ref):
    count = counts[b]
    ids = [lists[j, b] - base for j in range(SLOTS)]
    for n in range(1, SLOTS + 1):

        @pl.when(count == n)
        def _(n=n):
            attend(q_ref, [kb.at[i] for i in ids[:n]], [vb.at[i] for i in ids[:n]], o_ref)


def inner_kernel(pos, counts, lists, q, k, v, e, kb, vb, qb, eb, k_sem, v_sem, q_sem, e_sem):
    blocks = k.shape[0]
    base = pos[0] * blocks

    def keys(i):
        return pltpu.make_async_copy(k.at[i], kb.at[i], k_sem.at[i])

    def values(i):
        return pltpu.make_async_copy(v.at[i], vb.at[i], v_sem.at[i])

    def queries(i):
        return pltpu.make_async_copy(q.at[i], qb.at[i], q_sem.at[i])

    def result(i):
        return pltpu.make_async_copy(eb.at[i], e.at[i], e_sem)

    for i in range(blocks):
        keys(i).start()
        values(i).start()
        if REACH <= i < blocks - REACH:
            queries(i).start()
    for i in range(2 * REACH):
        keys(i).wait()
        values(i).wait()

    @pl.loop(REACH, blocks - REACH)
    def _(b):
        keys(b + REACH).wait()
        values(b + REACH).wait()
        queries(b).wait()
        encode_block(b, base, counts, lists, qb.at[b], kb, vb, eb.at[b])
        result(b).start()

    for i in range(REACH, blocks - REACH):
        result(i).wait()


def edge_kernel(
    pos, counts, lists, q, k, v, beside, beyond, _, e, kb, vb, qb, eb, far_sem, in_sem, e_sem
):
    blocks = k.shape[0]
    near = 2 * REACH
    even = pos[0] % 2 == 0
    base = pos[0] * blocks - REACH

    def edges(up, down):
        pairs = (
            (up.at[pl.ds(0, REACH)], kb.at[pl.ds(0, REACH)]),
            (up.at[pl.ds(REACH, REACH)], vb.at[pl.ds(0, REACH)]),
            (down.at[pl.ds(0, REACH)], kb.at[pl.ds(REACH + blocks, REACH)]),
            (down.at[pl.ds(REACH, REACH)], vb.at[pl.ds(REACH + blocks, REACH)]),
        )
        return [pltpu.make_async_copy(a, b, far_sem) for a, b in pairs]

    local = []
    for start in (0, blocks - near):
        here = pl.ds(start, near)
        there = pl.ds(REACH + start, near)
        local.append(pltpu.make_async_copy(k.at[here], kb.at[there], in_sem))
        local.append(pltpu.make_async_copy(v.at[here], vb.at[there], in_sem))
    for i, start in enumerate((0, blocks - REACH)):
        local.append(
            pltpu.make_async_copy(q.at[pl.ds(start, REACH)], qb.at[pl.ds(i * REACH, REACH)], in_sem)
        )
    for copy in local:
        copy.start()

    @pl.when(even)
    def _():
        for copy in edges(beyond, beside):
            copy.start()

    @pl.when(jnp.logical_not(even))
    def _():
        for copy in edges(beside, beyond):
            copy.start()

    for copy in local + edges(beyond, beside):
        copy.wait()

    @pl.loop(0, near)
    def _(t):
        b = jnp.where(t < REACH, t, blocks - near + t)
        encode_block(b, base, counts, lists, qb.at[t], kb, vb, eb.at[t])
        pltpu.make_async_copy(eb.at[t], e.at[b], e_sem).start()

    for t in range(near):
        pltpu.make_async_copy(eb.at[t], e.at[t], e_sem).wait()


def encoder_call(position, counts, lists, q, k3, v3, edges=None):
    blocks, _, width = k3.shape
    smem = pl.BlockSpec(memory_space=pltpu.SMEM)
    hbm = pl.BlockSpec(memory_space=pl.ANY)
    dma = pltpu.SemaphoreType.DMA

    def room(n):
        return pltpu.VMEM((n, BLK, width), jnp.bfloat16)

    shape = jax.ShapeDtypeStruct(k3.shape, jnp.bfloat16)
    args = (position, counts, lists, cut(q), k3, v3)
    if edges is None:
        return pl.pallas_call(
            inner_kernel,
            in_specs=[smem] * 3 + [hbm] * 3,
            out_specs=hbm,
            out_shape=shape,
            scratch_shapes=[room(blocks)] * 4 + [dma((blocks,))] * 3 + [dma],
            name="encoder_inner",
        )(*args)
    beside, beyond, partial = edges
    return pl.pallas_call(
        edge_kernel,
        in_specs=[smem] * 3 + [hbm] * 3 + [pl.BlockSpec(memory_space=pltpu.VMEM)] * 2 + [hbm],
        out_specs=hbm,
        out_shape=shape,
        scratch_shapes=[room(blocks + 2 * REACH)] * 2 + [room(2 * REACH)] * 2 + [dma] * 3,
        input_output_aliases={8: 0},
        name="encoder_edge",
    )(*args, in_vmem(cut(beside)), in_vmem(cut(beyond)), partial)


def serve_kernel(pos, owners, slots, k, e, *refs):
    sources = (len(refs) - 6) // (1 + ANSWERS)
    queries = refs[:sources]
    answers = refs[sources : (1 + ANSWERS) * sources]
    kb, eb, qb, ob, load_sems, answer_sem = refs[(1 + ANSWERS) * sources :]
    mine = pos[0]
    per = queries[0].shape[0]
    total = owners.shape[0] // per
    ahead = jnp.where(mine % 2 == 0, 1, -1)
    shifts = (0,) if sources == 1 else (ahead, -ahead)

    def candidate(i, t):
        source = mine + shifts[i]
        d = jnp.clip(source, 0, total - 1) * per + t
        live = (source >= 0) & (source < total) & (owners[d] == mine)
        return live, slots[0, d], slots[1, d]

    def loads(i, t, s0, s1):
        n = i * per + t
        sem = load_sems.at[n]
        return [
            pltpu.make_async_copy(a, b, sem)
            for a, b in (
                (queries[i].at[t], qb.at[n]),
                (k.at[s0], kb.at[n, 0]),
                (k.at[s1], kb.at[n, 1]),
                (e.at[s0], eb.at[n, 0]),
                (e.at[s1], eb.at[n, 1]),
            )
        ]

    for i in range(sources):
        for t in range(per):
            live, s0, s1 = candidate(i, t)

            @pl.when(live)
            def _(i=i, t=t, s0=s0, s1=s1):
                for copy in loads(i, t, s0, s1):
                    copy.start()

    share = per // ANSWERS

    def answer(part, i):
        rows = ob.at[pl.ds(i * per + part * share, share)]
        return pltpu.make_async_copy(rows, answers[part * sources + i], answer_sem)

    for part in range(ANSWERS):
        for i in range(sources):

            @pl.loop(part * share, (part + 1) * share)
            def _(t, i=i):
                live, s0, s1 = candidate(i, t)
                n = i * per + t

                @pl.when(live)
                def _():
                    for copy in loads(i, t, s0, s1):
                        copy.wait()
                    attend(
                        qb.at[n],
                        [kb.at[n, j] for j in range(CROSS)],
                        [eb.at[n, j] for j in range(CROSS)],
                        ob.at[n],
                    )

                @pl.when(jnp.logical_not(live))
                def _():
                    ob[n] = jnp.zeros(ob.shape[1:], ob.dtype)

            answer(part, i).start()

    for part in range(ANSWERS):
        for i in range(sources):
            answer(part, i).wait()


def serve_call(position, owners, slots, k3, e3, queries):
    width = k3.shape[-1]
    sources = len(queries)
    queries = [cut(x) for x in queries]
    per = queries[0].shape[0]
    smem = pl.BlockSpec(memory_space=pltpu.SMEM)
    hbm = pl.BlockSpec(memory_space=pl.ANY)
    vmem = pl.BlockSpec(memory_space=pltpu.VMEM)
    served = per * sources
    if sources > 1:
        queries = [in_vmem(x) for x in queries]
    out = pl.pallas_call(
        serve_kernel,
        in_specs=[smem] * 3 + [hbm] * 2 + [vmem if sources > 1 else hbm] * sources,
        out_specs=[hbm] * (sources * ANSWERS),
        out_shape=[jax.ShapeDtypeStruct((per // ANSWERS, BLK, width), jnp.bfloat16)]
        * (sources * ANSWERS),
        scratch_shapes=[
            pltpu.VMEM((served, CROSS, BLK, width), jnp.bfloat16),
            pltpu.VMEM((served, CROSS, BLK, width), jnp.bfloat16),
            pltpu.VMEM((served, BLK, width), jnp.bfloat16),
            pltpu.VMEM((served, BLK, width), jnp.bfloat16),
            pltpu.SemaphoreType.DMA((served,)),
            pltpu.SemaphoreType.DMA,
        ],
    )(position, owners, slots, k3, e3, *queries)
    return [x.reshape(-1, width) for x in out]


def cut(x):
    return x.reshape(-1, BLK, x.shape[-1])


def in_vmem(x):
    return pltpu.with_memory_space_constraint(x, pltpu.VMEM)


def move(plan, stages, load_sem, store_sem):
    loads = [pltpu.make_async_copy(src, stages[i], load_sem.at[i]) for i, (src, _) in enumerate(plan)]
    stores = [pltpu.make_async_copy(stages[i], dst, store_sem) for i, (_, dst) in enumerate(plan)]
    for load in loads:
        load.start()
    for load, store in zip(loads, stores):
        load.wait()
        store.start()
    for store in stores:
        store.wait()


def cut_kernel(part, w, a, b, c, d, sa, sb, sc, sd, load_sem, store_sem):
    columns = a.shape[1]
    split = a.shape[0]
    plan = []
    for flip, rows, dst in (
        (2, pl.ds(0, split), a),
        (2, pl.ds(split, w.shape[0] - split), b),
        (3, pl.ds(0, w.shape[0]), c),
        (1, pl.ds(0, w.shape[0]), d),
    ):
        start = pl.multiple_of((part[0] ^ flip) * columns, columns)
        plan.append((w.at[rows, pl.ds(start, columns)], dst))
    move(plan, (sa, sb, sc, sd), load_sem, store_sem)


def cut_call(part, w, columns):
    rows = w.shape[0]
    split = rows * 3 // 4
    shapes = [(n, columns) for n in (split, rows - split, rows, rows)]
    hbm = pl.BlockSpec(memory_space=pl.ANY)
    return pl.pallas_call(
        cut_kernel,
        in_specs=[pl.BlockSpec(memory_space=pltpu.SMEM), hbm],
        out_specs=[hbm] * 4,
        out_shape=[jax.ShapeDtypeStruct(x, w.dtype) for x in shapes],
        scratch_shapes=[pltpu.VMEM(x, w.dtype) for x in shapes]
        + [pltpu.SemaphoreType.DMA((4,)), pltpu.SemaphoreType.DMA],
        name="cut_weight",
    )(part, w)


def project_kernel(counts, part, c0, c1, *refs):
    first, second = counts
    weights = refs[: first + second]
    r_ref = refs[first + second]
    total = r_ref[...].astype(jnp.float32)
    for c, ws in ((c0, weights[:first]), (c1, weights[first:])):
        w = jnp.concatenate([x[...] for x in ws], axis=0) if len(ws) > 1 else ws[0][...]
        total = total + jnp.dot(c[...], w, preferred_element_type=jnp.float32)
    refs[-1][...] = total.astype(refs[-1].dtype)


def project_call(part, contexts, weights, added, dtype, index, out_tokens, earlier=None):
    tokens, width = contexts[0].shape
    columns = added.shape[1]
    here = index if added.shape[0] > tokens else 0
    there = index if out_tokens > tokens else 0
    c_spec = pl.BlockSpec((tokens, width), lambda i, p: (0, 0))
    flat = [w for ws in weights for w in ws]
    w_specs = [
        pl.BlockSpec((w.shape[0], columns), lambda i, p: (0, p[0]))
        if w.shape[1] > columns
        else pl.BlockSpec((w.shape[0], columns), lambda i, p: (0, 0))
        for w in flat
    ]
    more = [] if earlier is None else [earlier]
    return pl.pallas_call(
        functools.partial(project_kernel, tuple(len(ws) for ws in weights)),
        grid_spec=pltpu.PrefetchScalarGridSpec(
            num_scalar_prefetch=1,
            grid=(1,),
            in_specs=[c_spec] * 2
            + w_specs
            + [pl.BlockSpec((tokens, columns), lambda i, p: (here, 0))]
            + [pl.BlockSpec(memory_space=pl.ANY)] * len(more),
            out_specs=pl.BlockSpec((tokens, columns), lambda i, p: (there, 0)),
        ),
        out_shape=jax.ShapeDtypeStruct((out_tokens, columns), dtype),
        input_output_aliases={4 + len(flat): 0} if more else {},
    )(part, *[in_vmem(c) for c in contexts], *flat, added, *more)


def exchanged(block, first):
    route = []
    for i in range(first, lax.axis_size("seq") - 1, 2):
        route += [(i, i + 1), (i + 1, i)]
    return lax.ppermute(block, "seq", route)


def swapped(block, flip):
    return lax.ppermute(block, HEAD, [(i, i ^ flip) for i in range(4)])


def other_side(block, flip):
    axes = ("seq", *HEAD)
    route = []
    for s in range(lax.axis_size("seq")):
        for h in range(4):
            route.append((s * 4 + h, (s ^ Z_CHIPS) * 4 + (h ^ flip)))
    return lax.ppermute(block, axes, route)


def body(
    encoder_queries,
    encoder_keys,
    encoder_values,
    block_lists,
    block_counts,
    decoder_queries,
    span_owner,
    cross_slots,
    out_weight,
    decoder_input,
):
    position = lax.axis_index("seq").astype(jnp.int32).reshape(1)
    part = lax.axis_index(HEAD).astype(jnp.int32).reshape(1)
    blocks = encoder_queries.shape[0] // BLK
    width = encoder_queries.shape[1]
    columns = decoder_input.shape[1]
    lists = block_lists.T
    slots = cross_slots.T
    k3 = cut(encoder_keys)
    v3 = cut(encoder_values)
    beside, beyond = send_call(position, encoder_keys, encoder_values)
    beside = exchanged(beside, 0)
    beyond = exchanged(beyond, 1)
    q_beside = exchanged(decoder_queries, 0)
    q_beyond = exchanged(decoder_queries, 1)
    across2, around2, across3, across1 = cut_call(part, out_weight, columns)
    w2_most = swapped(across2, 2)
    w2_rest = other_side(around2, 2)
    w3 = other_side(across3, 3)
    w1 = swapped(across1, 1)
    encoder_args = (position, block_counts, lists, encoder_queries, k3, v3)
    partial = encoder_call(*encoder_args)
    e3 = encoder_call(*encoder_args, edges=(beside, beyond, partial))
    tables = (position, span_owner, slots, k3, e3)
    answers = serve_call(*tables, [q_beside, q_beyond])
    from_beside = exchanged(answers[0], 0)
    from_beyond = exchanged(answers[1], 1)
    (own,) = serve_call(*tables, [decoder_queries])
    tokens = decoder_input.shape[0]
    share = tokens // PARTS
    decoder_out = None
    for i in range(PARTS):
        rows = slice(i * share, (i + 1) * share)
        context = own[rows] + from_beside[rows] + from_beyond[rows]
        across = swapped(context, 2)
        aside = swapped(context, 1)
        corner = swapped(across, 1)
        total = project_call(
            part, [context, aside], [[out_weight], [w1]], decoder_input, jnp.float32, i, share
        )
        decoder_out = project_call(
            part,
            [across, corner],
            [[in_vmem(w2_most), in_vmem(w2_rest)], [w3]],
            total,
            jnp.bfloat16,
            i,
            tokens,
            decoder_out,
        )
    return (e3.reshape(blocks * BLK, width), decoder_out)


def solution(mesh):
    split = Mesh(mesh.devices.reshape(mesh.shape["seq"], 2, 2), ("seq", "head_0", "head_1"))
    placed = (
        P("seq", HEAD),
        P("seq", HEAD),
        P("seq", HEAD),
        P("seq", None),
        P("seq"),
        P("seq", HEAD),
        P(),
        P(),
        P(HEAD, None),
        P("seq", HEAD),
    )
    return jax.shard_map(
        body,
        mesh=split,
        in_specs=placed,
        out_specs=(P("seq", HEAD), P("seq", HEAD)),
        check_vma=False,
    )
```

```python
import functools

import jax
import jax.numpy as jnp
from jax import lax
from jax.experimental import pallas as pl
from jax.experimental.pallas import tpu as pltpu
from jax.sharding import Mesh
from jax.sharding import PartitionSpec as P


HD = 64
BLK = 128
REACH = 2
SLOTS = 4
CROSS = 2
QUAD = 4
PARTS = 2
ANSWERS = 1
Z_CHIPS = 8
QW = HD * QUAD
HEAD = ("head_0", "head_1")
EXP_SCALE = 0.125 * 1.4426950408889634


def attend(q_ref, k_refs, v_refs, o_ref):
    quads = [pl.ds(c * QW, QW) for c in range(q_ref.shape[-1] // QW)]
    lane = lax.broadcasted_iota(jnp.int32, (BLK, QW), 1) // HD
    scores = []
    for cols in quads:
        q = q_ref[:, cols]
        zero = jnp.zeros_like(q)
        rows = jnp.concatenate([jnp.where(lane == h, q, zero) for h in range(QUAD)], axis=0)
        k = jnp.concatenate([r[:, cols] for r in k_refs], axis=0)
        scores.append(
            lax.dot_general(rows, k, (((1,), (1,)), ((), ())), preferred_element_type=jnp.float32)
        )
    for cols, s in zip(quads, scores):
        m = jnp.max(s, axis=1, keepdims=True)
        p = jnp.exp2((s - m) * EXP_SCALE)
        l = jnp.sum(p, axis=1, keepdims=True)
        v = jnp.concatenate([r[:, cols] for r in v_refs], axis=0)
        o = lax.dot_general(
            p.astype(jnp.bfloat16), v, (((1,), (0,)), ((), ())), preferred_element_type=jnp.float32
        )
        o = o * (1.0 / l)
        out = o[:BLK]
        for h in range(1, QUAD):
            out = jnp.where(lane == h, o[h * BLK : (h + 1) * BLK], out)
        o_ref[:, cols] = out.astype(jnp.bfloat16)


def send_kernel(pos, k, v, beside, beyond, s0, s1, s2, s3, load_sem, store_sem):
    halo = REACH * BLK
    tail = pl.ds(k.shape[0] - halo, halo)
    head = pl.ds(0, halo)
    values = pl.ds(halo, halo)
    sources = ((k.at[tail], s0), (v.at[tail], s1), (k.at[head], s2), (v.at[head], s3))
    loads = [pltpu.make_async_copy(x, y, load_sem) for x, y in sources]
    for load in loads:
        load.start()
    for load in loads:
        load.wait()

    def stores(up, down):
        pairs = ((s0, up.at[head]), (s1, up.at[values]), (s2, down.at[head]), (s3, down.at[values]))
        return [pltpu.make_async_copy(a, b, store_sem) for a, b in pairs]

    even = pos[0] % 2 == 0

    @pl.when(even)
    def _():
        for store in stores(beside, beyond):
            store.start()

    @pl.when(jnp.logical_not(even))
    def _():
        for store in stores(beyond, beside):
            store.start()

    for store in stores(beside, beyond):
        store.wait()


def send_call(position, k, v):
    halo = REACH * BLK
    width = k.shape[1]
    shape = jax.ShapeDtypeStruct((2 * halo, width), k.dtype)
    hbm = pl.BlockSpec(memory_space=pl.ANY)
    return pl.pallas_call(
        send_kernel,
        in_specs=[pl.BlockSpec(memory_space=pltpu.SMEM)] + [hbm] * 2,
        out_specs=[hbm] * 2,
        out_shape=[shape] * 2,
        scratch_shapes=[pltpu.VMEM((halo, width), k.dtype)] * 4
        + [pltpu.SemaphoreType.DMA, pltpu.SemaphoreType.DMA],
        name="pack_edges",
    )(position, k, v)


def encode_block(b, base, counts, lists, q_ref, kb, vb, o_ref):
    count = counts[b]
    ids = [lists[j, b] - base for j in range(SLOTS)]
    for n in range(1, SLOTS + 1):

        @pl.when(count == n)
        def _(n=n):
            attend(q_ref, [kb.at[i] for i in ids[:n]], [vb.at[i] for i in ids[:n]], o_ref)


def inner_kernel(pos, counts, lists, part, q, k, v, w, e, *refs):
    pieces, (kb, vb, qb, eb) = refs[:4], refs[4:8]
    stages = refs[8:12]
    k_sem, v_sem, q_sem, e_sem, load_sem, store_sem = refs[12:]
    columns = pieces[0].shape[1]
    split = pieces[0].shape[0]
    cuts = (
        (2, pl.ds(0, split)),
        (2, pl.ds(split, w.shape[0] - split)),
        (3, pl.ds(0, w.shape[0])),
        (1, pl.ds(0, w.shape[0])),
    )

    def load(i):
        flip, rows = cuts[i]
        start = pl.multiple_of((part[0] ^ flip) * columns, columns)
        return pltpu.make_async_copy(w.at[rows, pl.ds(start, columns)], stages[i], load_sem.at[i])

    def store(i):
        return pltpu.make_async_copy(stages[i], pieces[i], store_sem.at[i])

    blocks = k.shape[0]
    base = pos[0] * blocks

    def keys(i):
        return pltpu.make_async_copy(k.at[i], kb.at[i], k_sem.at[i])

    def values(i):
        return pltpu.make_async_copy(v.at[i], vb.at[i], v_sem.at[i])

    def queries(i):
        return pltpu.make_async_copy(q.at[i], qb.at[i], q_sem.at[i])

    def result(i):
        return pltpu.make_async_copy(eb.at[i], e.at[i], e_sem)

    for i in range(blocks):
        keys(i).start()
        values(i).start()
        if REACH <= i < blocks - REACH:
            queries(i).start()
    for i in range(len(cuts)):
        load(i).start()
    for i in range(2 * REACH):
        keys(i).wait()
        values(i).wait()

    @pl.loop(REACH, blocks - REACH)
    def _(b):
        keys(b + REACH).wait()
        values(b + REACH).wait()
        queries(b).wait()
        encode_block(b, base, counts, lists, qb.at[b], kb, vb, eb.at[b])
        result(b).start()
        for i in range(len(cuts)):

            @pl.when(b == REACH + 1 + i)
            def _(i=i):
                load(i).wait()
                store(i).start()

    for i in range(REACH, blocks - REACH):
        result(i).wait()
    for i in range(len(cuts)):
        store(i).wait()


def edge_kernel(
    pos, counts, lists, q, k, v, beside, beyond, _, e, kb, vb, qb, eb, far_sem, in_sem, e_sem
):
    blocks = k.shape[0]
    near = 2 * REACH
    even = pos[0] % 2 == 0
    base = pos[0] * blocks - REACH

    def edges(up, down):
        pairs = (
            (up.at[pl.ds(0, REACH)], kb.at[pl.ds(0, REACH)]),
            (up.at[pl.ds(REACH, REACH)], vb.at[pl.ds(0, REACH)]),
            (down.at[pl.ds(0, REACH)], kb.at[pl.ds(REACH + blocks, REACH)]),
            (down.at[pl.ds(REACH, REACH)], vb.at[pl.ds(REACH + blocks, REACH)]),
        )
        return [pltpu.make_async_copy(a, b, far_sem) for a, b in pairs]

    local = []
    for start in (0, blocks - near):
        here = pl.ds(start, near)
        there = pl.ds(REACH + start, near)
        local.append(pltpu.make_async_copy(k.at[here], kb.at[there], in_sem))
        local.append(pltpu.make_async_copy(v.at[here], vb.at[there], in_sem))
    for i, start in enumerate((0, blocks - REACH)):
        local.append(
            pltpu.make_async_copy(q.at[pl.ds(start, REACH)], qb.at[pl.ds(i * REACH, REACH)], in_sem)
        )
    for copy in local:
        copy.start()

    @pl.when(even)
    def _():
        for copy in edges(beyond, beside):
            copy.start()

    @pl.when(jnp.logical_not(even))
    def _():
        for copy in edges(beside, beyond):
            copy.start()

    for copy in local + edges(beyond, beside):
        copy.wait()

    @pl.loop(0, near)
    def _(t):
        b = jnp.where(t < REACH, t, blocks - near + t)
        encode_block(b, base, counts, lists, qb.at[t], kb, vb, eb.at[t])
        pltpu.make_async_copy(eb.at[t], e.at[b], e_sem).start()

    for t in range(near):
        pltpu.make_async_copy(eb.at[t], e.at[t], e_sem).wait()


def encoder_call(position, counts, lists, q, k3, v3, weight=None, edges=None):
    blocks, _, width = k3.shape
    smem = pl.BlockSpec(memory_space=pltpu.SMEM)
    hbm = pl.BlockSpec(memory_space=pl.ANY)
    dma = pltpu.SemaphoreType.DMA

    def room(n):
        return pltpu.VMEM((n, BLK, width), jnp.bfloat16)

    shape = jax.ShapeDtypeStruct(k3.shape, jnp.bfloat16)
    args = (position, counts, lists, cut(q), k3, v3)
    if edges is None:
        part, w, columns = weight
        rows = w.shape[0]
        split = rows * 3 // 4
        pieces = [(n, columns) for n in (split, rows - split, rows, rows)]
        return pl.pallas_call(
            inner_kernel,
            in_specs=[smem] * 4 + [hbm] * 4,
            out_specs=[hbm] * 5,
            out_shape=[shape] + [jax.ShapeDtypeStruct(x, w.dtype) for x in pieces],
            scratch_shapes=[room(blocks)] * 4
            + [pltpu.VMEM(x, w.dtype) for x in pieces]
            + [dma((blocks,))] * 3
            + [dma, dma((4,)), dma((4,))],
            name="encoder_inner",
        )(*args[:3], part, *args[3:], w)
    beside, beyond, partial = edges
    return pl.pallas_call(
        edge_kernel,
        in_specs=[smem] * 3 + [hbm] * 3 + [pl.BlockSpec(memory_space=pltpu.VMEM)] * 2 + [hbm],
        out_specs=hbm,
        out_shape=shape,
        scratch_shapes=[room(blocks + 2 * REACH)] * 2 + [room(2 * REACH)] * 2 + [dma] * 3,
        input_output_aliases={8: 0},
        name="encoder_edge",
    )(*args, in_vmem(cut(beside)), in_vmem(cut(beyond)), partial)


def serve_kernel(pos, owners, slots, k, e, *refs):
    sources = (len(refs) - 6) // (1 + ANSWERS)
    queries = refs[:sources]
    answers = refs[sources : (1 + ANSWERS) * sources]
    kb, eb, qb, ob, load_sems, answer_sem = refs[(1 + ANSWERS) * sources :]
    mine = pos[0]
    per = queries[0].shape[0]
    total = owners.shape[0] // per
    ahead = jnp.where(mine % 2 == 0, 1, -1)
    shifts = (0,) if sources == 1 else (ahead, -ahead)

    def candidate(i, t):
        source = mine + shifts[i]
        d = jnp.clip(source, 0, total - 1) * per + t
        live = (source >= 0) & (source < total) & (owners[d] == mine)
        return live, slots[0, d], slots[1, d]

    def loads(i, t, s0, s1):
        n = i * per + t
        sem = load_sems.at[n]
        return [
            pltpu.make_async_copy(a, b, sem)
            for a, b in (
                (queries[i].at[t], qb.at[n]),
                (k.at[s0], kb.at[n, 0]),
                (k.at[s1], kb.at[n, 1]),
                (e.at[s0], eb.at[n, 0]),
                (e.at[s1], eb.at[n, 1]),
            )
        ]

    for i in range(sources):
        for t in range(per):
            live, s0, s1 = candidate(i, t)

            @pl.when(live)
            def _(i=i, t=t, s0=s0, s1=s1):
                for copy in loads(i, t, s0, s1):
                    copy.start()

    share = per // ANSWERS

    def answer(part, i):
        rows = ob.at[pl.ds(i * per + part * share, share)]
        return pltpu.make_async_copy(rows, answers[part * sources + i], answer_sem)

    for part in range(ANSWERS):
        for i in range(sources):

            @pl.loop(part * share, (part + 1) * share)
            def _(t, i=i):
                live, s0, s1 = candidate(i, t)
                n = i * per + t

                @pl.when(live)
                def _():
                    for copy in loads(i, t, s0, s1):
                        copy.wait()
                    attend(
                        qb.at[n],
                        [kb.at[n, j] for j in range(CROSS)],
                        [eb.at[n, j] for j in range(CROSS)],
                        ob.at[n],
                    )

                @pl.when(jnp.logical_not(live))
                def _():
                    ob[n] = jnp.zeros(ob.shape[1:], ob.dtype)

            answer(part, i).start()

    for part in range(ANSWERS):
        for i in range(sources):
            answer(part, i).wait()


def serve_call(position, owners, slots, k3, e3, queries):
    width = k3.shape[-1]
    sources = len(queries)
    queries = [cut(x) for x in queries]
    per = queries[0].shape[0]
    smem = pl.BlockSpec(memory_space=pltpu.SMEM)
    hbm = pl.BlockSpec(memory_space=pl.ANY)
    vmem = pl.BlockSpec(memory_space=pltpu.VMEM)
    served = per * sources
    if sources > 1:
        queries = [in_vmem(x) for x in queries]
    out = pl.pallas_call(
        serve_kernel,
        in_specs=[smem] * 3 + [hbm] * 2 + [vmem if sources > 1 else hbm] * sources,
        out_specs=[hbm] * (sources * ANSWERS),
        out_shape=[jax.ShapeDtypeStruct((per // ANSWERS, BLK, width), jnp.bfloat16)]
        * (sources * ANSWERS),
        scratch_shapes=[
            pltpu.VMEM((served, CROSS, BLK, width), jnp.bfloat16),
            pltpu.VMEM((served, CROSS, BLK, width), jnp.bfloat16),
            pltpu.VMEM((served, BLK, width), jnp.bfloat16),
            pltpu.VMEM((served, BLK, width), jnp.bfloat16),
            pltpu.SemaphoreType.DMA((served,)),
            pltpu.SemaphoreType.DMA,
        ],
    )(position, owners, slots, k3, e3, *queries)
    return [x.reshape(-1, width) for x in out]


def cut(x):
    return x.reshape(-1, BLK, x.shape[-1])


def in_vmem(x):
    return pltpu.with_memory_space_constraint(x, pltpu.VMEM)


def project_kernel(counts, part, c0, c1, *refs):
    first, second = counts
    weights = refs[: first + second]
    r_ref = refs[first + second]
    total = r_ref[...].astype(jnp.float32)
    for c, ws in ((c0, weights[:first]), (c1, weights[first:])):
        w = jnp.concatenate([x[...] for x in ws], axis=0) if len(ws) > 1 else ws[0][...]
        total = total + jnp.dot(c[...], w, preferred_element_type=jnp.float32)
    refs[-1][...] = total.astype(refs[-1].dtype)


def project_call(part, contexts, weights, added, dtype, index, out_tokens, earlier=None):
    tokens, width = contexts[0].shape
    columns = added.shape[1]
    tile = min(tokens, out_tokens // PARTS)
    here = index if added.shape[0] > tokens else 0
    there = index if out_tokens > tokens else 0
    c_spec = pl.BlockSpec((tile, width), lambda i, p: (i, 0))
    flat = [w for ws in weights for w in ws]
    w_specs = [
        pl.BlockSpec((w.shape[0], columns), lambda i, p: (0, p[0]))
        if w.shape[1] > columns
        else pl.BlockSpec((w.shape[0], columns), lambda i, p: (0, 0))
        for w in flat
    ]
    more = [] if earlier is None else [earlier]
    return pl.pallas_call(
        functools.partial(project_kernel, tuple(len(ws) for ws in weights)),
        grid_spec=pltpu.PrefetchScalarGridSpec(
            num_scalar_prefetch=1,
            grid=(tokens // tile,),
            in_specs=[c_spec] * 2
            + w_specs
            + [pl.BlockSpec((tile, columns), lambda i, p: (here + i, 0))]
            + [pl.BlockSpec(memory_space=pl.ANY)] * len(more),
            out_specs=pl.BlockSpec((tile, columns), lambda i, p: (there + i, 0)),
        ),
        out_shape=jax.ShapeDtypeStruct((out_tokens, columns), dtype),
        input_output_aliases={4 + len(flat): 0} if more else {},
    )(part, *[in_vmem(c) for c in contexts], *flat, added, *more)


def exchanged(block, first):
    route = []
    for i in range(first, lax.axis_size("seq") - 1, 2):
        route += [(i, i + 1), (i + 1, i)]
    return lax.ppermute(block, "seq", route)


def swapped(block, flip):
    return lax.ppermute(block, HEAD, [(i, i ^ flip) for i in range(4)])


def other_side(block, flip):
    axes = ("seq", *HEAD)
    route = []
    for s in range(lax.axis_size("seq")):
        for h in range(4):
            route.append((s * 4 + h, (s ^ Z_CHIPS) * 4 + (h ^ flip)))
    return lax.ppermute(block, axes, route)


def body(
    encoder_queries,
    encoder_keys,
    encoder_values,
    block_lists,
    block_counts,
    decoder_queries,
    span_owner,
    cross_slots,
    out_weight,
    decoder_input,
):
    position = lax.axis_index("seq").astype(jnp.int32).reshape(1)
    part = lax.axis_index(HEAD).astype(jnp.int32).reshape(1)
    blocks = encoder_queries.shape[0] // BLK
    width = encoder_queries.shape[1]
    columns = decoder_input.shape[1]
    lists = block_lists.T
    slots = cross_slots.T
    k3 = cut(encoder_keys)
    v3 = cut(encoder_values)
    beside, beyond = send_call(position, encoder_keys, encoder_values)
    beside = exchanged(beside, 0)
    beyond = exchanged(beyond, 1)
    q_beside = exchanged(decoder_queries, 0)
    q_beyond = exchanged(decoder_queries, 1)
    encoder_args = (position, block_counts, lists, encoder_queries, k3, v3)
    partial, across2, around2, across3, across1 = encoder_call(
        *encoder_args, weight=(part, out_weight, columns)
    )
    w2_most = swapped(across2, 2)
    w2_rest = other_side(around2, 2)
    w3 = other_side(across3, 3)
    w1 = swapped(across1, 1)
    e3 = encoder_call(*encoder_args, edges=(beside, beyond, partial))
    tables = (position, span_owner, slots, k3, e3)
    answers = serve_call(*tables, [q_beside, q_beyond])
    from_beside = exchanged(answers[0], 0)
    from_beyond = exchanged(answers[1], 1)
    (own,) = serve_call(*tables, [decoder_queries])
    tokens = decoder_input.shape[0]
    share = tokens // PARTS
    context = own + from_beside + from_beyond
    halves = []
    for i in range(PARTS):
        across = swapped(context[i * share : (i + 1) * share], 2)
        corner = swapped(across, 1)
        halves.append([across, corner])
    aside = swapped(context, 1)
    total = project_call(
        part, [context, aside], [[out_weight], [w1]], decoder_input, jnp.float32, 0, tokens
    )
    decoder_out = None
    for i in range(PARTS):
        decoder_out = project_call(
            part,
            halves[i],
            [[in_vmem(w2_most), in_vmem(w2_rest)], [w3]],
            total,
            jnp.bfloat16,
            i,
            tokens,
            decoder_out,
        )
    return (e3.reshape(blocks * BLK, width), decoder_out)


def solution(mesh):
    split = Mesh(mesh.devices.reshape(mesh.shape["seq"], 2, 2), ("seq", "head_0", "head_1"))
    placed = (
        P("seq", HEAD),
        P("seq", HEAD),
        P("seq", HEAD),
        P("seq", None),
        P("seq"),
        P("seq", HEAD),
        P(),
        P(),
        P(HEAD, None),
        P("seq", HEAD),
    )
    return jax.shard_map(
        body,
        mesh=split,
        in_specs=placed,
        out_specs=(P("seq", HEAD), P("seq", HEAD)),
        check_vma=False,
    )
```

```python
import functools

import jax
import jax.numpy as jnp
from jax import lax
from jax.experimental import pallas as pl
from jax.experimental.pallas import tpu as pltpu
from jax.sharding import Mesh
from jax.sharding import PartitionSpec as P


HD = 64
BLK = 128
REACH = 2
SLOTS = 4
CROSS = 2
QUAD = 4
PARTS = 2
ANSWERS = 1
Z_CHIPS = 8
QW = HD * QUAD
HEAD = ("head_0", "head_1")
EXP_SCALE = 0.125 * 1.4426950408889634


def attend(q_ref, k_refs, v_refs, o_ref):
    quads = [pl.ds(c * QW, QW) for c in range(q_ref.shape[-1] // QW)]
    lane = lax.broadcasted_iota(jnp.int32, (BLK, QW), 1) // HD
    scores = []
    for cols in quads:
        q = q_ref[:, cols]
        zero = jnp.zeros_like(q)
        rows = jnp.concatenate([jnp.where(lane == h, q, zero) for h in range(QUAD)], axis=0)
        k = jnp.concatenate([r[:, cols] for r in k_refs], axis=0)
        scores.append(
            lax.dot_general(rows, k, (((1,), (1,)), ((), ())), preferred_element_type=jnp.float32)
        )
    for cols, s in zip(quads, scores):
        m = jnp.max(s, axis=1, keepdims=True)
        p = jnp.exp2((s - m) * EXP_SCALE)
        l = jnp.sum(p, axis=1, keepdims=True)
        v = jnp.concatenate([r[:, cols] for r in v_refs], axis=0)
        o = lax.dot_general(
            p.astype(jnp.bfloat16), v, (((1,), (0,)), ((), ())), preferred_element_type=jnp.float32
        )
        o = o * (1.0 / l)
        out = o[:BLK]
        for h in range(1, QUAD):
            out = jnp.where(lane == h, o[h * BLK : (h + 1) * BLK], out)
        o_ref[:, cols] = out.astype(jnp.bfloat16)


def send_kernel(pos, k, v, beside, beyond, s0, s1, s2, s3, load_sem, store_sem):
    halo = REACH * BLK
    tail = pl.ds(k.shape[0] - halo, halo)
    head = pl.ds(0, halo)
    values = pl.ds(halo, halo)
    sources = ((k.at[tail], s0), (v.at[tail], s1), (k.at[head], s2), (v.at[head], s3))
    loads = [pltpu.make_async_copy(x, y, load_sem) for x, y in sources]
    for load in loads:
        load.start()
    for load in loads:
        load.wait()

    def stores(up, down):
        pairs = ((s0, up.at[head]), (s1, up.at[values]), (s2, down.at[head]), (s3, down.at[values]))
        return [pltpu.make_async_copy(a, b, store_sem) for a, b in pairs]

    even = pos[0] % 2 == 0

    @pl.when(even)
    def _():
        for store in stores(beside, beyond):
            store.start()

    @pl.when(jnp.logical_not(even))
    def _():
        for store in stores(beyond, beside):
            store.start()

    for store in stores(beside, beyond):
        store.wait()


def send_call(position, k, v):
    halo = REACH * BLK
    width = k.shape[1]
    shape = jax.ShapeDtypeStruct((2 * halo, width), k.dtype)
    hbm = pl.BlockSpec(memory_space=pl.ANY)
    return pl.pallas_call(
        send_kernel,
        in_specs=[pl.BlockSpec(memory_space=pltpu.SMEM)] + [hbm] * 2,
        out_specs=[hbm] * 2,
        out_shape=[shape] * 2,
        scratch_shapes=[pltpu.VMEM((halo, width), k.dtype)] * 4
        + [pltpu.SemaphoreType.DMA, pltpu.SemaphoreType.DMA],
        name="pack_edges",
    )(position, k, v)


def encode_block(b, base, counts, lists, q_ref, kb, vb, o_ref):
    count = counts[b]
    ids = [lists[j, b] - base for j in range(SLOTS)]
    for n in range(1, SLOTS + 1):

        @pl.when(count == n)
        def _(n=n):
            attend(q_ref, [kb.at[i] for i in ids[:n]], [vb.at[i] for i in ids[:n]], o_ref)


def inner_kernel(pos, counts, lists, part, q, k, v, w, e, *refs):
    pieces, (kb, vb, qb, eb) = refs[:4], refs[4:8]
    stages = refs[8:12]
    k_sem, v_sem, q_sem, e_sem, load_sem, store_sem = refs[12:]
    columns = pieces[0].shape[1]
    split = pieces[0].shape[0]
    cuts = (
        (2, pl.ds(0, split)),
        (2, pl.ds(split, w.shape[0] - split)),
        (3, pl.ds(0, w.shape[0])),
        (1, pl.ds(0, w.shape[0])),
    )

    def load(i):
        flip, rows = cuts[i]
        start = pl.multiple_of((part[0] ^ flip) * columns, columns)
        return pltpu.make_async_copy(w.at[rows, pl.ds(start, columns)], stages[i], load_sem.at[i])

    def store(i):
        return pltpu.make_async_copy(stages[i], pieces[i], store_sem.at[i])

    blocks = k.shape[0]
    base = pos[0] * blocks

    def keys(i):
        return pltpu.make_async_copy(k.at[i], kb.at[i], k_sem.at[i])

    def values(i):
        return pltpu.make_async_copy(v.at[i], vb.at[i], v_sem.at[i])

    def queries(i):
        return pltpu.make_async_copy(q.at[i], qb.at[i], q_sem.at[i])

    def result(i):
        return pltpu.make_async_copy(eb.at[i], e.at[i], e_sem)

    for i in range(blocks):
        keys(i).start()
        values(i).start()
        if REACH <= i < blocks - REACH:
            queries(i).start()
    for i in range(len(cuts)):
        load(i).start()
    for i in range(2 * REACH):
        keys(i).wait()
        values(i).wait()

    @pl.loop(REACH, blocks - REACH)
    def _(b):
        keys(b + REACH).wait()
        values(b + REACH).wait()
        queries(b).wait()
        encode_block(b, base, counts, lists, qb.at[b], kb, vb, eb.at[b])
        result(b).start()
        for i in range(len(cuts)):

            @pl.when(b == REACH + 1 + i)
            def _(i=i):
                load(i).wait()
                store(i).start()

    for i in range(REACH, blocks - REACH):
        result(i).wait()
    for i in range(len(cuts)):
        store(i).wait()


def edge_kernel(
    per,
    awaited,
    pos,
    counts,
    lists,
    owners,
    slots,
    q,
    k,
    v,
    beside,
    beyond,
    _,
    e,
    kb,
    vb,
    qb,
    eb,
    far_sem,
    in_sem,
    e_sem,
):
    blocks = k.shape[0]
    total = owners.shape[0] // per
    named = jnp.int32(0)
    for shift in (-1, 1):
        source = pos[0] + shift
        for t in range(per):
            d = jnp.clip(source, 0, total - 1) * per + t
            live = (source >= 0) & (source < total) & (owners[d] == pos[0])
            bits = jnp.left_shift(jnp.int32(1), slots[0, d])
            bits = bits | jnp.left_shift(jnp.int32(1), slots[1, d])
            named = named | jnp.where(live, bits, 0)

    def block_of(t):
        return jnp.where(t < REACH, t, blocks - 2 * REACH + t)

    def due(t):
        return (jnp.right_shift(named, block_of(t)) & 1) == awaited

    near = 2 * REACH
    even = pos[0] % 2 == 0
    base = pos[0] * blocks - REACH

    def edges(up, down):
        pairs = (
            (up.at[pl.ds(0, REACH)], kb.at[pl.ds(0, REACH)]),
            (up.at[pl.ds(REACH, REACH)], vb.at[pl.ds(0, REACH)]),
            (down.at[pl.ds(0, REACH)], kb.at[pl.ds(REACH + blocks, REACH)]),
            (down.at[pl.ds(REACH, REACH)], vb.at[pl.ds(REACH + blocks, REACH)]),
        )
        return [pltpu.make_async_copy(a, b, far_sem) for a, b in pairs]

    local = []
    for start in (0, blocks - near):
        here = pl.ds(start, near)
        there = pl.ds(REACH + start, near)
        local.append(pltpu.make_async_copy(k.at[here], kb.at[there], in_sem))
        local.append(pltpu.make_async_copy(v.at[here], vb.at[there], in_sem))
    for i, start in enumerate((0, blocks - REACH)):
        local.append(
            pltpu.make_async_copy(q.at[pl.ds(start, REACH)], qb.at[pl.ds(i * REACH, REACH)], in_sem)
        )
    for copy in local:
        copy.start()

    @pl.when(even)
    def _():
        for copy in edges(beyond, beside):
            copy.start()

    @pl.when(jnp.logical_not(even))
    def _():
        for copy in edges(beside, beyond):
            copy.start()

    for copy in local + edges(beyond, beside):
        copy.wait()

    def result(t):
        return pltpu.make_async_copy(eb.at[t], e.at[block_of(t)], e_sem)

    @pl.loop(0, near)
    def _(t):
        @pl.when(due(t))
        def _():
            encode_block(block_of(t), base, counts, lists, qb.at[t], kb, vb, eb.at[t])
            result(t).start()

    @pl.loop(0, near)
    def _(t):
        @pl.when(due(t))
        def _():
            result(t).wait()


def encoder_call(position, counts, lists, q, k3, v3, weight=None, edges=None):
    blocks, _, width = k3.shape
    smem = pl.BlockSpec(memory_space=pltpu.SMEM)
    hbm = pl.BlockSpec(memory_space=pl.ANY)
    dma = pltpu.SemaphoreType.DMA

    def room(n):
        return pltpu.VMEM((n, BLK, width), jnp.bfloat16)

    shape = jax.ShapeDtypeStruct(k3.shape, jnp.bfloat16)
    args = (position, counts, lists, cut(q), k3, v3)
    if edges is None:
        part, w, columns = weight
        rows = w.shape[0]
        split = rows * 3 // 4
        pieces = [(n, columns) for n in (split, rows - split, rows, rows)]
        return pl.pallas_call(
            inner_kernel,
            in_specs=[smem] * 4 + [hbm] * 4,
            out_specs=[hbm] * 5,
            out_shape=[shape] + [jax.ShapeDtypeStruct(x, w.dtype) for x in pieces],
            scratch_shapes=[room(blocks)] * 4
            + [pltpu.VMEM(x, w.dtype) for x in pieces]
            + [dma((blocks,))] * 3
            + [dma, dma((4,)), dma((4,))],
            name="encoder_inner",
        )(*args[:3], part, *args[3:], w)
    per, awaited, owners, slots, beside, beyond, partial = edges
    return pl.pallas_call(
        functools.partial(edge_kernel, per, awaited),
        in_specs=[smem] * 5 + [hbm] * 3 + [pl.BlockSpec(memory_space=pltpu.VMEM)] * 2 + [hbm],
        out_specs=hbm,
        out_shape=shape,
        scratch_shapes=[room(blocks + 2 * REACH)] * 2 + [room(2 * REACH)] * 2 + [dma] * 3,
        input_output_aliases={10: 0},
        name="encoder_edge",
    )(*args[:3], owners, slots, *args[3:], in_vmem(cut(beside)), in_vmem(cut(beyond)), partial)


def serve_kernel(pos, owners, slots, k, e, *refs):
    sources = (len(refs) - 6) // (1 + ANSWERS)
    queries = refs[:sources]
    answers = refs[sources : (1 + ANSWERS) * sources]
    kb, eb, qb, ob, load_sems, answer_sem = refs[(1 + ANSWERS) * sources :]
    mine = pos[0]
    per = queries[0].shape[0]
    total = owners.shape[0] // per
    ahead = jnp.where(mine % 2 == 0, 1, -1)
    shifts = (0,) if sources == 1 else (ahead, -ahead)

    def candidate(i, t):
        source = mine + shifts[i]
        d = jnp.clip(source, 0, total - 1) * per + t
        live = (source >= 0) & (source < total) & (owners[d] == mine)
        return live, slots[0, d], slots[1, d]

    def loads(i, t, s0, s1):
        n = i * per + t
        sem = load_sems.at[n]
        return [
            pltpu.make_async_copy(a, b, sem)
            for a, b in (
                (queries[i].at[t], qb.at[n]),
                (k.at[s0], kb.at[n, 0]),
                (k.at[s1], kb.at[n, 1]),
                (e.at[s0], eb.at[n, 0]),
                (e.at[s1], eb.at[n, 1]),
            )
        ]

    for i in range(sources):
        for t in range(per):
            live, s0, s1 = candidate(i, t)

            @pl.when(live)
            def _(i=i, t=t, s0=s0, s1=s1):
                for copy in loads(i, t, s0, s1):
                    copy.start()

    share = per // ANSWERS

    def answer(part, i):
        rows = ob.at[pl.ds(i * per + part * share, share)]
        return pltpu.make_async_copy(rows, answers[part * sources + i], answer_sem)

    for part in range(ANSWERS):
        for i in range(sources):

            @pl.loop(part * share, (part + 1) * share)
            def _(t, i=i):
                live, s0, s1 = candidate(i, t)
                n = i * per + t

                @pl.when(live)
                def _():
                    for copy in loads(i, t, s0, s1):
                        copy.wait()
                    attend(
                        qb.at[n],
                        [kb.at[n, j] for j in range(CROSS)],
                        [eb.at[n, j] for j in range(CROSS)],
                        ob.at[n],
                    )

                @pl.when(jnp.logical_not(live))
                def _():
                    ob[n] = jnp.zeros(ob.shape[1:], ob.dtype)

            answer(part, i).start()

    for part in range(ANSWERS):
        for i in range(sources):
            answer(part, i).wait()


def serve_call(position, owners, slots, k3, e3, queries):
    width = k3.shape[-1]
    sources = len(queries)
    queries = [cut(x) for x in queries]
    per = queries[0].shape[0]
    smem = pl.BlockSpec(memory_space=pltpu.SMEM)
    hbm = pl.BlockSpec(memory_space=pl.ANY)
    vmem = pl.BlockSpec(memory_space=pltpu.VMEM)
    served = per * sources
    if sources > 1:
        queries = [in_vmem(x) for x in queries]
    out = pl.pallas_call(
        serve_kernel,
        in_specs=[smem] * 3 + [hbm] * 2 + [vmem if sources > 1 else hbm] * sources,
        out_specs=[hbm] * (sources * ANSWERS),
        out_shape=[jax.ShapeDtypeStruct((per // ANSWERS, BLK, width), jnp.bfloat16)]
        * (sources * ANSWERS),
        scratch_shapes=[
            pltpu.VMEM((served, CROSS, BLK, width), jnp.bfloat16),
            pltpu.VMEM((served, CROSS, BLK, width), jnp.bfloat16),
            pltpu.VMEM((served, BLK, width), jnp.bfloat16),
            pltpu.VMEM((served, BLK, width), jnp.bfloat16),
            pltpu.SemaphoreType.DMA((served,)),
            pltpu.SemaphoreType.DMA,
        ],
    )(position, owners, slots, k3, e3, *queries)
    return [x.reshape(-1, width) for x in out]


def cut(x):
    return x.reshape(-1, BLK, x.shape[-1])


def in_vmem(x):
    return pltpu.with_memory_space_constraint(x, pltpu.VMEM)


def project_kernel(counts, part, c0, c1, *refs):
    first, second = counts
    weights = refs[: first + second]
    r_ref = refs[first + second]
    total = r_ref[...].astype(jnp.float32)
    for c, ws in ((c0, weights[:first]), (c1, weights[first:])):
        w = jnp.concatenate([x[...] for x in ws], axis=0) if len(ws) > 1 else ws[0][...]
        total = total + jnp.dot(c[...], w, preferred_element_type=jnp.float32)
    refs[-1][...] = total.astype(refs[-1].dtype)


def project_call(part, contexts, weights, added, dtype, index, out_tokens, earlier=None):
    tokens, width = contexts[0].shape
    columns = added.shape[1]
    tile = min(tokens, out_tokens // PARTS)
    here = index if added.shape[0] > tokens else 0
    there = index if out_tokens > tokens else 0
    c_spec = pl.BlockSpec((tile, width), lambda i, p: (i, 0))
    flat = [w for ws in weights for w in ws]
    w_specs = [
        pl.BlockSpec((w.shape[0], columns), lambda i, p: (0, p[0]))
        if w.shape[1] > columns
        else pl.BlockSpec((w.shape[0], columns), lambda i, p: (0, 0))
        for w in flat
    ]
    more = [] if earlier is None else [earlier]
    return pl.pallas_call(
        functools.partial(project_kernel, tuple(len(ws) for ws in weights)),
        grid_spec=pltpu.PrefetchScalarGridSpec(
            num_scalar_prefetch=1,
            grid=(tokens // tile,),
            in_specs=[c_spec] * 2
            + w_specs
            + [pl.BlockSpec((tile, columns), lambda i, p: (here + i, 0))]
            + [pl.BlockSpec(memory_space=pl.ANY)] * len(more),
            out_specs=pl.BlockSpec((tile, columns), lambda i, p: (there + i, 0)),
        ),
        out_shape=jax.ShapeDtypeStruct((out_tokens, columns), dtype),
        input_output_aliases={4 + len(flat): 0} if more else {},
    )(part, *[in_vmem(c) for c in contexts], *flat, added, *more)


def exchanged(block, first):
    route = []
    for i in range(first, lax.axis_size("seq") - 1, 2):
        route += [(i, i + 1), (i + 1, i)]
    return lax.ppermute(block, "seq", route)


def swapped(block, flip):
    return lax.ppermute(block, HEAD, [(i, i ^ flip) for i in range(4)])


def other_side(block, flip):
    axes = ("seq", *HEAD)
    route = []
    for s in range(lax.axis_size("seq")):
        for h in range(4):
            route.append((s * 4 + h, (s ^ Z_CHIPS) * 4 + (h ^ flip)))
    return lax.ppermute(block, axes, route)


def body(
    encoder_queries,
    encoder_keys,
    encoder_values,
    block_lists,
    block_counts,
    decoder_queries,
    span_owner,
    cross_slots,
    out_weight,
    decoder_input,
):
    position = lax.axis_index("seq").astype(jnp.int32).reshape(1)
    part = lax.axis_index(HEAD).astype(jnp.int32).reshape(1)
    blocks = encoder_queries.shape[0] // BLK
    width = encoder_queries.shape[1]
    columns = decoder_input.shape[1]
    lists = block_lists.T
    slots = cross_slots.T
    k3 = cut(encoder_keys)
    v3 = cut(encoder_values)
    beside, beyond = send_call(position, encoder_keys, encoder_values)
    beside = exchanged(beside, 0)
    beyond = exchanged(beyond, 1)
    q_beside = exchanged(decoder_queries, 0)
    q_beyond = exchanged(decoder_queries, 1)
    encoder_args = (position, block_counts, lists, encoder_queries, k3, v3)
    partial, across2, around2, across3, across1 = encoder_call(
        *encoder_args, weight=(part, out_weight, columns)
    )
    w2_most = swapped(across2, 2)
    w2_rest = other_side(around2, 2)
    w3 = other_side(across3, 3)
    w1 = swapped(across1, 1)
    edges = (span_owner, slots, beside, beyond)
    per = decoder_queries.shape[0] // BLK
    e3 = encoder_call(*encoder_args, edges=(per, 1, *edges, partial))
    tables = (position, span_owner, slots, k3)
    answers = serve_call(*tables, e3, [q_beside, q_beyond])
    e3, *answers = lax.optimization_barrier((e3, *answers))
    from_beside = exchanged(answers[0], 0)
    from_beyond = exchanged(answers[1], 1)
    e3 = encoder_call(*encoder_args, edges=(per, 0, *edges, e3))
    (own,) = serve_call(*tables, e3, [decoder_queries])
    tokens = decoder_input.shape[0]
    share = tokens // PARTS
    context = own + from_beside + from_beyond
    halves = []
    for i in range(PARTS):
        across = swapped(context[i * share : (i + 1) * share], 2)
        corner = swapped(across, 1)
        halves.append([across, corner])
    aside = swapped(context, 1)
    total = project_call(
        part, [context, aside], [[out_weight], [w1]], decoder_input, jnp.float32, 0, tokens
    )
    decoder_out = None
    for i in range(PARTS):
        decoder_out = project_call(
            part,
            halves[i],
            [[in_vmem(w2_most), in_vmem(w2_rest)], [w3]],
            total,
            jnp.bfloat16,
            i,
            tokens,
            decoder_out,
        )
    return (e3.reshape(blocks * BLK, width), decoder_out)


def solution(mesh):
    split = Mesh(mesh.devices.reshape(mesh.shape["seq"], 2, 2), ("seq", "head_0", "head_1"))
    placed = (
        P("seq", HEAD),
        P("seq", HEAD),
        P("seq", HEAD),
        P("seq", None),
        P("seq"),
        P("seq", HEAD),
        P(),
        P(),
        P(HEAD, None),
        P("seq", HEAD),
    )
    return jax.shard_map(
        body,
        mesh=split,
        in_specs=placed,
        out_specs=(P("seq", HEAD), P("seq", HEAD)),
        check_vma=False,
    )
```
